256 devices in a mesh: seq: 8 (over z), chan: 16 (over y, x), rep: 2 (over core).
Axes of the slice: x: 4, y: 4, z: 8, core: 2. Of those that a mesh axis runs over, the one named last changes fastest.
Arguments:
- fine_codes: int32 [16384], P(('rep', 'seq')), parts along dimension 0, may hold values from 0 to 1023
- coarse_codes: int32 [8192], P(('rep', 'seq')), parts along dimension 0, may hold values from 0 to 1023
- frame_order: int32 [256], replicated, may hold values from 0 to 255, each once
- emb_fine: bfloat16 [1024, 4096], P(None, 'chan'), may hold values from -90 to 90
- emb_coarse: bfloat16 [1024, 4096], P(None, 'chan'), may hold values from -90 to 90
- norm_gain: bfloat16 [4096], P('chan'), may hold values from 0.099609375 to 1.8984375
- w_hyena: bfloat16 [4096, 3, 4096], P(None, None, 'chan'), may hold values from -0.09375 to 0.09375
- short_taps: bfloat16 [3, 256, 128], P(None, 'chan'), may hold values from -0.5 to 0.5
- long_filter: float32 [4096, 8192], P(('chan', 'seq')), may hold values from -5 to 5
- w_attn: bfloat16 [4096, 3, 2048], P(None, None, 'chan'), may hold values from -0.09375 to 0.09375
Outputs:
- hyena_out: bfloat16 [4096, 16384], P('chan', ('rep', 'seq')), parts along dimension 1
- attn_out: bfloat16 [16384, 2048], P(('rep', 'seq'), 'chan'), parts along dimension 0
The draws below stay inside these ranges and needn't reach their ends.
There are 2 independent parts, one for each index of `rep`. The reference program is written for one: setup_inputs(seed, part) draws one part's arguments, and reference() takes and returns one part's arrays. A program takes and returns all parts, laid end to end along the dimension named above; an argument that names none is the same for every part. Nothing has to cross between parts.
Inputs may be any that keep to these rules, and one draw needn't show every extreme that they name: `frame_order`: each of 0 to 255 once.
All inputs are finite; a program needn't handle non-finite values.
Results may differ from the reference program's by a relative error of at most 0.014.
The reference program's roundings to bfloat16 on the way count: a program that leaves them out, or rounds other values in their place, can miss the bound.
Values may be sent and summed in bfloat16 or wider, within the bound.
A program may use at most 128 MiB of HBM per device.

```python
import math
import jax
import jax.numpy as jnp
import numpy as np
from jax import lax

MODEL_WIDTH = 4096
HEADS = 16
HD = 128
VOCAB = 1024
TAPS = 128
FIR_GROUP = 16
FRAME = 256
BLOCK = 512
WINDOW_LENGTH = 8192


def table_draw(key, stream):
    row_key, column_key, base_key = jax.random.split(jax.random.fold_in(key, stream), 3)
    column_index = jnp.arange(MODEL_WIDTH, dtype=jnp.float32)
    rising = jnp.exp(column_index * (math.log(10.0) / MODEL_WIDTH))[None, :]
    jitter = jnp.exp(jax.random.uniform(column_key, (1, MODEL_WIDTH), jnp.float32, math.log(0.6), math.log(1.6)))
    row_scale = jnp.exp(jax.random.uniform(row_key, (VOCAB, 1), jnp.float32, 0.0, math.log(10.0)))
    entries = jnp.clip(jax.random.normal(base_key, (VOCAB, MODEL_WIDTH), jnp.float32), -5.0, 5.0)
    return entries * row_scale * rising * jitter * 0.1


def draw_emb_fine(key, part):
    return table_draw(key, 3).astype(jnp.bfloat16)


def draw_emb_coarse(key, part):
    return table_draw(key, 5).astype(jnp.bfloat16)


def draw_long_filter(key, part):
    reach_key, noise_key, position_random_key, height_random_key = jax.random.split(jax.random.fold_in(key, 7), 4)
    low_end = math.log(40.0)
    high_end = math.log(2.0 * WINDOW_LENGTH)
    reaches = jnp.exp(jax.random.uniform(reach_key, (MODEL_WIDTH, 1), jnp.float32, low_end, high_end))
    temporal_delay = jnp.arange(WINDOW_LENGTH, dtype=jnp.int32)[None, :]
    decay_profile = jnp.exp(-temporal_delay.astype(jnp.float32) / reaches)
    spike_position = jax.random.randint(position_random_key, (MODEL_WIDTH, 3), 0, WINDOW_LENGTH)
    spike_height = jax.random.uniform(height_random_key, (MODEL_WIDTH, 3), jnp.float32, 0.5, 0.8)
    for spike_index in range(3):
        spike_mask = temporal_delay >= spike_position[:, spike_index:spike_index + 1]
        decay_profile = decay_profile * jnp.where(spike_mask, spike_height[:, spike_index:spike_index + 1], 1.0)
    entries = jnp.clip(jax.random.normal(noise_key, (MODEL_WIDTH, WINDOW_LENGTH), jnp.float32), -5.0, 5.0)
    energy = jnp.sqrt(jnp.sum(decay_profile * decay_profile, axis=1, keepdims=True))
    return entries * decay_profile / energy


def place_ends(array, stream_key, low, largest):
    extent = array.shape
    spot = [jax.random.randint(jax.random.fold_in(stream_key, axis), (), 0, extent[axis]) for axis in range(len(extent))]
    array = array.at[tuple(spot)].set(low)
    longest = extent.index(max(extent))
    spot[longest] = (spot[longest] + 1) % extent[longest]
    return array.at[tuple(spot)].set(largest)


def steps_of(rng, extent, pieces, low, high):
    level = 1.0
    for axis_at, shards_of in pieces:
        steps = jax.random.uniform(jax.random.fold_in(jax.random.fold_in(rng, 6), axis_at), (shards_of,), jnp.float32, low / len(pieces), high / len(pieces))
        level = level * jnp.repeat(jnp.exp(steps), extent[axis_at] // shards_of).reshape((-1,) + (1,) * (len(extent) - 1 - axis_at))
    return level


def rank_table(number_of, skew):
    portions = [(1 << 20) // math.isqrt(rank ** skew) + 1 for rank in range(1, number_of + 1)]
    width = 1 + sum(portions) // (1 << 30)
    return np.cumsum(np.array([max(1, weight // width) for weight in portions]))


def skewed_ids(own_key, shape, number_of, skew):
    grid = rank_table(number_of, skew)
    ticket = jax.random.randint(jax.random.fold_in(own_key, 1), shape, 0, int(grid[number_of - 1]))
    grade = jnp.searchsorted(jnp.asarray(grid, jnp.int32), ticket, side="right")
    return jax.random.permutation(jax.random.fold_in(own_key, 2), number_of)[grade].astype(jnp.int32)


def normal_values(own_key, shape, deviation, reach, shards=(), held_as=jnp.bfloat16):
    drawn = deviation * jax.random.normal(own_key, shape, jnp.float32)
    if shards:
        drawn = drawn * steps_of(own_key, shape, shards, -0.22, 0.18)
    return jnp.clip(drawn, -reach, reach).astype(held_as)


def setup_inputs(seed: int = 0, part: int = 0) -> dict:
    keys = jax.random.split(jax.random.key(seed), 11)
    part_keys = jax.random.split(jax.random.fold_in(keys[10], part), 11)
    return {
        "fine_codes": place_ends(skewed_ids(part_keys[0], (WINDOW_LENGTH,), VOCAB, 2), jax.random.fold_in(part_keys[0], 3), 0, VOCAB - 1).astype(jnp.int32),
        "coarse_codes": place_ends(skewed_ids(part_keys[1], (WINDOW_LENGTH // 2,), VOCAB, 1), jax.random.fold_in(part_keys[1], 3), 0, VOCAB - 1).astype(jnp.int32),
        "frame_order": jax.random.permutation(keys[2], FRAME).astype(jnp.int32),
        "emb_fine": draw_emb_fine(jax.random.fold_in(keys[10], 71), part),
        "emb_coarse": draw_emb_coarse(jax.random.fold_in(keys[10], 71), part),
        "norm_gain": jnp.clip(1.0 + 0.18 * jax.random.normal(keys[5], (MODEL_WIDTH,), jnp.float32), 0.099609375, 1.8984375).astype(jnp.bfloat16),
        "w_hyena": normal_values(keys[6], (MODEL_WIDTH, 3, MODEL_WIDTH), MODEL_WIDTH ** -0.5, 0.09375, ((2, 16),)),
        "short_taps": normal_values(keys[7], (3, MODEL_WIDTH // FIR_GROUP, TAPS), TAPS ** -0.5, 0.5, ((1, 16),)),
        "long_filter": draw_long_filter(jax.random.fold_in(keys[10], 71), part),
        "w_attn": normal_values(keys[9], (MODEL_WIDTH, 3, HEADS * HD), MODEL_WIDTH ** -0.5, 0.09375, ((2, 16),)),
    }


EPSILON = 1e-05

def rounded(tensor):
    return lax.optimization_barrier(tensor.astype(jnp.bfloat16)).astype(jnp.float32)

def banded(filter_taps):
    tap_count = filter_taps.shape[-1]
    row_index = lax.broadcasted_iota(jnp.int32, (tap_count, 2 * tap_count), 0)
    column_index = lax.broadcasted_iota(jnp.int32, (tap_count, 2 * tap_count), 1)
    tap_lag = row_index + tap_count - column_index
    which_tap = lax.broadcasted_iota(jnp.int32, (tap_count, tap_count, 2 * tap_count), 0)
    selector = (which_tap == tap_lag[None]).astype(filter_taps.dtype)
    flat_taps = filter_taps.reshape(-1, tap_count)
    spread_taps = jnp.dot(flat_taps, selector.reshape(tap_count, -1), preferred_element_type=jnp.float32)
    return spread_taps.reshape(filter_taps.shape[:-1] + (tap_count, 2 * tap_count)).astype(filter_taps.dtype)

def short_filter(sequence, filter_taps):
    channels, length = sequence.shape
    groups, tap_count = filter_taps.shape
    tile_count = length // tap_count
    padded = jnp.concatenate([jnp.zeros((channels, tap_count), sequence.dtype), sequence], axis=1)
    earlier_rows = padded[:, :length].reshape(groups, channels // groups, tile_count, tap_count)
    later_rows = padded[:, tap_count:].reshape(groups, channels // groups, tile_count, tap_count)
    window = jnp.concatenate([earlier_rows, later_rows], axis=3)
    toeplitz = banded(filter_taps).astype(jnp.float32)
    output = jnp.einsum('gab,gcnb->gcna', toeplitz, window.astype(jnp.float32), precision=lax.Precision.HIGHEST)
    return output.reshape(channels, length).astype(jnp.bfloat16)

def filter_one(operands):
    return short_filter(operands[0], operands[1])

def reference(fine_codes, coarse_codes, frame_order, emb_fine, emb_coarse, norm_gain, w_hyena, short_taps, long_filter, w_attn):
    peak_value = lax.Precision.HIGHEST
    frame_base = jnp.arange(WINDOW_LENGTH // FRAME, dtype=jnp.int32) * FRAME
    code_at = (frame_base[:, None] + frame_order.astype(jnp.int32)[None, :]).reshape(WINDOW_LENGTH)
    fine_ids = fine_codes[code_at]
    coarse_ids = coarse_codes[code_at // 2]
    values = rounded(emb_fine[fine_ids].astype(jnp.float32) + emb_coarse[coarse_ids].astype(jnp.float32))
    factor = lax.rsqrt(lax.optimization_barrier(jnp.mean(values * values, axis=1)) + EPSILON)
    normed = (values * factor[:, None] * norm_gain.astype(jnp.float32)[None, :]).astype(jnp.bfloat16)
    projected = jnp.dot(normed, w_hyena.reshape(MODEL_WIDTH, 3 * MODEL_WIDTH), preferred_element_type=jnp.float32)
    projected = projected.astype(jnp.bfloat16).reshape(WINDOW_LENGTH, 3, MODEL_WIDTH).transpose(1, 2, 0)
    filtered = lax.optimization_barrier(lax.map(filter_one, (projected, short_taps))).astype(jnp.float32)
    mixture = rounded(filtered[1] * filtered[2])
    spectrum = jnp.fft.rfft(mixture, n=2 * WINDOW_LENGTH, axis=1) * jnp.fft.rfft(long_filter, n=2 * WINDOW_LENGTH, axis=1)
    convolved = rounded(jnp.fft.irfft(spectrum, n=2 * WINDOW_LENGTH, axis=1)[:, :WINDOW_LENGTH])
    hyena_out = (filtered[0] * convolved).astype(jnp.bfloat16)
    blocks = WINDOW_LENGTH // BLOCK
    heads_all = jnp.dot(hyena_out.T, w_attn.reshape(MODEL_WIDTH, 3 * HEADS * HD), preferred_element_type=jnp.float32)
    heads_all = rounded(heads_all).reshape(blocks, BLOCK, 3, HEADS, HD)
    queries = heads_all[:, :, 0]
    keys_all = heads_all[:, :, 1]
    values_all = heads_all[:, :, 2]
    states = jnp.einsum('nshd,nshe->nhde', keys_all, values_all, precision=peak_value)
    running = jnp.cumsum(states, axis=0)
    earlier = rounded(jnp.concatenate([jnp.zeros_like(states[:1]), running[:-1]], axis=0))
    scores = jnp.einsum('nthd,nshd->nhts', queries, keys_all, precision=peak_value)
    causal = lax.broadcasted_iota(jnp.int32, (BLOCK, BLOCK), 0) >= lax.broadcasted_iota(jnp.int32, (BLOCK, BLOCK), 1)
    scores = rounded(jnp.where(causal, scores, 0.0))
    inside = jnp.einsum('nhts,nshe->nthe', scores, values_all, precision=peak_value)
    carried = jnp.einsum('nthd,nhde->nthe', queries, earlier, precision=peak_value)
    position = jnp.arange(WINDOW_LENGTH, dtype=jnp.int32).reshape(blocks, BLOCK) + 1
    divisor = jnp.sqrt((position * HD).astype(jnp.float32))
    attn_out = ((inside + carried) / divisor[:, :, None, None]).astype(jnp.bfloat16).reshape(WINDOW_LENGTH, HEADS * HD)
    return (hyena_out, attn_out)
```

```python
import functools
import math

import jax
import jax.numpy as jnp
import numpy as np
from jax import lax
from jax.experimental import pallas as pl
from jax.experimental.pallas import tpu as pltpu
from jax.sharding import PartitionSpec as P

HD = 128
FRAME = 256
BLOCK = 512
LANES = 128
EPSILON = 1e-05
F32 = jnp.float32
BF16 = jnp.bfloat16
ANY = pl.BlockSpec(memory_space=pl.ANY)
MESH = pl.DeviceIdType.MESH
BIG = 56 << 20

ROWS_W = 72
TILES = 64
POINTS = 2 * TILES * LANES


def split_np(x):
    hi = np.asarray(x, np.float32).astype(jnp.bfloat16)
    lo = (np.asarray(x, np.float64) - hi.astype(np.float64)).astype(np.float32).astype(jnp.bfloat16)
    return hi, lo


@functools.lru_cache(None)
def tables():
    w = np.arange(ROWS_W)[:, None]
    kept = (w <= 64).astype(np.float64)
    q = np.arange(TILES)[None, :]
    angle = 2 * np.pi * ((w * q) % 128) / 128
    outer = np.concatenate([np.cos(angle) * kept, -np.sin(angle) * kept], 0)
    a = np.arange(LANES)[None, :]
    turn = 2 * np.pi * (w * a) / POINTS
    twist = np.stack([np.cos(turn) * kept, np.sin(turn) * kept]).astype(np.float32)
    m = np.arange(LANES)
    inner = 2 * np.pi * ((m[:, None] * m[None, :]) % 128) / 128
    c, s = np.cos(inner), np.sin(inner)
    forward = np.block([[c, -s], [s, c]])
    backward = np.block([[c, s], [-s, c]])
    weight = np.where((w == 0) | (w == 64), 1.0, 2.0) * kept / POINTS
    inverse = np.concatenate([(np.cos(angle) * weight).T, (-np.sin(angle) * weight).T], 1)
    outer_hi, outer_lo = split_np(outer)
    inv_hi, inv_lo = split_np(inverse)
    fwd = np.stack(split_np(forward))
    bwd = np.stack(split_np(backward))
    outer3 = np.concatenate([outer_hi, outer_lo, outer_hi], 1)
    inv3 = np.concatenate([inv_hi, inv_lo, inv_hi], 1)
    return outer3, twist, fwd, bwd, inv3


def split(x):
    hi = x.astype(BF16)
    return hi, (x - hi.astype(F32)).astype(BF16)


def mm(a, b):
    return jnp.dot(a, b, preferred_element_type=F32)


def mm3(x, table):
    hi, lo = split(x)
    return mm(hi, table[0]) + (mm(lo, table[0]) + mm(hi, table[1]))


def ids_kernel(fine_ref, coarse_ref, order_ref, emb_fine_ref, emb_coarse_ref, ids_ref, sums_ref):
    order = order_ref[...]
    row = lax.broadcasted_iota(jnp.int32, (FRAME, FRAME), 0)
    pick = (row == order).astype(BF16)
    pick_half = (row[: FRAME // 2] == order // 2).astype(BF16)

    def looked(codes, pick):
        hi = (codes // 32).astype(F32).astype(BF16)
        lo = (codes % 32).astype(F32).astype(BF16)
        return (mm(hi, pick) * 32.0 + mm(lo, pick)).astype(jnp.int32)

    fine = looked(fine_ref[...], pick)
    coarse = looked(coarse_ref[...], pick_half)
    ids_ref[0:4, :] = fine
    ids_ref[4:8, :] = coarse
    vocab = lax.broadcasted_iota(jnp.int32, (emb_fine_ref.shape[0], FRAME), 0)
    dims = (((0,), (0,)), ((), ()))
    for frame in range(4):
        hot_fine = (vocab == fine[frame : frame + 1]).astype(BF16)
        hot_coarse = (vocab == coarse[frame : frame + 1]).astype(BF16)
        rows = lax.dot_general(emb_fine_ref[...], hot_fine, dims, preferred_element_type=F32)
        rows = rows + lax.dot_general(
            emb_coarse_ref[...], hot_coarse, dims, preferred_element_type=F32
        )
        rows = rows.astype(BF16).astype(F32)
        total = jnp.sum(rows * rows, axis=0, keepdims=True)
        sums_ref[2 * frame : 2 * frame + 1, :] = total[:, :LANES]
        sums_ref[2 * frame + 1 : 2 * frame + 2, :] = total[:, LANES:]


def local_ids(fine, coarse, order, emb_fine, emb_coarse, interpret=False):
    return pl.pallas_call(
        ids_kernel,
        out_shape=(
            jax.ShapeDtypeStruct((8, FRAME), jnp.int32),
            jax.ShapeDtypeStruct((8, LANES), F32),
        ),
        compiler_params=pltpu.CompilerParams(vmem_limit_bytes=BIG),
        interpret=interpret,
        name="local_ids",
    )(fine.reshape(4, FRAME), coarse.reshape(4, FRAME // 2), order[None], emb_fine, emb_coarse)


def project_kernel(rows_ref, side_ref, w_ref, out_ref, factor_ref, x_ref):
    chans = rows_ref.shape[0]

    @pl.when(pl.program_id(0) == 0)
    def _():
        for c in range(chans):
            x = rows_ref[c].astype(F32) * side_ref[c, 0:1, :FRAME]
            hi, lo = split(x)
            x_ref[0:128, c * 256 : (c + 1) * 256] = hi
            x_ref[128:256, c * 256 : (c + 1) * 256] = lo
        total = side_ref[0, :, FRAME:]
        for c in range(1, chans):
            total = total + side_ref[c, :, FRAME:]
        factor_ref[...] = lax.rsqrt(total / (chans * 256.0) + EPSILON)

    both = mm(x_ref[...], w_ref[0])
    hi, lo = split(jnp.transpose(both[:128] + both[128:]))
    out_ref[0, :, :128] = hi
    out_ref[0, :, 128:] = lo


def project(rows, side, w, interpret=False):
    chans = rows.shape[0]
    depth = w.shape[1]
    return pl.pallas_call(
        project_kernel,
        grid=(3,),
        in_specs=[
            pl.BlockSpec(rows.shape, lambda k: (0, 0, 0)),
            pl.BlockSpec(side.shape, lambda k: (0, 0, 0)),
            pl.BlockSpec((1, depth, 256), lambda k: (k, 0, 0)),
        ],
        out_specs=[
            pl.BlockSpec((1, 256, 256), lambda k: (k, 0, 0)),
            pl.BlockSpec((8, LANES), lambda k: (0, 0)),
        ],
        out_shape=(
            jax.ShapeDtypeStruct((3, 256, 256), BF16),
            jax.ShapeDtypeStruct((8, LANES), F32),
        ),
        scratch_shapes=[pltpu.VMEM((256, chans * 256), BF16)],
        compiler_params=pltpu.CompilerParams(vmem_limit_bytes=BIG),
        interpret=interpret,
        name="project",
    )(rows, side, w)


GROUP = 4


def twisted(step, twist_ref):
    cos, sin = twist_ref[0], twist_ref[1]
    rows = []
    for i in range(GROUP):
        re = step[:ROWS_W, i * LANES : (i + 1) * LANES]
        im = step[ROWS_W:, i * LANES : (i + 1) * LANES]
        rows.append(jnp.concatenate([re * cos + im * sin, im * cos - re * sin], 1))
    return jnp.concatenate(rows, 0)


def spectrum_kernel(h_ref, outer_ref, twist_ref, fwd_ref, out_ref, wide_ref):
    channels = h_ref.shape[0]
    for q in range(TILES):
        wide_ref[pl.ds(q, channels, stride=TILES), :] = h_ref[:, q * LANES : (q + 1) * LANES]

    @pl.loop(0, channels // GROUP)
    def _(step):
        pieces = []
        for i in range(GROUP):
            hi, lo = split(wide_ref[pl.ds((step * GROUP + i) * TILES, TILES), :])
            pieces.append(jnp.concatenate([hi, hi, lo], 0))
        first = mm(outer_ref[...], jnp.concatenate(pieces, 1))
        out_ref[pl.ds(step * GROUP * ROWS_W, GROUP * ROWS_W), :] = mm3(
            twisted(first, twist_ref), fwd_ref
        )


def spectrum(h, interpret=False):
    outer3, twist, fwd, _, _ = tables()
    return pl.pallas_call(
        spectrum_kernel,
        out_shape=jax.ShapeDtypeStruct((h.shape[0] * ROWS_W, 256), F32),
        scratch_shapes=[pltpu.VMEM((h.shape[0] * TILES, LANES), F32)],
        compiler_params=pltpu.CompilerParams(vmem_limit_bytes=BIG),
        interpret=interpret,
        name="spectrum",
    )(h, outer3, twist, fwd)


def convolve_kernel(
    proj_ref,
    ids_ref,
    factor_ref,
    taps_ref,
    spec_ref,
    outer_ref,
    twist_ref,
    fwd_ref,
    bwd_ref,
    inv_ref,
    out_ref,
    left_ref,
    wide_ref,
    gate_ref,
    mix_ref,
    y_ref,
):
    channels = 32
    for s in range(16):
        left_ref[0:96, s * 128 : (s + 1) * 128] = proj_ref[s, :, :128]
        left_ref[96:192, s * 128 : (s + 1) * 128] = proj_ref[s, :, 128:]
    vocab = lax.broadcasted_iota(jnp.int32, (1024, FRAME), 0)

    @pl.loop(0, 8)
    def _(z):
        ids = ids_ref[z]
        for i in range(4):
            hot = jnp.concatenate(
                [
                    (vocab == ids[i : i + 1]).astype(BF16),
                    (vocab == ids[4 + i : 5 + i]).astype(BF16),
                ],
                0,
            )
            both = mm(left_ref[...], hot)
            value = both[:96] + both[96:]
            for half in range(2):
                wide_ref[pl.ds(z * 8 + 2 * i + half, 96, stride=TILES), :] = value[
                    :, half * LANES : (half + 1) * LANES
                ]

    tap_row = lax.broadcasted_iota(jnp.int32, (LANES, LANES), 0)
    tap_col = lax.broadcasted_iota(jnp.int32, (LANES, LANES), 1)
    rows = 16 * TILES
    first_tile = lax.broadcasted_iota(jnp.int32, (rows, LANES), 0) % TILES == 0
    scale = jnp.concatenate([factor_ref[...]] * 16, 0)

    def filtered(k, g):
        taps = jnp.broadcast_to(taps_ref[2 * k + g : 2 * k + g + 1, :], (LANES, LANES))
        turned = pltpu.roll(taps, 0, 1, stride=1, stride_axis=0)
        both = jnp.concatenate(
            [
                jnp.where(tap_col >= tap_row, turned, 0.0),
                jnp.where(tap_col < tap_row, turned, 0.0),
            ],
            1,
        ).astype(BF16)
        start = (2 * k + g) * rows
        x = (wide_ref[start : start + rows, :] * scale).astype(BF16)
        parts = mm(x, both)
        carried = jnp.where(first_tile, 0.0, pltpu.roll(parts[:, LANES:], 1, 0))
        return (parts[:, :LANES] + carried).astype(BF16)

    for g in range(2):
        gate_ref[g * rows : (g + 1) * rows, :] = filtered(0, g)
        left = filtered(1, g).astype(F32)
        mix_ref[g * rows : (g + 1) * rows, :] = (left * filtered(2, g).astype(F32)).astype(BF16)

    @pl.loop(0, channels // GROUP)
    def _(step):
        pieces = []
        for i in range(GROUP):
            x = mix_ref[pl.ds((step * GROUP + i) * TILES, TILES), :]
            pieces.append(jnp.concatenate([x, x], 0))
        first = mm(outer_ref[:, : 2 * TILES], jnp.concatenate(pieces, 1))
        spec = mm3(twisted(first, twist_ref), fwd_ref)
        other = spec_ref[pl.ds(step * GROUP * ROWS_W, GROUP * ROWS_W), :]
        re, im = spec[:, :LANES], spec[:, LANES:]
        ore, oim = other[:, :LANES], other[:, LANES:]
        back = mm3(jnp.concatenate([re * ore - im * oim, re * oim + im * ore], 1), bwd_ref)
        cos, sin = twist_ref[0], twist_ref[1]
        columns = []
        for i in range(GROUP):
            bre = back[i * ROWS_W : (i + 1) * ROWS_W, :LANES]
            bim = back[i * ROWS_W : (i + 1) * ROWS_W, LANES:]
            undone = jnp.concatenate([bre * cos - bim * sin, bim * cos + bre * sin], 0)
            hi, lo = split(undone)
            columns.append(jnp.concatenate([hi, hi, lo], 0))
        result = mm(inv_ref[...], jnp.concatenate(columns, 1))
        for i in range(GROUP):
            at = pl.ds((step * GROUP + i) * TILES, TILES)
            conv = result[:, i * LANES : (i + 1) * LANES].astype(BF16).astype(F32)
            y_ref[at, :] = gate_ref[at, :].astype(F32) * conv

    for q in range(TILES):
        out_ref[q // 8, :, (q % 8) * LANES : (q % 8 + 1) * LANES] = y_ref[
            pl.ds(q, channels, stride=TILES), :
        ].astype(BF16)


def convolve(proj, ids, factor, taps, spec, interpret=False):
    outer3, twist, fwd, bwd, inv3 = tables()
    return pl.pallas_call(
        convolve_kernel,
        out_shape=jax.ShapeDtypeStruct((8, 32, 1024), BF16),
        scratch_shapes=[
            pltpu.VMEM((192, 2048), BF16),
            pltpu.VMEM((96 * TILES, LANES), F32),
            pltpu.VMEM((32 * TILES, LANES), BF16),
            pltpu.VMEM((32 * TILES, LANES), BF16),
            pltpu.VMEM((32 * TILES, LANES), F32),
        ],
        compiler_params=pltpu.CompilerParams(vmem_limit_bytes=BIG),
        interpret=interpret,
        name="convolve",
    )(proj, ids, factor, taps, spec, outer3, twist, fwd, bwd, inv3)


def heads_kernel(hy_ref, w_ref, out_ref, state_ref, acc_ref):
    step = pl.program_id(0)

    @pl.when(step == 0)
    def _():
        acc_ref[...] = jnp.zeros_like(acc_ref)

    x = hy_ref[0]
    for k in range(3):
        acc_ref[k] += lax.dot_general(
            w_ref[k], x, (((0,), (0,)), ((), ())), preferred_element_type=F32
        )

    @pl.when(step == pl.num_programs(0) - 1)
    def _():
        heads = acc_ref[...].astype(BF16)
        out_ref[...] = heads
        for b in range(heads.shape[2] // BLOCK):
            at = slice(b * BLOCK, (b + 1) * BLOCK)
            state_ref[b] = lax.dot_general(
                heads[1, :, at],
                heads[2, :, at],
                (((1,), (1,)), ((), ())),
                preferred_element_type=F32,
            )


def heads_of(hyena, w, interpret=False):
    chans, depth, length = hyena.shape
    return pl.pallas_call(
        heads_kernel,
        grid=(chans,),
        in_specs=[
            pl.BlockSpec((1, depth, length), lambda c: (c, 0, 0)),
            pl.BlockSpec((3, depth, HD), lambda c: (0, c, 0)),
        ],
        out_specs=[
            pl.BlockSpec((3, HD, length), lambda c: (0, 0, 0)),
            pl.BlockSpec((length // BLOCK, HD, HD), lambda c: (0, 0, 0)),
        ],
        out_shape=(
            jax.ShapeDtypeStruct((3, HD, length), BF16),
            jax.ShapeDtypeStruct((length // BLOCK, HD, HD), F32),
        ),
        scratch_shapes=[pltpu.VMEM((3, HD, length), F32)],
        compiler_params=pltpu.CompilerParams(vmem_limit_bytes=BIG),
        interpret=interpret,
        name="heads",
    )(hyena, w)


def attention_kernel(heads_ref, state_ref, parts_ref, mine_ref, out_ref):
    mine = mine_ref[0]
    incoming = jnp.zeros((HD, HD), F32)
    for z in range(parts_ref.shape[0]):
        incoming = incoming + jnp.where(z < mine, parts_ref[z, 0] + parts_ref[z, 1], 0.0)
    length = heads_ref.shape[2]
    row = lax.broadcasted_iota(jnp.int32, (BLOCK, BLOCK), 0)
    column = lax.broadcasted_iota(jnp.int32, (BLOCK, BLOCK), 1)
    place = lax.broadcasted_iota(jnp.int32, (BLOCK, HD), 0)
    for b in range(length // BLOCK):
        at = slice(b * BLOCK, (b + 1) * BLOCK)
        queries = jnp.transpose(heads_ref[0, :, at].astype(F32)).astype(BF16)
        scores = mm(queries, heads_ref[1, :, at])
        scores = jnp.where(row >= column, scores, 0.0).astype(BF16)
        inside = lax.dot_general(
            scores, heads_ref[2, :, at], (((1,), (1,)), ((), ())), preferred_element_type=F32
        )
        carried = mm(queries, incoming.astype(BF16))
        position = mine * length + b * BLOCK + place + 1
        divisor = jnp.sqrt((position * HD).astype(F32))
        out_ref[at, :] = ((inside + carried) / divisor).astype(BF16)
        incoming = incoming + state_ref[b]


def attention(heads, state, parts, mine, interpret=False):
    vmem = pl.BlockSpec(memory_space=pltpu.VMEM)
    return pl.pallas_call(
        attention_kernel,
        in_specs=[vmem, vmem, vmem, pl.BlockSpec(memory_space=pltpu.SMEM)],
        out_shape=jax.ShapeDtypeStruct((heads.shape[2], HD), BF16),
        compiler_params=pltpu.CompilerParams(vmem_limit_bytes=BIG),
        interpret=interpret,
        name="attention",
    )(heads, state, parts, mine)


def here():
    return lax.axis_index("seq"), lax.axis_index("chan"), lax.axis_index("rep")


def greet(peers):
    barrier = pltpu.get_barrier_semaphore()
    for peer in peers:
        pl.semaphore_signal(barrier, inc=1, device_id=peer, device_id_type=MESH)
    pl.semaphore_wait(barrier, len(peers))


def push(src, dst, sems, index, peer):
    copy = pltpu.make_async_remote_copy(
        src_ref=src,
        dst_ref=dst,
        send_sem=sems[0].at[index],
        recv_sem=sems[1].at[index],
        device_id=peer,
        device_id_type=MESH,
    )
    copy.start()
    return copy


def comm_call(kernel, outs, copies, locals_, collective_id, name, *args):
    return pl.pallas_call(
        kernel,
        in_specs=[ANY] * len(args),
        out_specs=[ANY] * len(outs) if isinstance(outs, tuple) else ANY,
        out_shape=outs,
        scratch_shapes=[
            pltpu.SemaphoreType.DMA((copies,)),
            pltpu.SemaphoreType.DMA((copies,)),
            pltpu.SemaphoreType.DMA((locals_,)),
        ],
        compiler_params=pltpu.CompilerParams(collective_id=collective_id, has_side_effects=True),
        name=name,
    )(*args)


def share_kernel(rows_ref, side_ref, ids_ref, rows_out, side_out, ids_out, send, recv, own):
    z, c, r = here()
    sems = (send, recv)
    plane = [(z, lax.rem(c + j, 16), r) for j in range(1, 16)]
    line = [(lax.rem(z + j, 8), c, r) for j in range(1, 8)]
    greet(plane + line)
    copies = []
    for j, peer in enumerate(plane):
        copies.append(push(rows_ref, rows_out.at[c], sems, j, peer))
        copies.append(push(side_ref, side_out.at[c], sems, 15 + j, peer))
    for j, peer in enumerate(line):
        copies.append(push(ids_ref, ids_out.at[z], sems, 30 + j, peer))
    mine = [
        pltpu.make_async_copy(rows_ref, rows_out.at[c], own.at[0]),
        pltpu.make_async_copy(side_ref, side_out.at[c], own.at[1]),
        pltpu.make_async_copy(ids_ref, ids_out.at[z], own.at[2]),
    ]
    for copy in mine:
        copy.start()
    for copy in mine + copies:
        copy.wait()


def deal_kernel(proj_ref, factor_ref, proj_out, factor_out, send, recv, own):
    z, c, r = here()
    sems = (send, recv)
    slot = r * 8 + z
    peers = []
    for flip in range(2):
        for j in range(8):
            if flip or j:
                peers.append((lax.rem(z + j, 8), c, lax.rem(r + flip, 2)))
    greet(peers)

    def piece(to):
        return proj_ref.at[:, pl.ds(pl.multiple_of(to * 32, 32), 32), :]

    copies = []
    for index, peer in enumerate(peers):
        copies.append(push(piece(peer[0]), proj_out.at[slot], sems, index, peer))
    for j in range(7):
        copies.append(push(factor_ref, factor_out.at[z], sems, 15 + j, peers[j]))
    mine = [
        pltpu.make_async_copy(piece(z), proj_out.at[slot], own.at[0]),
        pltpu.make_async_copy(factor_ref, factor_out.at[z], own.at[1]),
    ]
    for copy in mine:
        copy.start()
    for copy in mine + copies:
        copy.wait()


def turn_kernel(y_ref, out_ref, send, recv, own):
    z, c, r = here()
    peers = [(lax.rem(z + j, 8), c, r) for j in range(1, 8)]
    greet(peers)
    place = out_ref.at[pl.ds(pl.multiple_of(z * 32, 32), 32), :]
    copies = [
        push(y_ref.at[peer[0]], place, (send, recv), j, peer) for j, peer in enumerate(peers)
    ]
    mine = pltpu.make_async_copy(y_ref.at[z], place, own.at[0])
    mine.start()
    mine.wait()
    for copy in copies:
        copy.wait()


def gather_kernel(x_ref, out_ref, send, recv, own):
    z, c, r = here()
    y, x = c // 4, lax.rem(c, 4)
    sems = (send, recv)

    def chan(at_x, at_y):
        return lax.rem(at_y + 8, 4) * 4 + lax.rem(at_x + 8, 4)

    def device(at_x, at_y):
        return (z, chan(at_x, at_y), r)

    greet([device(x + 1, y), device(x - 1, y), device(x, y + 1), device(x, y - 1)])
    half = x_ref.shape[0] // 2
    quarter = half // 2
    index = [0]
    sent = []

    def send_block(lead, along, across, part, direction, phase):
        axes = (0, 1) if lead == 0 else (1, 0)
        offset = [0, 0]
        offset[axes[0]], offset[axes[1]] = along, across
        origin = chan(x - offset[0], y - offset[1])
        step = [0, 0]
        step[axes[phase]] = direction
        target = device(x + step[0], y + step[1])
        start = lead * half + (0 if part is None else part * quarter)
        size = half if part is None else quarter
        rows = pl.ds(start, size)
        dst = out_ref.at[origin, rows, :]
        src = x_ref.at[rows, :] if along == 0 and across == 0 else dst
        number = index[0]
        index[0] += 1
        copy = push(src, dst, sems, number, target)
        sent.append(copy)
        came = [offset[0] + step[0], offset[1] + step[1]]
        landed = out_ref.at[chan(x - came[0], y - came[1]), rows, :]
        arrival = pltpu.make_async_remote_copy(
            src_ref=landed,
            dst_ref=landed,
            send_sem=send.at[number],
            recv_sem=recv.at[number],
            device_id=target,
            device_id_type=MESH,
        )
        return arrival

    mine = pltpu.make_async_copy(x_ref, out_ref.at[c], own.at[0])
    first = {}
    second = {}
    for lead in range(2):
        for d in (1, -1):
            first[lead, d] = send_block(lead, 0, 0, None, d, 0)
    for lead in range(2):
        for d in (1, -1):
            second[lead, 0, d] = send_block(lead, 0, 0, None, d, 1)
    mine.start()
    turned = {}
    for d in (1, -1):
        for lead in range(2):
            first[lead, d].wait_recv()
            turned[lead, d] = send_block(lead, d, 0, 0 if d == 1 else 1, d, 0)
            for e in (1, -1):
                second[lead, d, e] = send_block(lead, d, 0, None, e, 1)
    last = []

    def onward(lead, along):
        for e in (1, -1):
            second[lead, along, e].wait_recv()
            last.append(send_block(lead, along, e, 0 if e == 1 else 1, e, 1))

    for lead in range(2):
        onward(lead, 0)
    for lead in range(2):
        turned[lead, 1].wait_recv()
        turned[lead, -1].wait_recv()
        for e in (1, -1):
            second[lead, 2, e] = send_block(lead, 2, 0, None, e, 1)
    for along in (1, -1, 2):
        for lead in range(2):
            onward(lead, along)
    for arrival in last:
        arrival.wait_recv()
    for copy in sent:
        copy.wait_send()
    mine.wait()


def states_kernel(state_ref, out_ref, send, recv, own):
    z, c, r = here()
    peers = [(lax.rem(z + j, 8), c, r) for j in range(1, 8)]
    greet(peers)
    copies = [
        push(state_ref, out_ref.at[z], (send, recv), j, peer) for j, peer in enumerate(peers)
    ]
    mine = pltpu.make_async_copy(state_ref, out_ref.at[z], own.at[0])
    mine.start()
    mine.wait()
    for copy in copies:
        copy.wait()


def shards(
    fine_codes,
    coarse_codes,
    frame_order,
    emb_fine,
    emb_coarse,
    norm_gain,
    w_hyena,
    short_taps,
    long_filter,
    w_attn,
):
    z, r = lax.axis_index("seq"), lax.axis_index("rep")
    spec = spectrum(long_filter)
    ids, sums = local_ids(fine_codes, coarse_codes, frame_order, emb_fine, emb_coarse)
    fine_rows = lax.dynamic_slice_in_dim(emb_fine, z * 128, 128, 0)
    coarse_rows = lax.dynamic_slice_in_dim(emb_coarse, z * 128, 128, 0)
    rows = jnp.where(r == 0, fine_rows, coarse_rows)
    side = jnp.concatenate(
        [jnp.broadcast_to(norm_gain.astype(F32)[None], (8, 256)), sums], axis=1
    )
    rows_all, side_all, ids_all = comm_call(
        share_kernel,
        (
            jax.ShapeDtypeStruct((16, 128, 256), BF16),
            jax.ShapeDtypeStruct((16, 8, 384), F32),
            jax.ShapeDtypeStruct((8, 8, FRAME), jnp.int32),
        ),
        37,
        3,
        0,
        "share",
        rows,
        side,
        ids,
    )
    proj, factor = project(rows_all, side_all, jnp.transpose(w_hyena, (1, 0, 2)))
    proj_all, factor_all = comm_call(
        deal_kernel,
        (
            jax.ShapeDtypeStruct((16, 3, 32, 256), BF16),
            jax.ShapeDtypeStruct((8, 8, LANES), F32),
        ),
        22,
        2,
        1,
        "deal",
        proj,
        factor,
    )
    taps = lax.dynamic_slice_in_dim(short_taps, z * 2, 2, 1).reshape(6, LANES).astype(F32)
    y = convolve(
        proj_all.reshape(16, 96, 256), ids_all, factor_all.reshape(TILES, LANES), taps, spec
    )
    hyena_out = comm_call(
        turn_kernel, jax.ShapeDtypeStruct((256, 1024), BF16), 7, 1, 2, "turn", y
    )
    hyena_all = comm_call(
        gather_kernel, jax.ShapeDtypeStruct((16, 256, 1024), BF16), 40, 1, 3, "gather", hyena_out
    )
    heads, state = heads_of(hyena_all, jnp.transpose(w_attn, (1, 0, 2)))
    parts = comm_call(
        states_kernel, jax.ShapeDtypeStruct((8, 2, HD, HD), F32), 7, 1, 4, "states", state
    )
    attn_out = attention(heads, state, parts, z.astype(jnp.int32)[None])
    return (hyena_out, attn_out)


def solution(mesh):
    return jax.shard_map(
        shards,
        mesh=mesh,
        in_specs=(
            P(("rep", "seq")),
            P(("rep", "seq")),
            P(),
            P(None, "chan"),
            P(None, "chan"),
            P("chan"),
            P(None, None, "chan"),
            P(None, "chan", None),
            P(("chan", "seq"), None),
            P(None, None, "chan"),
        ),
        out_specs=(P("chan", ("rep", "seq")), P(("rep", "seq"), "chan")),
        check_vma=False,
    )
```

```python
import functools
import math

import jax
import jax.numpy as jnp
import numpy as np
from jax import lax
from jax.experimental import pallas as pl
from jax.experimental.pallas import tpu as pltpu
from jax.sharding import PartitionSpec as P

HD = 128
FRAME = 256
BLOCK = 512
LANES = 128
EPSILON = 1e-05
F32 = jnp.float32
BF16 = jnp.bfloat16
ANY = pl.BlockSpec(memory_space=pl.ANY)
MESH = pl.DeviceIdType.MESH
BIG = 56 << 20

ROWS_W = 72
TILES = 64
POINTS = 2 * TILES * LANES


def split_np(x):
    hi = np.asarray(x, np.float32).astype(jnp.bfloat16)
    lo = (np.asarray(x, np.float64) - hi.astype(np.float64)).astype(np.float32).astype(jnp.bfloat16)
    return hi, lo


@functools.lru_cache(None)
def tables():
    w = np.arange(ROWS_W)[:, None]
    kept = (w <= 64).astype(np.float64)
    q = np.arange(TILES)[None, :]
    angle = 2 * np.pi * ((w * q) % 128) / 128
    outer = np.concatenate([np.cos(angle) * kept, -np.sin(angle) * kept], 0)
    a = np.arange(LANES)[None, :]
    turn = 2 * np.pi * (w * a) / POINTS
    twist = np.stack([np.cos(turn) * kept, np.sin(turn) * kept]).astype(np.float32)
    m = np.arange(LANES)
    inner = 2 * np.pi * ((m[:, None] * m[None, :]) % 128) / 128
    c, s = np.cos(inner), np.sin(inner)
    forward = np.block([[c, -s], [s, c]])
    backward = np.block([[c, s], [-s, c]])
    weight = np.where((w == 0) | (w == 64), 1.0, 2.0) * kept / POINTS
    inverse = np.concatenate([(np.cos(angle) * weight).T, (-np.sin(angle) * weight).T], 1)
    outer_hi, outer_lo = split_np(outer)
    inv_hi, inv_lo = split_np(inverse)
    fwd = np.stack(split_np(forward))
    bwd = np.stack(split_np(backward))
    outer3 = np.concatenate([outer_hi, outer_lo, outer_hi], 1)
    inv3 = np.concatenate([inv_hi, inv_lo, inv_hi], 1)
    return outer3, twist, fwd, bwd, inv3


def split(x):
    hi = x.astype(BF16)
    return hi, (x - hi.astype(F32)).astype(BF16)


def mm(a, b):
    return jnp.dot(a, b, preferred_element_type=F32)


def mm3(x, table):
    hi, lo = split(x)
    return mm(hi, table[0]) + (mm(lo, table[0]) + mm(hi, table[1]))


def local_sums(fine_ref, coarse_ref, order_ref, emb_fine_ref, emb_coarse_ref, ids_ref, side_ref):
    order = order_ref[...]
    row = lax.broadcasted_iota(jnp.int32, (FRAME, FRAME), 0)
    pick = (row == order).astype(BF16)
    pick_half = (row[: FRAME // 2] == order // 2).astype(BF16)

    def looked(codes, pick):
        hi = (codes // 32).astype(F32).astype(BF16)
        lo = (codes % 32).astype(F32).astype(BF16)
        return (mm(hi, pick) * 32.0 + mm(lo, pick)).astype(jnp.int32)

    fine = looked(fine_ref[...], pick)
    coarse = looked(coarse_ref[...], pick_half)
    ids_ref[0:4, :] = fine
    ids_ref[4:8, :] = coarse
    vocab = lax.broadcasted_iota(jnp.int32, (emb_fine_ref.shape[0], FRAME), 0)
    dims = (((0,), (0,)), ((), ()))
    for frame in range(4):
        hot_fine = (vocab == fine[frame : frame + 1]).astype(BF16)
        hot_coarse = (vocab == coarse[frame : frame + 1]).astype(BF16)
        rows = lax.dot_general(emb_fine_ref[...], hot_fine, dims, preferred_element_type=F32)
        rows = rows + lax.dot_general(
            emb_coarse_ref[...], hot_coarse, dims, preferred_element_type=F32
        )
        rows = rows.astype(BF16).astype(F32)
        total = jnp.sum(rows * rows, axis=0, keepdims=True)
        side_ref[2 * frame : 2 * frame + 1, FRAME:] = total[:, :LANES]
        side_ref[2 * frame + 1 : 2 * frame + 2, FRAME:] = total[:, LANES:]


def project_kernel(rows_ref, side_ref, w_ref, out_ref, factor_ref, x_ref):
    chans = rows_ref.shape[0]

    @pl.when(pl.program_id(0) == 0)
    def _():
        for c in range(chans):
            x = rows_ref[c].astype(F32) * side_ref[c, 0:1, :FRAME]
            hi, lo = split(x)
            x_ref[0:128, c * 256 : (c + 1) * 256] = hi
            x_ref[128:256, c * 256 : (c + 1) * 256] = lo
        total = side_ref[0, :, FRAME:]
        for c in range(1, chans):
            total = total + side_ref[c, :, FRAME:]
        factor_ref[...] = lax.rsqrt(total / (chans * 256.0) + EPSILON)

    both = mm(x_ref[...], w_ref[0])
    hi, lo = split(jnp.transpose(both[:128] + both[128:]))
    out_ref[0, :, :128] = hi
    out_ref[0, :, 128:] = lo


def project(rows, side, w, interpret=False):
    chans = rows.shape[0]
    depth = w.shape[1]
    return pl.pallas_call(
        project_kernel,
        grid=(3,),
        in_specs=[
            pl.BlockSpec(rows.shape, lambda k: (0, 0, 0)),
            pl.BlockSpec(side.shape, lambda k: (0, 0, 0)),
            pl.BlockSpec((1, depth, 256), lambda k: (k, 0, 0)),
        ],
        out_specs=[
            pl.BlockSpec((1, 256, 256), lambda k: (k, 0, 0)),
            pl.BlockSpec((8, LANES), lambda k: (0, 0)),
        ],
        out_shape=(
            jax.ShapeDtypeStruct((3, 256, 256), BF16),
            jax.ShapeDtypeStruct((8, LANES), F32),
        ),
        scratch_shapes=[pltpu.VMEM((256, chans * 256), BF16)],
        compiler_params=pltpu.CompilerParams(vmem_limit_bytes=BIG),
        interpret=interpret,
        name="project",
    )(rows, side, w)


GROUP = 4


def twisted(step, twist_ref):
    cos, sin = twist_ref[0], twist_ref[1]
    rows = []
    for i in range(GROUP):
        re = step[:ROWS_W, i * LANES : (i + 1) * LANES]
        im = step[ROWS_W:, i * LANES : (i + 1) * LANES]
        rows.append(jnp.concatenate([re * cos + im * sin, im * cos - re * sin], 1))
    return jnp.concatenate(rows, 0)


def spectrum_kernel(h_ref, outer_ref, twist_ref, fwd_ref, out_ref, wide_ref):
    channels = h_ref.shape[0]
    for q in range(TILES):
        wide_ref[pl.ds(q, channels, stride=TILES), :] = h_ref[:, q * LANES : (q + 1) * LANES]

    @pl.loop(0, channels // GROUP)
    def _(step):
        pieces = []
        for i in range(GROUP):
            hi, lo = split(wide_ref[pl.ds((step * GROUP + i) * TILES, TILES), :])
            pieces.append(jnp.concatenate([hi, hi, lo], 0))
        first = mm(outer_ref[...], jnp.concatenate(pieces, 1))
        out_ref[pl.ds(step * GROUP * ROWS_W, GROUP * ROWS_W), :] = mm3(
            twisted(first, twist_ref), fwd_ref
        )


def convolve_kernel(
    proj_ref,
    ids_ref,
    factor_ref,
    taps_ref,
    spec_ref,
    outer_ref,
    twist_ref,
    fwd_ref,
    bwd_ref,
    inv_ref,
    out_ref,
    left_ref,
    wide_ref,
    gate_ref,
    mix_ref,
    y_ref,
):
    channels = 32
    for s in range(16):
        left_ref[0:96, s * 128 : (s + 1) * 128] = proj_ref[s, :, :128]
        left_ref[96:192, s * 128 : (s + 1) * 128] = proj_ref[s, :, 128:]
    vocab = lax.broadcasted_iota(jnp.int32, (1024, FRAME), 0)

    @pl.loop(0, 8)
    def _(z):
        ids = ids_ref[z]
        for i in range(4):
            hot = jnp.concatenate(
                [
                    (vocab == ids[i : i + 1]).astype(BF16),
                    (vocab == ids[4 + i : 5 + i]).astype(BF16),
                ],
                0,
            )
            both = mm(left_ref[...], hot)
            value = both[:96] + both[96:]
            for half in range(2):
                wide_ref[pl.ds(z * 8 + 2 * i + half, 96, stride=TILES), :] = value[
                    :, half * LANES : (half + 1) * LANES
                ]

    tap_row = lax.broadcasted_iota(jnp.int32, (LANES, LANES), 0)
    tap_col = lax.broadcasted_iota(jnp.int32, (LANES, LANES), 1)
    rows = 16 * TILES
    first_tile = lax.broadcasted_iota(jnp.int32, (rows, LANES), 0) % TILES == 0
    scale = jnp.concatenate([factor_ref[...]] * 16, 0)

    def filtered(k, g):
        taps = jnp.broadcast_to(taps_ref[2 * k + g : 2 * k + g + 1, :], (LANES, LANES))
        turned = pltpu.roll(taps, 0, 1, stride=1, stride_axis=0)
        both = jnp.concatenate(
            [
                jnp.where(tap_col >= tap_row, turned, 0.0),
                jnp.where(tap_col < tap_row, turned, 0.0),
            ],
            1,
        ).astype(BF16)
        start = (2 * k + g) * rows
        x = (wide_ref[start : start + rows, :] * scale).astype(BF16)
        parts = mm(x, both)
        carried = jnp.where(first_tile, 0.0, pltpu.roll(parts[:, LANES:], 1, 0))
        return (parts[:, :LANES] + carried).astype(BF16)

    for g in range(2):
        gate_ref[g * rows : (g + 1) * rows, :] = filtered(0, g)
        left = filtered(1, g).astype(F32)
        mix_ref[g * rows : (g + 1) * rows, :] = (left * filtered(2, g).astype(F32)).astype(BF16)

    @pl.loop(0, channels // GROUP)
    def _(step):
        pieces = []
        for i in range(GROUP):
            x = mix_ref[pl.ds((step * GROUP + i) * TILES, TILES), :]
            pieces.append(jnp.concatenate([x, x], 0))
        first = mm(outer_ref[:, : 2 * TILES], jnp.concatenate(pieces, 1))
        spec = mm3(twisted(first, twist_ref), fwd_ref)
        other = spec_ref[pl.ds(step * GROUP * ROWS_W, GROUP * ROWS_W), :]
        re, im = spec[:, :LANES], spec[:, LANES:]
        ore, oim = other[:, :LANES], other[:, LANES:]
        back = mm3(jnp.concatenate([re * ore - im * oim, re * oim + im * ore], 1), bwd_ref)
        cos, sin = twist_ref[0], twist_ref[1]
        columns = []
        for i in range(GROUP):
            bre = back[i * ROWS_W : (i + 1) * ROWS_W, :LANES]
            bim = back[i * ROWS_W : (i + 1) * ROWS_W, LANES:]
            undone = jnp.concatenate([bre * cos - bim * sin, bim * cos + bre * sin], 0)
            hi, lo = split(undone)
            columns.append(jnp.concatenate([hi, hi, lo], 0))
        result = mm(inv_ref[...], jnp.concatenate(columns, 1))
        for i in range(GROUP):
            at = pl.ds((step * GROUP + i) * TILES, TILES)
            conv = result[:, i * LANES : (i + 1) * LANES].astype(BF16).astype(F32)
            y_ref[at, :] = gate_ref[at, :].astype(F32) * conv

    for q in range(TILES):
        out_ref[q // 8, :, (q % 8) * LANES : (q % 8 + 1) * LANES] = y_ref[
            pl.ds(q, channels, stride=TILES), :
        ].astype(BF16)


def convolve(proj, ids, factor, taps, spec, interpret=False):
    outer3, twist, fwd, bwd, inv3 = tables()
    return pl.pallas_call(
        convolve_kernel,
        out_shape=jax.ShapeDtypeStruct((8, 32, 1024), BF16),
        scratch_shapes=[
            pltpu.VMEM((192, 2048), BF16),
            pltpu.VMEM((96 * TILES, LANES), F32),
            pltpu.VMEM((32 * TILES, LANES), BF16),
            pltpu.VMEM((32 * TILES, LANES), BF16),
            pltpu.VMEM((32 * TILES, LANES), F32),
        ],
        compiler_params=pltpu.CompilerParams(vmem_limit_bytes=BIG),
        interpret=interpret,
        name="convolve",
    )(proj, ids, factor, taps, spec, outer3, twist, fwd, bwd, inv3)


def here():
    return lax.axis_index("seq"), lax.axis_index("chan"), lax.axis_index("rep")


def greet(peers):
    barrier = pltpu.get_barrier_semaphore()
    for peer in peers:
        pl.semaphore_signal(barrier, inc=1, device_id=peer, device_id_type=MESH)
    pl.semaphore_wait(barrier, len(peers))


def push(src, dst, sems, index, peer):
    copy = pltpu.make_async_remote_copy(
        src_ref=src,
        dst_ref=dst,
        send_sem=sems[0].at[index],
        recv_sem=sems[1].at[index],
        device_id=peer,
        device_id_type=MESH,
    )
    copy.start()
    return copy


def share_kernel(
    fine_ref,
    coarse_ref,
    order_ref,
    emb_fine_ref,
    emb_coarse_ref,
    gain_ref,
    filter_ref,
    outer_ref,
    twist_ref,
    fwd_ref,
    rows_out,
    side_out,
    ids_out,
    spec_ref,
    rows_ref,
    side_ref,
    ids_ref,
    wide_ref,
    send,
    recv,
    own,
):
    z, c, r = here()
    sems = (send, recv)
    plane = [(z, lax.rem(c + j, 16), r) for j in range(1, 16)]
    line = [(lax.rem(z + j, 8), c, r) for j in range(1, 8)]
    at = pl.ds(pl.multiple_of(z * 128, 128), 128)

    @pl.when(r == 0)
    def _():
        rows_ref[...] = emb_fine_ref[at, :]

    @pl.when(r != 0)
    def _():
        rows_ref[...] = emb_coarse_ref[at, :]

    greet(plane + line)
    copies = []
    for j, peer in enumerate(plane):
        copies.append(push(rows_ref, rows_out.at[c], sems, j, peer))
    side_ref[:, :FRAME] = jnp.broadcast_to(gain_ref[...].astype(F32), (8, FRAME))
    local_sums(fine_ref, coarse_ref, order_ref, emb_fine_ref, emb_coarse_ref, ids_ref, side_ref)
    for j, peer in enumerate(plane):
        copies.append(push(side_ref, side_out.at[c], sems, 15 + j, peer))
    for j, peer in enumerate(line):
        copies.append(push(ids_ref, ids_out.at[z], sems, 30 + j, peer))
    mine = [
        pltpu.make_async_copy(rows_ref, rows_out.at[c], own.at[0]),
        pltpu.make_async_copy(side_ref, side_out.at[c], own.at[1]),
        pltpu.make_async_copy(ids_ref, ids_out.at[z], own.at[2]),
    ]
    for copy in mine:
        copy.start()
    spectrum_kernel(filter_ref, outer_ref, twist_ref, fwd_ref, spec_ref, wide_ref)
    for copy in mine + copies:
        copy.wait()


def share(fine, coarse, order, emb_fine, emb_coarse, gain, long_filter):
    outer3, twist, fwd, _, _ = tables()
    channels = long_filter.shape[0]
    vmem = pl.BlockSpec(memory_space=pltpu.VMEM)
    return pl.pallas_call(
        share_kernel,
        in_specs=[vmem] * 10,
        out_specs=[ANY, ANY, ANY, vmem],
        out_shape=(
            jax.ShapeDtypeStruct((16, 128, 256), BF16),
            jax.ShapeDtypeStruct((16, 8, 384), F32),
            jax.ShapeDtypeStruct((8, 8, FRAME), jnp.int32),
            jax.ShapeDtypeStruct((channels * ROWS_W, 256), F32),
        ),
        scratch_shapes=[
            pltpu.VMEM((128, 256), BF16),
            pltpu.VMEM((8, 384), F32),
            pltpu.VMEM((8, FRAME), jnp.int32),
            pltpu.VMEM((channels * TILES, LANES), F32),
            pltpu.SemaphoreType.DMA((37,)),
            pltpu.SemaphoreType.DMA((37,)),
            pltpu.SemaphoreType.DMA((3,)),
        ],
        compiler_params=pltpu.CompilerParams(
            collective_id=0, has_side_effects=True, vmem_limit_bytes=BIG
        ),
        name="share",
    )(
        fine.reshape(4, FRAME),
        coarse.reshape(4, FRAME // 2),
        order[None],
        emb_fine,
        emb_coarse,
        gain[None],
        long_filter,
        outer3,
        twist,
        fwd,
    )


def deal_kernel(proj_ref, factor_ref, proj_out, factor_out, send, recv, own):
    z, c, r = here()
    sems = (send, recv)
    slot = r * 8 + z
    line = [(lax.rem(z + j, 8), c, r) for j in range(1, 8)]
    sibling = (z, c, 1 - r)
    greet(line + [sibling])

    def piece(to):
        return proj_ref.at[:, pl.ds(pl.multiple_of(to * 32, 32), 32), :]

    copies = []
    for j, peer in enumerate(line):
        copies.append(push(piece(peer[0]), proj_out.at[slot], sems, j, peer))
    for j, peer in enumerate(line):
        copies.append(push(factor_ref, factor_out.at[z], sems, 7 + j, peer))
    across = [push(piece(z), proj_out.at[slot], sems, 14, sibling)]
    mine = [
        pltpu.make_async_copy(piece(z), proj_out.at[slot], own.at[0]),
        pltpu.make_async_copy(factor_ref, factor_out.at[z], own.at[1]),
    ]
    for copy in mine:
        copy.start()
    for j in range(7):
        copies[j].wait_recv()
        landed = proj_out.at[r * 8 + lax.rem(z + 7 - j, 8)]
        across.append(push(landed, landed, sems, 15 + j, sibling))
    for copy in across + copies[7:]:
        copy.wait_recv()
    for copy in across + copies:
        copy.wait_send()
    for copy in mine:
        copy.wait()


def deal(proj, factor):
    return pl.pallas_call(
        deal_kernel,
        in_specs=[ANY] * 2,
        out_specs=[ANY] * 2,
        out_shape=(
            jax.ShapeDtypeStruct((16, 3, 32, 256), BF16),
            jax.ShapeDtypeStruct((8, 8, LANES), F32),
        ),
        scratch_shapes=[
            pltpu.SemaphoreType.DMA((22,)),
            pltpu.SemaphoreType.DMA((22,)),
            pltpu.SemaphoreType.DMA((2,)),
        ],
        compiler_params=pltpu.CompilerParams(collective_id=1, has_side_effects=True),
        name="deal",
    )(proj, factor)


CHUNKS = 2


def tail_kernel(
    y_ref,
    w_ref,
    hyena_ref,
    attn_ref,
    wv_ref,
    x_ref,
    land_ref,
    acc_ref,
    state_ref,
    parts_ref,
    prefix_ref,
    incoming_ref,
    send,
    recv,
    own,
):
    z, c, r = here()
    y, x = c // 4, lax.rem(c, 4)
    sems = (send, recv)
    length = x_ref.shape[1]
    span = length // CHUNKS

    def chan(at_x, at_y):
        return lax.rem(at_y + 8, 4) * 4 + lax.rem(at_x + 8, 4)

    def device(at_x, at_y):
        return (z, chan(at_x, at_y), r)

    line = [(lax.rem(z + j, 8), c, r) for j in range(1, 8)]
    weights = pltpu.make_async_copy(w_ref, wv_ref, own.at[0])
    weights.start()
    greet(line + [device(x + 1, y), device(x - 1, y), device(x, y + 1), device(x, y - 1)])
    index = [0]
    sent = []

    def tell(src, dst, peer):
        copy = push(src, dst, sems, index[0], peer)
        index[0] += 1
        sent.append(copy)
        return copy

    mine_rows = pl.ds(pl.multiple_of(z * 32, 32), 32)
    turned = []
    kept = []
    for t in range(CHUNKS):
        at = pl.ds(t * span, span)
        kept.append(
            pltpu.make_async_copy(y_ref.at[z, :, at], x_ref.at[mine_rows, at], own.at[1 + t])
        )
        kept[-1].start()
        turned.append([tell(y_ref.at[p[0], :, at], x_ref.at[mine_rows, at], p) for p in line])
    half = x_ref.shape[0] // 2
    quarter = half // 2

    def send_block(t, lead, along, across, part, direction, phase):
        axes = (0, 1) if lead == 0 else (1, 0)
        offset = [0, 0]
        offset[axes[0]], offset[axes[1]] = along, across
        step = [0, 0]
        step[axes[phase]] = direction
        target = device(x + step[0], y + step[1])
        start = lead * half + (0 if part is None else part * quarter)
        rows = pl.ds(start, half if part is None else quarter)
        at = pl.ds(t * span, span)
        dst = land_ref.at[chan(x - offset[0], y - offset[1]), rows, at]
        src = x_ref.at[rows, at] if along == 0 and across == 0 else dst
        number = index[0]
        tell(src, dst, target)
        came = [offset[0] + step[0], offset[1] + step[1]]
        landed = land_ref.at[chan(x - came[0], y - came[1]), rows, at]
        return pltpu.make_async_remote_copy(
            src_ref=landed,
            dst_ref=landed,
            send_sem=send.at[number],
            recv_sem=recv.at[number],
            device_id=target,
            device_id_type=MESH,
        )

    first = {}
    second = {}
    forward = {}
    pending = []

    def multiply(t, lead, along, across):
        at = slice(t * span, (t + 1) * span)
        rows = slice(lead * half, (lead + 1) * half)
        offset = (along, across) if lead == 0 else (across, along)
        origin = chan(x - offset[0], y - offset[1])
        block = x_ref[rows, at] if offset == (0, 0) else land_ref[origin, rows, at]
        depth = pl.ds(pl.multiple_of(origin * 2 * half + lead * half, half), half)
        for k in range(3):
            product = lax.dot_general(
                wv_ref[k, depth, :], block, (((0,), (0,)), ((), ())), preferred_element_type=F32
            )
            if (along, across, lead) == (0, 0, 0):
                acc_ref[k, :, at] = product
            else:
                acc_ref[k, :, at] += product

    def drain(count):
        for _ in range(min(count, len(pending))):
            multiply(*pending.pop(0))

    def open_chunk(t):
        kept[t].wait()
        for copy in turned[t]:
            copy.wait_recv()
        for lead in range(2):
            for d in (1, -1):
                first[t, lead, d] = send_block(t, lead, 0, 0, None, d, 0)
        for lead in range(2):
            for d in (1, -1):
                second[t, lead, 0, d] = send_block(t, lead, 0, 0, None, d, 1)
        for lead in range(2):
            pending.append((t, lead, 0, 0))

    last = []

    def onward(t, lead, along):
        for e in (1, -1):
            second[t, lead, along, e].wait_recv()
            last.append((t, lead, along, send_block(t, lead, along, e, 0 if e == 1 else 1, e, 1)))
        for e in (1, -1):
            pending.append((t, lead, along, e))

    for t in range(CHUNKS):
        open_chunk(t)
    weights.wait()
    back = pltpu.make_async_copy(x_ref, hyena_ref, own.at[CHUNKS + 1])
    back.start()
    for t in range(CHUNKS):
        for d in (1, -1):
            for lead in range(2):
                first[t, lead, d].wait_recv()
                forward[t, lead, d] = send_block(t, lead, d, 0, 0 if d == 1 else 1, d, 0)
                for e in (1, -1):
                    second[t, lead, d, e] = send_block(t, lead, d, 0, None, e, 1)
                pending.append((t, lead, d, 0))
        drain(2)
        for lead in range(2):
            onward(t, lead, 0)
            drain(1)
        for lead in range(2):
            forward[t, lead, 1].wait_recv()
            forward[t, lead, -1].wait_recv()
            for e in (1, -1):
                second[t, lead, 2, e] = send_block(t, lead, 2, 0, None, e, 1)
            pending.append((t, lead, 2, 0))
            drain(1)
    for t in range(CHUNKS):
        for along in (1, -1, 2):
            for lead in range(2):
                onward(t, lead, along)
                drain(3)
    for t, lead, along, arrival in last:
        arrival.wait_recv()
    for position in range(0, len(last), 2):
        t, lead, along, _ = last[position]
        pending.append((t, lead, along, 2))
    drain(len(pending))

    blocks = length // BLOCK
    heads = [[acc_ref[k, :, b * BLOCK : (b + 1) * BLOCK].astype(BF16) for b in range(blocks)] for k in range(3)]
    states = [
        lax.dot_general(
            heads[1][b], heads[2][b], (((1,), (1,)), ((), ())), preferred_element_type=F32
        )
        for b in range(blocks)
    ]
    total = states[0]
    for b in range(1, blocks):
        total = total + states[b]
    state_ref[...] = total.reshape(8, HD // 8, HD)
    parts_ref[z] = state_ref[z]
    gathered = [tell(state_ref.at[p[0]], parts_ref.at[z], p) for p in line]
    row = lax.broadcasted_iota(jnp.int32, (BLOCK, BLOCK), 0)
    column = lax.broadcasted_iota(jnp.int32, (BLOCK, BLOCK), 1)
    queries = []
    inside = []

    def local(b):
        queries.append(jnp.transpose(heads[0][b].astype(F32)).astype(BF16))
        scores = mm(queries[b], heads[1][b])
        scores = jnp.where(row >= column, scores, 0.0).astype(BF16)
        inside.append(
            lax.dot_general(
                scores, heads[2][b], (((1,), (1,)), ((), ())), preferred_element_type=F32
            )
        )

    local(0)
    for copy in gathered:
        copy.wait_recv()
    running = jnp.zeros((HD // 8, HD), F32)
    for step in range(8):
        prefix_ref[step] = running
        running = running + parts_ref[step]
    incoming_ref[z] = prefix_ref[z]
    dealt = [tell(prefix_ref.at[p[0]], incoming_ref.at[z], p) for p in line]
    for b in range(1, blocks):
        local(b)
    for copy in dealt:
        copy.wait_recv()
    earlier = incoming_ref[...].reshape(HD, HD)
    place = lax.broadcasted_iota(jnp.int32, (BLOCK, HD), 0)
    for b in range(blocks):
        carried = mm(queries[b], earlier.astype(BF16))
        position = z * length + b * BLOCK + place + 1
        divisor = jnp.sqrt((position * HD).astype(F32))
        attn_ref[b * BLOCK : (b + 1) * BLOCK, :] = ((inside[b] + carried) / divisor).astype(BF16)
        earlier = earlier + states[b]
    for copy in sent:
        copy.wait_send()
    back.wait()


def tail(y, w):
    seqs, channels, length = y.shape
    depth = seqs * channels
    vmem = pl.BlockSpec(memory_space=pltpu.VMEM)
    copies = CHUNKS * (7 + 40) + 14
    return pl.pallas_call(
        tail_kernel,
        in_specs=[ANY, ANY],
        out_specs=[ANY, vmem],
        out_shape=(
            jax.ShapeDtypeStruct((depth, length), BF16),
            jax.ShapeDtypeStruct((length, HD), BF16),
        ),
        scratch_shapes=[
            pltpu.VMEM(w.shape, BF16),
            pltpu.VMEM((depth, length), BF16),
            pltpu.VMEM((16, depth, length), BF16),
            pltpu.VMEM((3, HD, length), F32),
            pltpu.VMEM((8, HD // 8, HD), F32),
            pltpu.VMEM((8, HD // 8, HD), F32),
            pltpu.VMEM((8, HD // 8, HD), F32),
            pltpu.VMEM((8, HD // 8, HD), F32),
            pltpu.SemaphoreType.DMA((copies,)),
            pltpu.SemaphoreType.DMA((copies,)),
            pltpu.SemaphoreType.DMA((CHUNKS + 2,)),
        ],
        compiler_params=pltpu.CompilerParams(
            collective_id=2, has_side_effects=True, vmem_limit_bytes=BIG
        ),
        name="tail",
    )(y, w)


def shards(
    fine_codes,
    coarse_codes,
    frame_order,
    emb_fine,
    emb_coarse,
    norm_gain,
    w_hyena,
    short_taps,
    long_filter,
    w_attn,
):
    z = lax.axis_index("seq")
    rows_all, side_all, ids_all, spec = share(
        fine_codes, coarse_codes, frame_order, emb_fine, emb_coarse, norm_gain, long_filter
    )
    proj, factor = project(rows_all, side_all, jnp.transpose(w_hyena, (1, 0, 2)))
    proj_all, factor_all = deal(proj, factor)
    taps = lax.dynamic_slice_in_dim(short_taps, z * 2, 2, 1).reshape(6, LANES).astype(F32)
    y = convolve(
        proj_all.reshape(16, 96, 256), ids_all, factor_all.reshape(TILES, LANES), taps, spec
    )
    return tail(y, jnp.transpose(w_attn, (1, 0, 2)))


def solution(mesh):
    return jax.shard_map(
        shards,
        mesh=mesh,
        in_specs=(
            P(("rep", "seq")),
            P(("rep", "seq")),
            P(),
            P(None, "chan"),
            P(None, "chan"),
            P("chan"),
            P(None, None, "chan"),
            P(None, "chan", None),
            P(("chan", "seq"), None),
            P(None, None, "chan"),
        ),
        out_specs=(P("chan", ("rep", "seq")), P(("rep", "seq"), "chan")),
        check_vma=False,
    )
```

```python
import functools
import math

import jax
import jax.numpy as jnp
import numpy as np
from jax import lax
from jax.experimental import pallas as pl
from jax.experimental.pallas import tpu as pltpu
from jax.sharding import PartitionSpec as P

HD = 128
FRAME = 256
BLOCK = 512
LANES = 128
EPSILON = 1e-05
F32 = jnp.float32
BF16 = jnp.bfloat16
ANY = pl.BlockSpec(memory_space=pl.ANY)
MESH = pl.DeviceIdType.MESH
BIG = 56 << 20

ROWS_W = 72
TILES = 64
POINTS = 2 * TILES * LANES


def split_np(x):
    hi = np.asarray(x, np.float32).astype(jnp.bfloat16)
    lo = (np.asarray(x, np.float64) - hi.astype(np.float64)).astype(np.float32).astype(jnp.bfloat16)
    return hi, lo


@functools.lru_cache(None)
def tables():
    w = np.arange(ROWS_W)[:, None]
    kept = (w <= 64).astype(np.float64)
    q = np.arange(TILES)[None, :]
    angle = 2 * np.pi * ((w * q) % 128) / 128
    outer = np.concatenate([np.cos(angle) * kept, -np.sin(angle) * kept], 0)
    a = np.arange(LANES)[None, :]
    turn = 2 * np.pi * (w * a) / POINTS
    twist = np.stack([np.cos(turn) * kept, np.sin(turn) * kept]).astype(np.float32)
    m = np.arange(LANES)
    inner = 2 * np.pi * ((m[:, None] * m[None, :]) % 128) / 128
    c, s = np.cos(inner), np.sin(inner)
    forward = np.block([[c, -s], [s, c]])
    backward = np.block([[c, s], [-s, c]])
    weight = np.where((w == 0) | (w == 64), 1.0, 2.0) * kept / POINTS
    inverse = np.concatenate([(np.cos(angle) * weight).T, (-np.sin(angle) * weight).T], 1)
    outer_hi, outer_lo = split_np(outer)
    inv_hi, inv_lo = split_np(inverse)
    fwd = np.stack(split_np(forward))
    bwd = np.stack(split_np(backward))
    outer3 = np.concatenate([outer_hi, outer_lo, outer_hi], 1)
    inv3 = np.concatenate([inv_hi, inv_lo, inv_hi], 1)
    return outer3, twist, fwd, bwd, inv3


def split(x):
    hi = x.astype(BF16)
    return hi, (x - hi.astype(F32)).astype(BF16)


def mm(a, b):
    return jnp.dot(a, b, preferred_element_type=F32)


def mm3(x, table):
    hi, lo = split(x)
    return mm(hi, table[0]) + (mm(lo, table[0]) + mm(hi, table[1]))


def local_sums(codes_ref, order, emb_fine_ref, emb_coarse_ref, ids_ref, sums_ref):
    row = lax.broadcasted_iota(jnp.int32, (FRAME, FRAME), 0)
    pick = (row == order).astype(BF16)
    pick_half = (row[: FRAME // 2] == order // 2).astype(BF16)

    def looked(codes, pick):
        hi = (codes // 32).astype(F32).astype(BF16)
        lo = (codes % 32).astype(F32).astype(BF16)
        return (mm(hi, pick) * 32.0 + mm(lo, pick)).astype(jnp.int32)

    fine = looked(codes_ref[0:4, :], pick)
    coarse = looked(codes_ref[4:8, : FRAME // 2], pick_half)
    ids_ref[0:4, :] = fine
    ids_ref[4:8, :] = coarse
    vocab = lax.broadcasted_iota(jnp.int32, (emb_fine_ref.shape[0], FRAME), 0)
    dims = (((0,), (0,)), ((), ()))
    for frame in range(4):
        hot_fine = (vocab == fine[frame : frame + 1]).astype(BF16)
        hot_coarse = (vocab == coarse[frame : frame + 1]).astype(BF16)
        rows = lax.dot_general(emb_fine_ref[...], hot_fine, dims, preferred_element_type=F32)
        rows = rows + lax.dot_general(
            emb_coarse_ref[...], hot_coarse, dims, preferred_element_type=F32
        )
        rows = rows.astype(BF16).astype(F32)
        total = jnp.sum(rows * rows, axis=0, keepdims=True)
        sums_ref[2 * frame : 2 * frame + 1, :] = total[:, :LANES]
        sums_ref[2 * frame + 1 : 2 * frame + 2, :] = total[:, LANES:]


GROUP = 4


def twisted(step, twist_ref):
    cos, sin = twist_ref[0], twist_ref[1]
    rows = []
    for i in range(GROUP):
        re = step[:ROWS_W, i * LANES : (i + 1) * LANES]
        im = step[ROWS_W:, i * LANES : (i + 1) * LANES]
        rows.append(jnp.concatenate([re * cos + im * sin, im * cos - re * sin], 1))
    return jnp.concatenate(rows, 0)


def spectrum_kernel(h_ref, outer_ref, twist_ref, fwd_ref, out_ref, wide_ref):
    channels = h_ref.shape[0]
    for q in range(TILES):
        wide_ref[pl.ds(q, channels, stride=TILES), :] = h_ref[:, q * LANES : (q + 1) * LANES]

    @pl.loop(0, channels // GROUP)
    def _(step):
        pieces = []
        for i in range(GROUP):
            hi, lo = split(wide_ref[pl.ds((step * GROUP + i) * TILES, TILES), :])
            pieces.append(jnp.concatenate([hi, hi, lo], 0))
        first = mm(outer_ref[...], jnp.concatenate(pieces, 1))
        out_ref[pl.ds(step * GROUP * ROWS_W, GROUP * ROWS_W), :] = mm3(
            twisted(first, twist_ref), fwd_ref
        )


def convolve_kernel(
    proj_ref,
    ids_ref,
    factor_ref,
    taps_ref,
    spec_ref,
    outer_ref,
    twist_ref,
    fwd_ref,
    bwd_ref,
    inv_ref,
    out_ref,
    left_ref,
    wide_ref,
    gate_ref,
    mix_ref,
    y_ref,
):
    channels = 32
    for s in range(16):
        left_ref[0:96, s * 128 : (s + 1) * 128] = proj_ref[s, :, :128]
        left_ref[96:192, s * 128 : (s + 1) * 128] = proj_ref[s, :, 128:]
    vocab = lax.broadcasted_iota(jnp.int32, (1024, FRAME), 0)

    @pl.loop(0, 8)
    def _(z):
        ids = ids_ref[z]
        for i in range(4):
            hot = jnp.concatenate(
                [
                    (vocab == ids[i : i + 1]).astype(BF16),
                    (vocab == ids[4 + i : 5 + i]).astype(BF16),
                ],
                0,
            )
            both = mm(left_ref[...], hot)
            value = both[:96] + both[96:]
            for half in range(2):
                wide_ref[pl.ds(z * 8 + 2 * i + half, 96, stride=TILES), :] = value[
                    :, half * LANES : (half + 1) * LANES
                ]

    tap_row = lax.broadcasted_iota(jnp.int32, (LANES, LANES), 0)
    tap_col = lax.broadcasted_iota(jnp.int32, (LANES, LANES), 1)
    group_row = lax.broadcasted_iota(jnp.int32, taps_ref.shape[1:], 0)
    rows = 16 * TILES
    first_tile = lax.broadcasted_iota(jnp.int32, (rows, LANES), 0) % TILES == 0
    scale = jnp.concatenate([factor_ref[...]] * 16, 0)

    def filtered(k, g):
        wanted = 2 * lax.axis_index("seq") + g
        own = jnp.where(group_row == wanted, taps_ref[k].astype(F32), 0.0)
        taps = jnp.broadcast_to(jnp.sum(own, axis=0, keepdims=True), (LANES, LANES))
        turned = pltpu.roll(taps, 0, 1, stride=1, stride_axis=0)
        both = jnp.concatenate(
            [
                jnp.where(tap_col >= tap_row, turned, 0.0),
                jnp.where(tap_col < tap_row, turned, 0.0),
            ],
            1,
        ).astype(BF16)
        start = (2 * k + g) * rows
        x = (wide_ref[start : start + rows, :] * scale).astype(BF16)
        parts = mm(x, both)
        carried = jnp.where(first_tile, 0.0, pltpu.roll(parts[:, LANES:], 1, 0))
        return (parts[:, :LANES] + carried).astype(BF16)

    for g in range(2):
        gate_ref[g * rows : (g + 1) * rows, :] = filtered(0, g)
        left = filtered(1, g).astype(F32)
        mix_ref[g * rows : (g + 1) * rows, :] = (left * filtered(2, g).astype(F32)).astype(BF16)

    @pl.loop(0, channels // GROUP)
    def _(step):
        pieces = []
        for i in range(GROUP):
            x = mix_ref[pl.ds((step * GROUP + i) * TILES, TILES), :]
            pieces.append(jnp.concatenate([x, x], 0))
        first = mm(outer_ref[:, : 2 * TILES], jnp.concatenate(pieces, 1))
        spec = mm3(twisted(first, twist_ref), fwd_ref)
        other = spec_ref[pl.ds(step * GROUP * ROWS_W, GROUP * ROWS_W), :]
        re, im = spec[:, :LANES], spec[:, LANES:]
        ore, oim = other[:, :LANES], other[:, LANES:]
        back = mm3(jnp.concatenate([re * ore - im * oim, re * oim + im * ore], 1), bwd_ref)
        cos, sin = twist_ref[0], twist_ref[1]
        columns = []
        for i in range(GROUP):
            bre = back[i * ROWS_W : (i + 1) * ROWS_W, :LANES]
            bim = back[i * ROWS_W : (i + 1) * ROWS_W, LANES:]
            undone = jnp.concatenate([bre * cos - bim * sin, bim * cos + bre * sin], 0)
            hi, lo = split(undone)
            columns.append(jnp.concatenate([hi, hi, lo], 0))
        result = mm(inv_ref[...], jnp.concatenate(columns, 1))
        for i in range(GROUP):
            at = pl.ds((step * GROUP + i) * TILES, TILES)
            conv = result[:, i * LANES : (i + 1) * LANES].astype(BF16).astype(F32)
            y_ref[at, :] = gate_ref[at, :].astype(F32) * conv

    for q in range(TILES):
        out_ref[q // 8, :, (q % 8) * LANES : (q % 8 + 1) * LANES] = y_ref[
            pl.ds(q, channels, stride=TILES), :
        ].astype(BF16)


def convolve(proj, ids, factor, taps, spec, interpret=False):
    outer3, twist, fwd, bwd, inv3 = tables()
    return pl.pallas_call(
        convolve_kernel,
        out_shape=jax.ShapeDtypeStruct((8, 32, 1024), BF16),
        scratch_shapes=[
            pltpu.VMEM((192, 2048), BF16),
            pltpu.VMEM((96 * TILES, LANES), F32),
            pltpu.VMEM((32 * TILES, LANES), BF16),
            pltpu.VMEM((32 * TILES, LANES), BF16),
            pltpu.VMEM((32 * TILES, LANES), F32),
        ],
        compiler_params=pltpu.CompilerParams(vmem_limit_bytes=BIG),
        interpret=interpret,
        name="convolve",
    )(proj, ids, factor, taps, spec, outer3, twist, fwd, bwd, inv3)


def here():
    return lax.axis_index("seq"), lax.axis_index("chan"), lax.axis_index("rep")


def greet(peers):
    barrier = pltpu.get_barrier_semaphore()
    for peer in peers:
        pl.semaphore_signal(barrier, inc=1, device_id=peer, device_id_type=MESH)
    pl.semaphore_wait(barrier, len(peers))


def push(src, dst, sems, index, peer):
    copy = pltpu.make_async_remote_copy(
        src_ref=src,
        dst_ref=dst,
        send_sem=sems[0].at[index],
        recv_sem=sems[1].at[index],
        device_id=peer,
        device_id_type=MESH,
    )
    copy.start()
    return copy


def front_kernel(
    fine_ref,
    coarse_ref,
    order_ref,
    gain_ref,
    emb_fine_ref,
    emb_coarse_ref,
    filter_ref,
    outer_ref,
    twist_ref,
    fwd_ref,
    w_ref,
    proj_out,
    factor_out,
    ids_out,
    spec_ref,
    codes_ref,
    rows_ref,
    gains_ref,
    sums_ref,
    x_ref,
    wv_ref,
    proj_ref,
    wide_ref,
    send,
    recv,
    own,
):
    z, c, r = here()
    sems = (send, recv)
    plane = [(z, lax.rem(c + j, 16), r) for j in range(1, 16)]
    line = [(lax.rem(z + j, 8), c, r) for j in range(1, 8)]
    sibling = (z, c, 1 - r)
    slot = r * 8 + z
    weights = [pltpu.make_async_copy(w_ref.at[k], wv_ref.at[k], own.at[k]) for k in range(3)]
    for copy in weights:
        copy.start()
    at = pl.ds(pl.multiple_of(z * 128, 128), 128)

    @pl.when(r == 0)
    def _():
        rows_ref[c] = emb_fine_ref[at, :]

    @pl.when(r != 0)
    def _():
        rows_ref[c] = emb_coarse_ref[at, :]

    gains_ref[c] = jnp.broadcast_to(gain_ref[...].reshape(1, FRAME).astype(F32), (8, FRAME))
    greet(plane + line + [sibling])
    sent = []
    index = [0]

    def tell(src, dst, peer):
        copy = push(src, dst, sems, index[0], peer)
        index[0] += 1
        sent.append(copy)
        return copy

    gains = [tell(gains_ref.at[c], gains_ref.at[c], peer) for peer in plane]
    rows = [tell(rows_ref.at[c], rows_ref.at[c], peer) for peer in plane]
    for i in range(4):
        codes_ref[i : i + 1, :] = fine_ref[i * FRAME : (i + 1) * FRAME].reshape(1, FRAME)
        codes_ref[4 + i : 5 + i, : FRAME // 2] = coarse_ref[
            i * FRAME // 2 : (i + 1) * FRAME // 2
        ].reshape(1, FRAME // 2)
    local_sums(
        codes_ref,
        order_ref[...].reshape(1, FRAME),
        emb_fine_ref,
        emb_coarse_ref,
        ids_out.at[z],
        sums_ref.at[c],
    )
    sums = [tell(sums_ref.at[c], sums_ref.at[c], peer) for peer in plane]
    ids = [tell(ids_out.at[z], ids_out.at[z], peer) for peer in line]

    def prepare(origin):
        hi, lo = split(rows_ref[origin].astype(F32) * gains_ref[origin, 0:1, :])
        columns = pl.ds(pl.multiple_of(origin * 256, 256), 256)
        x_ref[0:128, columns] = hi
        x_ref[128:256, columns] = lo

    prepare(c)
    for j in range(1, 16):
        gains[j - 1].wait_recv()
        rows[j - 1].wait_recv()
        prepare(lax.rem(c + 16 - j, 16))
    dealt = [[] for _ in range(7)]
    for k in range(3):
        weights[k].wait()
        both = mm(x_ref[...], wv_ref[k])
        hi, lo = split(jnp.transpose(both[:128] + both[128:]))
        proj_ref[k, :, :128] = hi
        proj_ref[k, :, 128:] = lo
        for j, peer in enumerate(line):
            src = proj_ref.at[k, pl.ds(pl.multiple_of(peer[0] * 32, 32), 32), :]
            dealt[j].append(tell(src, proj_out.at[slot, k], peer))
    for copy in sums:
        copy.wait_recv()
    total = sums_ref[0]
    for other in range(1, 16):
        total = total + sums_ref[other]
    factor_out[z] = lax.rsqrt(total / (16 * 256.0) + EPSILON)
    factors = [tell(factor_out.at[z], factor_out.at[z], peer) for peer in line]
    proj_out[slot] = proj_ref[:, pl.ds(pl.multiple_of(z * 32, 32), 32), :]
    across = [tell(proj_out.at[slot], proj_out.at[slot], sibling)]
    spectrum_kernel(filter_ref, outer_ref, twist_ref, fwd_ref, spec_ref, wide_ref)
    for j in range(7):
        for copy in dealt[j]:
            copy.wait_recv()
        landed = proj_out.at[r * 8 + lax.rem(z + 7 - j, 8)]
        across.append(tell(landed, landed, sibling))
    for copy in ids + factors + across:
        copy.wait_recv()
    for copy in sent:
        copy.wait_send()


def front(fine, coarse, order, gain, emb_fine, emb_coarse, long_filter, w):
    outer3, twist, fwd, _, _ = tables()
    channels = long_filter.shape[0]
    vmem = pl.BlockSpec(memory_space=pltpu.VMEM)
    copies = 45 + 7 + 21 + 7 + 8
    return pl.pallas_call(
        front_kernel,
        in_specs=[vmem] * 10 + [ANY],
        out_specs=[vmem] * 4,
        out_shape=(
            jax.ShapeDtypeStruct((16, 3, 32, 256), BF16),
            jax.ShapeDtypeStruct((8, 8, LANES), F32),
            jax.ShapeDtypeStruct((8, 8, FRAME), jnp.int32),
            jax.ShapeDtypeStruct((channels * ROWS_W, 256), F32),
        ),
        scratch_shapes=[
            pltpu.VMEM((8, FRAME), jnp.int32),
            pltpu.VMEM((16, 128, 256), BF16),
            pltpu.VMEM((16, 8, FRAME), F32),
            pltpu.VMEM((16, 8, LANES), F32),
            pltpu.VMEM((256, 4096), BF16),
            pltpu.VMEM((3, 4096, 256), BF16),
            pltpu.VMEM((3, 256, 256), BF16),
            pltpu.VMEM((channels * TILES, LANES), F32),
            pltpu.SemaphoreType.DMA((copies,)),
            pltpu.SemaphoreType.DMA((copies,)),
            pltpu.SemaphoreType.DMA((3,)),
        ],
        compiler_params=pltpu.CompilerParams(
            collective_id=0, has_side_effects=True, vmem_limit_bytes=BIG
        ),
        name="front",
    )(fine, coarse, order, gain, emb_fine, emb_coarse, long_filter, outer3, twist, fwd, w)


CHUNKS = 2


def tail_kernel(
    y_ref,
    w_ref,
    hyena_ref,
    attn_ref,
    wv_ref,
    x_ref,
    land_ref,
    acc_ref,
    state_ref,
    parts_ref,
    prefix_ref,
    incoming_ref,
    send,
    recv,
    own,
):
    z, c, r = here()
    y, x = c // 4, lax.rem(c, 4)
    sems = (send, recv)
    length = x_ref.shape[1]
    span = length // CHUNKS

    def chan(at_x, at_y):
        return lax.rem(at_y + 8, 4) * 4 + lax.rem(at_x + 8, 4)

    def device(at_x, at_y):
        return (z, chan(at_x, at_y), r)

    line = [(lax.rem(z + j, 8), c, r) for j in range(1, 8)]
    weights = pltpu.make_async_copy(w_ref, wv_ref, own.at[0])
    weights.start()
    greet(line + [device(x + 1, y), device(x - 1, y), device(x, y + 1), device(x, y - 1)])
    index = [0]
    sent = []

    def tell(src, dst, peer):
        copy = push(src, dst, sems, index[0], peer)
        index[0] += 1
        sent.append(copy)
        return copy

    mine_rows = pl.ds(pl.multiple_of(z * 32, 32), 32)
    turned = []
    kept = []
    for t in range(CHUNKS):
        at = pl.ds(t * span, span)
        kept.append(
            pltpu.make_async_copy(y_ref.at[z, :, at], x_ref.at[mine_rows, at], own.at[1 + t])
        )
        kept[-1].start()
        turned.append([tell(y_ref.at[p[0], :, at], x_ref.at[mine_rows, at], p) for p in line])
    half = x_ref.shape[0] // 2
    quarter = half // 2

    def send_block(t, lead, along, across, part, direction, phase):
        axes = (0, 1) if lead == 0 else (1, 0)
        offset = [0, 0]
        offset[axes[0]], offset[axes[1]] = along, across
        step = [0, 0]
        step[axes[phase]] = direction
        target = device(x + step[0], y + step[1])
        start = lead * half + (0 if part is None else part * quarter)
        rows = pl.ds(start, half if part is None else quarter)
        at = pl.ds(t * span, span)
        dst = land_ref.at[chan(x - offset[0], y - offset[1]), rows, at]
        src = x_ref.at[rows, at] if along == 0 and across == 0 else dst
        number = index[0]
        tell(src, dst, target)
        came = [offset[0] + step[0], offset[1] + step[1]]
        landed = land_ref.at[chan(x - came[0], y - came[1]), rows, at]
        return pltpu.make_async_remote_copy(
            src_ref=landed,
            dst_ref=landed,
            send_sem=send.at[number],
            recv_sem=recv.at[number],
            device_id=target,
            device_id_type=MESH,
        )

    first = {}
    second = {}
    forward = {}
    pending = []

    def multiply(t, lead, along, across):
        at = slice(t * span, (t + 1) * span)
        rows = slice(lead * half, (lead + 1) * half)
        offset = (along, across) if lead == 0 else (across, along)
        origin = chan(x - offset[0], y - offset[1])
        block = x_ref[rows, at] if offset == (0, 0) else land_ref[origin, rows, at]
        depth = pl.ds(pl.multiple_of(origin * 2 * half + lead * half, half), half)
        for k in range(3):
            product = lax.dot_general(
                wv_ref[k, depth, :], block, (((0,), (0,)), ((), ())), preferred_element_type=F32
            )
            if (along, across, lead) == (0, 0, 0):
                acc_ref[k, :, at] = product
            else:
                acc_ref[k, :, at] += product

    def drain(count):
        for _ in range(min(count, len(pending))):
            multiply(*pending.pop(0))

    def open_chunk(t):
        kept[t].wait()
        for copy in turned[t]:
            copy.wait_recv()
        for lead in range(2):
            for d in (1, -1):
                first[t, lead, d] = send_block(t, lead, 0, 0, None, d, 0)
        for lead in range(2):
            for d in (1, -1):
                second[t, lead, 0, d] = send_block(t, lead, 0, 0, None, d, 1)
        for lead in range(2):
            pending.append((t, lead, 0, 0))

    last = []

    def onward(t, lead, along):
        for e in (1, -1):
            second[t, lead, along, e].wait_recv()
            last.append((t, lead, along, send_block(t, lead, along, e, 0 if e == 1 else 1, e, 1)))
        for e in (1, -1):
            pending.append((t, lead, along, e))

    for t in range(CHUNKS):
        open_chunk(t)
    weights.wait()
    back = pltpu.make_async_copy(x_ref, hyena_ref, own.at[CHUNKS + 1])
    back.start()
    for t in range(CHUNKS):
        for d in (1, -1):
            for lead in range(2):
                first[t, lead, d].wait_recv()
                forward[t, lead, d] = send_block(t, lead, d, 0, 0 if d == 1 else 1, d, 0)
                for e in (1, -1):
                    second[t, lead, d, e] = send_block(t, lead, d, 0, None, e, 1)
                pending.append((t, lead, d, 0))
        drain(2)
        for lead in range(2):
            onward(t, lead, 0)
            drain(1)
        for lead in range(2):
            forward[t, lead, 1].wait_recv()
            forward[t, lead, -1].wait_recv()
            for e in (1, -1):
                second[t, lead, 2, e] = send_block(t, lead, 2, 0, None, e, 1)
            pending.append((t, lead, 2, 0))
            drain(1)
    for t in range(CHUNKS):
        for along in (1, -1, 2):
            for lead in range(2):
                onward(t, lead, along)
                drain(3)
    for t, lead, along, arrival in last:
        arrival.wait_recv()
    for position in range(0, len(last), 2):
        t, lead, along, _ = last[position]
        pending.append((t, lead, along, 2))
    drain(len(pending))

    blocks = length // BLOCK
    heads = [[acc_ref[k, :, b * BLOCK : (b + 1) * BLOCK].astype(BF16) for b in range(blocks)] for k in range(3)]
    states = [
        lax.dot_general(
            heads[1][b], heads[2][b], (((1,), (1,)), ((), ())), preferred_element_type=F32
        )
        for b in range(blocks)
    ]
    total = states[0]
    for b in range(1, blocks):
        total = total + states[b]
    state_ref[...] = total.reshape(8, HD // 8, HD)
    parts_ref[z] = state_ref[z]
    gathered = [tell(state_ref.at[p[0]], parts_ref.at[z], p) for p in line]
    row = lax.broadcasted_iota(jnp.int32, (BLOCK, BLOCK), 0)
    column = lax.broadcasted_iota(jnp.int32, (BLOCK, BLOCK), 1)
    queries = []
    inside = []

    def local(b):
        queries.append(jnp.transpose(heads[0][b].astype(F32)).astype(BF16))
        scores = mm(queries[b], heads[1][b])
        scores = jnp.where(row >= column, scores, 0.0).astype(BF16)
        inside.append(
            lax.dot_general(
                scores, heads[2][b], (((1,), (1,)), ((), ())), preferred_element_type=F32
            )
        )

    local(0)
    for copy in gathered:
        copy.wait_recv()
    running = jnp.zeros((HD // 8, HD), F32)
    for step in range(8):
        prefix_ref[step] = running
        running = running + parts_ref[step]
    incoming_ref[z] = prefix_ref[z]
    dealt = [tell(prefix_ref.at[p[0]], incoming_ref.at[z], p) for p in line]
    for b in range(1, blocks):
        local(b)
    for copy in dealt:
        copy.wait_recv()
    earlier = incoming_ref[...].reshape(HD, HD)
    place = lax.broadcasted_iota(jnp.int32, (BLOCK, HD), 0)
    for b in range(blocks):
        carried = mm(queries[b], earlier.astype(BF16))
        position = z * length + b * BLOCK + place + 1
        divisor = jnp.sqrt((position * HD).astype(F32))
        attn_ref[b * BLOCK : (b + 1) * BLOCK, :] = ((inside[b] + carried) / divisor).astype(BF16)
        earlier = earlier + states[b]
    for copy in sent:
        copy.wait_send()
    back.wait()


def tail(y, w):
    seqs, channels, length = y.shape
    depth = seqs * channels
    vmem = pl.BlockSpec(memory_space=pltpu.VMEM)
    copies = CHUNKS * (7 + 40) + 14
    return pl.pallas_call(
        tail_kernel,
        in_specs=[ANY, ANY],
        out_specs=[ANY, vmem],
        out_shape=(
            jax.ShapeDtypeStruct((depth, length), BF16),
            jax.ShapeDtypeStruct((length, HD), BF16),
        ),
        scratch_shapes=[
            pltpu.VMEM(w.shape, BF16),
            pltpu.VMEM((depth, length), BF16),
            pltpu.VMEM((16, depth, length), BF16),
            pltpu.VMEM((3, HD, length), F32),
            pltpu.VMEM((8, HD // 8, HD), F32),
            pltpu.VMEM((8, HD // 8, HD), F32),
            pltpu.VMEM((8, HD // 8, HD), F32),
            pltpu.VMEM((8, HD // 8, HD), F32),
            pltpu.SemaphoreType.DMA((copies,)),
            pltpu.SemaphoreType.DMA((copies,)),
            pltpu.SemaphoreType.DMA((CHUNKS + 2,)),
        ],
        compiler_params=pltpu.CompilerParams(
            collective_id=2, has_side_effects=True, vmem_limit_bytes=BIG
        ),
        name="tail",
    )(y, w)


def shards(
    fine_codes,
    coarse_codes,
    frame_order,
    emb_fine,
    emb_coarse,
    norm_gain,
    w_hyena,
    short_taps,
    long_filter,
    w_attn,
):
    proj_all, factor_all, ids_all, spec = front(
        fine_codes,
        coarse_codes,
        frame_order,
        norm_gain,
        emb_fine,
        emb_coarse,
        long_filter,
        jnp.transpose(w_hyena, (1, 0, 2)),
    )
    y = convolve(
        proj_all.reshape(16, 96, 256), ids_all, factor_all.reshape(TILES, LANES), short_taps, spec
    )
    return tail(y, jnp.transpose(w_attn, (1, 0, 2)))


def solution(mesh):
    return jax.shard_map(
        shards,
        mesh=mesh,
        in_specs=(
            P(("rep", "seq")),
            P(("rep", "seq")),
            P(),
            P(None, "chan"),
            P(None, "chan"),
            P("chan"),
            P(None, None, "chan"),
            P(None, "chan", None),
            P(("chan", "seq"), None),
            P(None, None, "chan"),
        ),
        out_specs=(P("chan", ("rep", "seq")), P(("rep", "seq"), "chan")),
        check_vma=False,
    )
```

```python
import functools
import math

import jax
import jax.numpy as jnp
import numpy as np
from jax import lax
from jax.experimental import pallas as pl
from jax.experimental.pallas import tpu as pltpu
from jax.sharding import PartitionSpec as P

HD = 128
FRAME = 256
BLOCK = 512
LANES = 128
EPSILON = 1e-05
F32 = jnp.float32
BF16 = jnp.bfloat16
ANY = pl.BlockSpec(memory_space=pl.ANY)
MESH = pl.DeviceIdType.MESH
BIG = 56 << 20

ROWS_W = 72
TILES = 64
POINTS = 2 * TILES * LANES


def split_np(x):
    hi = np.asarray(x, np.float32).astype(jnp.bfloat16)
    lo = (np.asarray(x, np.float64) - hi.astype(np.float64)).astype(np.float32).astype(jnp.bfloat16)
    return hi, lo


@functools.lru_cache(None)
def tables():
    w = np.arange(ROWS_W)[:, None]
    kept = (w <= 64).astype(np.float64)
    q = np.arange(TILES)[None, :]
    angle = 2 * np.pi * ((w * q) % 128) / 128
    outer = np.concatenate([np.cos(angle) * kept, -np.sin(angle) * kept], 0)
    a = np.arange(LANES)[None, :]
    turn = 2 * np.pi * (w * a) / POINTS
    twist = np.stack([np.cos(turn) * kept, np.sin(turn) * kept]).astype(np.float32)
    m = np.arange(LANES)
    inner = 2 * np.pi * ((m[:, None] * m[None, :]) % 128) / 128
    c, s = np.cos(inner), np.sin(inner)
    forward = np.block([[c, -s], [s, c]])
    backward = np.block([[c, s], [-s, c]])
    weight = np.where((w == 0) | (w == 64), 1.0, 2.0) * kept / POINTS
    inverse = np.concatenate([(np.cos(angle) * weight).T, (-np.sin(angle) * weight).T], 1)
    outer_hi, outer_lo = split_np(outer)
    inv_hi, inv_lo = split_np(inverse)
    fwd = np.stack(split_np(forward))
    bwd = np.stack(split_np(backward))
    outer3 = np.concatenate([outer_hi, outer_lo, outer_hi], 1)
    inv3 = np.concatenate([inv_hi, inv_lo, inv_hi], 1)
    return outer3, twist, fwd, bwd, inv3


def split(x):
    hi = x.astype(BF16)
    return hi, (x - hi.astype(F32)).astype(BF16)


def mm(a, b):
    return jnp.dot(a, b, preferred_element_type=F32)


def mm3(x, table):
    hi, lo = split(x)
    return mm(hi, table[0]) + (mm(lo, table[0]) + mm(hi, table[1]))


def local_sums(codes_ref, order, emb_fine_ref, emb_coarse_ref, ids_ref, sums_ref):
    row = lax.broadcasted_iota(jnp.int32, (FRAME, FRAME), 0)
    pick = (row == order).astype(BF16)
    pick_half = (row[: FRAME // 2] == order // 2).astype(BF16)

    def looked(codes, pick):
        hi = (codes // 32).astype(F32).astype(BF16)
        lo = (codes % 32).astype(F32).astype(BF16)
        return (mm(hi, pick) * 32.0 + mm(lo, pick)).astype(jnp.int32)

    fine = looked(codes_ref[0:4, :], pick)
    coarse = looked(codes_ref[4:8, : FRAME // 2], pick_half)
    ids_ref[0:4, :] = fine
    ids_ref[4:8, :] = coarse
    vocab = lax.broadcasted_iota(jnp.int32, (emb_fine_ref.shape[0], FRAME), 0)
    dims = (((0,), (0,)), ((), ()))
    for frame in range(4):
        hot_fine = (vocab == fine[frame : frame + 1]).astype(BF16)
        hot_coarse = (vocab == coarse[frame : frame + 1]).astype(BF16)
        rows = lax.dot_general(emb_fine_ref[...], hot_fine, dims, preferred_element_type=F32)
        rows = rows + lax.dot_general(
            emb_coarse_ref[...], hot_coarse, dims, preferred_element_type=F32
        )
        rows = rows.astype(BF16).astype(F32)
        total = jnp.sum(rows * rows, axis=0, keepdims=True)
        sums_ref[2 * frame : 2 * frame + 1, :] = total[:, :LANES]
        sums_ref[2 * frame + 1 : 2 * frame + 2, :] = total[:, LANES:]


GROUP = 16


def twisted(step, twist_ref):
    cos, sin = twist_ref[0], twist_ref[1]
    rows = []
    for i in range(GROUP):
        re = step[:ROWS_W, i * LANES : (i + 1) * LANES]
        im = step[ROWS_W:, i * LANES : (i + 1) * LANES]
        rows.append(jnp.concatenate([re * cos + im * sin, im * cos - re * sin], 1))
    return jnp.concatenate(rows, 0)


def spectrum_kernel(h_ref, outer_ref, twist_ref, fwd_ref, out_ref, wide_ref):
    channels = h_ref.shape[0]
    for q in range(TILES):
        wide_ref[pl.ds(q, channels, stride=TILES), :] = h_ref[:, q * LANES : (q + 1) * LANES]

    @pl.loop(0, channels // GROUP)
    def _(step):
        pieces = []
        for i in range(GROUP):
            hi, lo = split(wide_ref[pl.ds((step * GROUP + i) * TILES, TILES), :])
            pieces.append(jnp.concatenate([hi, hi, lo], 0))
        first = mm(outer_ref[...], jnp.concatenate(pieces, 1))
        out_ref[pl.ds(step * GROUP * ROWS_W, GROUP * ROWS_W), :] = mm3(
            twisted(first, twist_ref), fwd_ref
        )


def convolve_kernel(
    proj_ref,
    ids_ref,
    factor_ref,
    taps_ref,
    spec_ref,
    outer_ref,
    twist_ref,
    fwd_ref,
    bwd_ref,
    inv_ref,
    out_ref,
    left_ref,
    wide_ref,
    gate_ref,
    mix_ref,
    y_ref,
):
    channels = 32
    for s in range(16):
        left_ref[0:96, s * 128 : (s + 1) * 128] = proj_ref[s, :, :128]
        left_ref[96:192, s * 128 : (s + 1) * 128] = proj_ref[s, :, 128:]
    vocab = lax.broadcasted_iota(jnp.int32, (1024, FRAME), 0)

    @pl.loop(0, 8)
    def _(z):
        ids = ids_ref[z]
        for i in range(4):
            hot = jnp.concatenate(
                [
                    (vocab == ids[i : i + 1]).astype(BF16),
                    (vocab == ids[4 + i : 5 + i]).astype(BF16),
                ],
                0,
            )
            both = mm(left_ref[...], hot)
            value = both[:96] + both[96:]
            for half in range(2):
                wide_ref[pl.ds(z * 8 + 2 * i + half, 96, stride=TILES), :] = value[
                    :, half * LANES : (half + 1) * LANES
                ]

    tap_row = lax.broadcasted_iota(jnp.int32, (LANES, LANES), 0)
    tap_col = lax.broadcasted_iota(jnp.int32, (LANES, LANES), 1)
    group_row = lax.broadcasted_iota(jnp.int32, taps_ref.shape[1:], 0)
    rows = 16 * TILES
    first_tile = lax.broadcasted_iota(jnp.int32, (rows, LANES), 0) % TILES == 0
    scale = jnp.concatenate([factor_ref[...]] * 16, 0)

    def filtered(k, g):
        wanted = 2 * lax.axis_index("seq") + g
        own = jnp.where(group_row == wanted, taps_ref[k].astype(F32), 0.0)
        taps = jnp.broadcast_to(jnp.sum(own, axis=0, keepdims=True), (LANES, LANES))
        turned = pltpu.roll(taps, 0, 1, stride=1, stride_axis=0)
        both = jnp.concatenate(
            [
                jnp.where(tap_col >= tap_row, turned, 0.0),
                jnp.where(tap_col < tap_row, turned, 0.0),
            ],
            1,
        ).astype(BF16)
        start = (2 * k + g) * rows
        x = (wide_ref[start : start + rows, :] * scale).astype(BF16)
        parts = mm(x, both)
        carried = jnp.where(first_tile, 0.0, pltpu.roll(parts[:, LANES:], 1, 0))
        return (parts[:, :LANES] + carried).astype(BF16)

    for g in range(2):
        gate_ref[g * rows : (g + 1) * rows, :] = filtered(0, g)
        left = filtered(1, g).astype(F32)
        mix_ref[g * rows : (g + 1) * rows, :] = (left * filtered(2, g).astype(F32)).astype(BF16)

    @pl.loop(0, channels // GROUP)
    def _(step):
        pieces = []
        for i in range(GROUP):
            x = mix_ref[pl.ds((step * GROUP + i) * TILES, TILES), :]
            pieces.append(jnp.concatenate([x, x], 0))
        first = mm(outer_ref[:, : 2 * TILES], jnp.concatenate(pieces, 1))
        spec = mm3(twisted(first, twist_ref), fwd_ref)
        other = spec_ref[pl.ds(step * GROUP * ROWS_W, GROUP * ROWS_W), :]
        re, im = spec[:, :LANES], spec[:, LANES:]
        ore, oim = other[:, :LANES], other[:, LANES:]
        back = mm3(jnp.concatenate([re * ore - im * oim, re * oim + im * ore], 1), bwd_ref)
        cos, sin = twist_ref[0], twist_ref[1]
        columns = []
        for i in range(GROUP):
            bre = back[i * ROWS_W : (i + 1) * ROWS_W, :LANES]
            bim = back[i * ROWS_W : (i + 1) * ROWS_W, LANES:]
            undone = jnp.concatenate([bre * cos - bim * sin, bim * cos + bre * sin], 0)
            hi, lo = split(undone)
            columns.append(jnp.concatenate([hi, hi, lo], 0))
        result = mm(inv_ref[...], jnp.concatenate(columns, 1))
        for i in range(GROUP):
            at = pl.ds((step * GROUP + i) * TILES, TILES)
            conv = result[:, i * LANES : (i + 1) * LANES].astype(BF16).astype(F32)
            y_ref[at, :] = gate_ref[at, :].astype(F32) * conv

    for q in range(TILES):
        out_ref[q // 8, :, (q % 8) * LANES : (q % 8 + 1) * LANES] = y_ref[
            pl.ds(q, channels, stride=TILES), :
        ].astype(BF16)


def convolve(proj, ids, factor, taps, spec, interpret=False):
    outer3, twist, fwd, bwd, inv3 = tables()
    return pl.pallas_call(
        convolve_kernel,
        out_shape=jax.ShapeDtypeStruct((8, 32, 1024), BF16),
        scratch_shapes=[
            pltpu.VMEM((192, 2048), BF16),
            pltpu.VMEM((96 * TILES, LANES), F32),
            pltpu.VMEM((32 * TILES, LANES), BF16),
            pltpu.VMEM((32 * TILES, LANES), BF16),
            pltpu.VMEM((32 * TILES, LANES), F32),
        ],
        compiler_params=pltpu.CompilerParams(vmem_limit_bytes=BIG),
        interpret=interpret,
        name="convolve",
    )(proj, ids, factor, taps, spec, outer3, twist, fwd, bwd, inv3)


def here():
    return lax.axis_index("seq"), lax.axis_index("chan"), lax.axis_index("rep")


def greet(peers):
    barrier = pltpu.get_barrier_semaphore()
    for peer in peers:
        pl.semaphore_signal(barrier, inc=1, device_id=peer, device_id_type=MESH)
    pl.semaphore_wait(barrier, len(peers))


def push(src, dst, sems, index, peer):
    copy = pltpu.make_async_remote_copy(
        src_ref=src,
        dst_ref=dst,
        send_sem=sems[0].at[index],
        recv_sem=sems[1].at[index],
        device_id=peer,
        device_id_type=MESH,
    )
    copy.start()
    return copy


def front_kernel(
    fine_ref,
    coarse_ref,
    order_ref,
    gain_ref,
    emb_fine_ref,
    emb_coarse_ref,
    filter_ref,
    outer_ref,
    twist_ref,
    fwd_ref,
    w_ref,
    proj_out,
    factor_out,
    ids_out,
    spec_ref,
    codes_ref,
    rows_ref,
    gains_ref,
    sums_ref,
    x_ref,
    wv_ref,
    proj_ref,
    wide_ref,
    send,
    recv,
    own,
):
    z, c, r = here()
    sems = (send, recv)
    plane = [(z, lax.rem(c + j, 16), r) for j in range(1, 16)]
    line = [(lax.rem(z + j, 8), c, r) for j in range(1, 8)]
    sibling = (z, c, 1 - r)
    slot = r * 8 + z
    weights = [pltpu.make_async_copy(w_ref.at[k], wv_ref.at[k], own.at[k]) for k in range(3)]
    for copy in weights:
        copy.start()
    at = pl.ds(pl.multiple_of(z * 128, 128), 128)

    @pl.when(r == 0)
    def _():
        rows_ref[c] = emb_fine_ref[at, :]

    @pl.when(r != 0)
    def _():
        rows_ref[c] = emb_coarse_ref[at, :]

    gains_ref[c] = jnp.broadcast_to(gain_ref[...].reshape(1, FRAME).astype(F32), (8, FRAME))
    greet(plane + line + [sibling])
    sent = []
    index = [0]

    def tell(src, dst, peer):
        copy = push(src, dst, sems, index[0], peer)
        index[0] += 1
        sent.append(copy)
        return copy

    gains = [tell(gains_ref.at[c], gains_ref.at[c], peer) for peer in plane]
    rows = [tell(rows_ref.at[c], rows_ref.at[c], peer) for peer in plane]
    for i in range(4):
        codes_ref[i : i + 1, :] = fine_ref[i * FRAME : (i + 1) * FRAME].reshape(1, FRAME)
        codes_ref[4 + i : 5 + i, : FRAME // 2] = coarse_ref[
            i * FRAME // 2 : (i + 1) * FRAME // 2
        ].reshape(1, FRAME // 2)
    local_sums(
        codes_ref,
        order_ref[...].reshape(1, FRAME),
        emb_fine_ref,
        emb_coarse_ref,
        ids_out.at[z],
        sums_ref.at[c],
    )
    sums = [tell(sums_ref.at[c], sums_ref.at[c], peer) for peer in plane]
    ids = [tell(ids_out.at[z], ids_out.at[z], peer) for peer in line]

    def prepare(origin):
        hi, lo = split(rows_ref[origin].astype(F32) * gains_ref[origin, 0:1, :])
        columns = pl.ds(pl.multiple_of(origin * 256, 256), 256)
        x_ref[0:128, columns] = hi
        x_ref[128:256, columns] = lo

    prepare(c)
    for j in range(1, 16):
        gains[j - 1].wait_recv()
        rows[j - 1].wait_recv()
        prepare(lax.rem(c + 16 - j, 16))
    dealt = [[] for _ in range(7)]
    for k in range(3):
        weights[k].wait()
        both = mm(x_ref[...], wv_ref[k])
        hi, lo = split(jnp.transpose(both[:128] + both[128:]))
        proj_ref[k, :, :128] = hi
        proj_ref[k, :, 128:] = lo
        for j, peer in enumerate(line):
            src = proj_ref.at[k, pl.ds(pl.multiple_of(peer[0] * 32, 32), 32), :]
            dealt[j].append(tell(src, proj_out.at[slot, k], peer))
    for copy in sums:
        copy.wait_recv()
    total = sums_ref[0]
    for other in range(1, 16):
        total = total + sums_ref[other]
    factor_out[z] = lax.rsqrt(total / (16 * 256.0) + EPSILON)
    factors = [tell(factor_out.at[z], factor_out.at[z], peer) for peer in line]
    proj_out[slot] = proj_ref[:, pl.ds(pl.multiple_of(z * 32, 32), 32), :]
    across = [tell(proj_out.at[slot], proj_out.at[slot], sibling)]
    spectrum_kernel(filter_ref, outer_ref, twist_ref, fwd_ref, spec_ref, wide_ref)
    for j in range(7):
        for copy in dealt[j]:
            copy.wait_recv()
        landed = proj_out.at[r * 8 + lax.rem(z + 7 - j, 8)]
        across.append(tell(landed, landed, sibling))
    for copy in ids + factors + across:
        copy.wait_recv()
    for copy in sent:
        copy.wait_send()


def front(fine, coarse, order, gain, emb_fine, emb_coarse, long_filter, w):
    outer3, twist, fwd, _, _ = tables()
    channels = long_filter.shape[0]
    vmem = pl.BlockSpec(memory_space=pltpu.VMEM)
    copies = 45 + 7 + 21 + 7 + 8
    return pl.pallas_call(
        front_kernel,
        in_specs=[vmem] * 10 + [ANY],
        out_specs=[vmem] * 4,
        out_shape=(
            jax.ShapeDtypeStruct((16, 3, 32, 256), BF16),
            jax.ShapeDtypeStruct((8, 8, LANES), F32),
            jax.ShapeDtypeStruct((8, 8, FRAME), jnp.int32),
            jax.ShapeDtypeStruct((channels * ROWS_W, 256), F32),
        ),
        scratch_shapes=[
            pltpu.VMEM((8, FRAME), jnp.int32),
            pltpu.VMEM((16, 128, 256), BF16),
            pltpu.VMEM((16, 8, FRAME), F32),
            pltpu.VMEM((16, 8, LANES), F32),
            pltpu.VMEM((256, 4096), BF16),
            pltpu.VMEM((3, 4096, 256), BF16),
            pltpu.VMEM((3, 256, 256), BF16),
            pltpu.VMEM((channels * TILES, LANES), F32),
            pltpu.SemaphoreType.DMA((copies,)),
            pltpu.SemaphoreType.DMA((copies,)),
            pltpu.SemaphoreType.DMA((3,)),
        ],
        compiler_params=pltpu.CompilerParams(
            collective_id=0, has_side_effects=True, vmem_limit_bytes=BIG
        ),
        name="front",
    )(fine, coarse, order, gain, emb_fine, emb_coarse, long_filter, outer3, twist, fwd, w)


CHUNKS = 2


def tail_kernel(
    y_ref,
    w_ref,
    hyena_ref,
    attn_ref,
    wv_ref,
    x_ref,
    land_ref,
    acc_ref,
    state_ref,
    parts_ref,
    prefix_ref,
    incoming_ref,
    send,
    recv,
    own,
):
    z, c, r = here()
    y, x = c // 4, lax.rem(c, 4)
    sems = (send, recv)
    length = x_ref.shape[1]
    span = length // CHUNKS

    def chan(at_x, at_y):
        return lax.rem(at_y + 8, 4) * 4 + lax.rem(at_x + 8, 4)

    def device(at_x, at_y):
        return (z, chan(at_x, at_y), r)

    line = [(lax.rem(z + j, 8), c, r) for j in range(1, 8)]
    weights = pltpu.make_async_copy(w_ref, wv_ref, own.at[0])
    weights.start()
    greet(line + [device(x + 1, y), device(x - 1, y), device(x, y + 1), device(x, y - 1)])
    index = [0]
    sent = []

    def tell(src, dst, peer):
        copy = push(src, dst, sems, index[0], peer)
        index[0] += 1
        sent.append(copy)
        return copy

    mine_rows = pl.ds(pl.multiple_of(z * 32, 32), 32)
    turned = []
    kept = []
    for t in range(CHUNKS):
        at = pl.ds(t * span, span)
        kept.append(
            pltpu.make_async_copy(y_ref.at[z, :, at], x_ref.at[mine_rows, at], own.at[1 + t])
        )
        kept[-1].start()
        if t == 0:
            turned.append([tell(y_ref.at[p[0], :, at], x_ref.at[mine_rows, at], p) for p in line])
    half = x_ref.shape[0] // 2
    quarter = half // 2

    def send_block(t, lead, along, across, part, direction, phase):
        axes = (0, 1) if lead == 0 else (1, 0)
        offset = [0, 0]
        offset[axes[0]], offset[axes[1]] = along, across
        step = [0, 0]
        step[axes[phase]] = direction
        target = device(x + step[0], y + step[1])
        start = lead * half + (0 if part is None else part * quarter)
        rows = pl.ds(start, half if part is None else quarter)
        at = pl.ds(t * span, span)
        dst = land_ref.at[chan(x - offset[0], y - offset[1]), rows, at]
        src = x_ref.at[rows, at] if along == 0 and across == 0 else dst
        number = index[0]
        tell(src, dst, target)
        came = [offset[0] + step[0], offset[1] + step[1]]
        landed = land_ref.at[chan(x - came[0], y - came[1]), rows, at]
        return pltpu.make_async_remote_copy(
            src_ref=landed,
            dst_ref=landed,
            send_sem=send.at[number],
            recv_sem=recv.at[number],
            device_id=target,
            device_id_type=MESH,
        )

    first = {}
    second = {}
    forward = {}
    pending = []

    def multiply(t, lead, along, across):
        at = slice(t * span, (t + 1) * span)
        rows = slice(lead * half, (lead + 1) * half)
        offset = (along, across) if lead == 0 else (across, along)
        origin = chan(x - offset[0], y - offset[1])
        block = x_ref[rows, at] if offset == (0, 0) else land_ref[origin, rows, at]
        depth = pl.ds(pl.multiple_of(origin * 2 * half + lead * half, half), half)
        for k in range(3):
            product = lax.dot_general(
                wv_ref[k, depth, :], block, (((0,), (0,)), ((), ())), preferred_element_type=F32
            )
            if (along, across, lead) == (0, 0, 0):
                acc_ref[k, :, at] = product
            else:
                acc_ref[k, :, at] += product

    def drain(count):
        for _ in range(min(count, len(pending))):
            multiply(*pending.pop(0))

    def open_chunk(t):
        kept[t].wait()
        for copy in turned[t]:
            copy.wait_recv()
        if t + 1 < CHUNKS:
            at = pl.ds((t + 1) * span, span)
            turned.append([tell(y_ref.at[p[0], :, at], x_ref.at[mine_rows, at], p) for p in line])
        for lead in range(2):
            for d in (1, -1):
                first[t, lead, d] = send_block(t, lead, 0, 0, None, d, 0)
        for lead in range(2):
            for d in (1, -1):
                second[t, lead, 0, d] = send_block(t, lead, 0, 0, None, d, 1)
        for lead in range(2):
            pending.append((t, lead, 0, 0))

    last = []

    def onward(t, lead, along):
        for e in (1, -1):
            second[t, lead, along, e].wait_recv()
            last.append((t, lead, along, send_block(t, lead, along, e, 0 if e == 1 else 1, e, 1)))
        for e in (1, -1):
            pending.append((t, lead, along, e))

    open_chunk(0)
    weights.wait()
    for t in range(CHUNKS):
        for d in (1, -1):
            for lead in range(2):
                first[t, lead, d].wait_recv()
                forward[t, lead, d] = send_block(t, lead, d, 0, 0 if d == 1 else 1, d, 0)
                for e in (1, -1):
                    second[t, lead, d, e] = send_block(t, lead, d, 0, None, e, 1)
                pending.append((t, lead, d, 0))
        if t + 1 < CHUNKS:
            open_chunk(t + 1)
        else:
            back = pltpu.make_async_copy(x_ref, hyena_ref, own.at[CHUNKS + 1])
            back.start()
        drain(2)
        for lead in range(2):
            onward(t, lead, 0)
            drain(1)
        for lead in range(2):
            forward[t, lead, 1].wait_recv()
            forward[t, lead, -1].wait_recv()
            for e in (1, -1):
                second[t, lead, 2, e] = send_block(t, lead, 2, 0, None, e, 1)
            pending.append((t, lead, 2, 0))
            drain(1)
    for t in range(CHUNKS):
        for along in (1, -1, 2):
            for lead in range(2):
                onward(t, lead, along)
                drain(3)
    for t, lead, along, arrival in last:
        arrival.wait_recv()
    for position in range(0, len(last), 2):
        t, lead, along, _ = last[position]
        pending.append((t, lead, along, 2))
    drain(len(pending))

    blocks = length // BLOCK
    heads = [[acc_ref[k, :, b * BLOCK : (b + 1) * BLOCK].astype(BF16) for b in range(blocks)] for k in range(3)]
    states = [
        lax.dot_general(
            heads[1][b], heads[2][b], (((1,), (1,)), ((), ())), preferred_element_type=F32
        )
        for b in range(blocks)
    ]
    total = states[0]
    for b in range(1, blocks):
        total = total + states[b]
    state_ref[...] = total.reshape(8, HD // 8, HD)
    parts_ref[z] = state_ref[z]
    gathered = [tell(state_ref.at[p[0]], parts_ref.at[z], p) for p in line]
    row = lax.broadcasted_iota(jnp.int32, (BLOCK, BLOCK), 0)
    column = lax.broadcasted_iota(jnp.int32, (BLOCK, BLOCK), 1)
    queries = []
    inside = []

    def local(b):
        queries.append(jnp.transpose(heads[0][b].astype(F32)).astype(BF16))
        scores = mm(queries[b], heads[1][b])
        scores = jnp.where(row >= column, scores, 0.0).astype(BF16)
        inside.append(
            lax.dot_general(
                scores, heads[2][b], (((1,), (1,)), ((), ())), preferred_element_type=F32
            )
        )

    local(0)
    for copy in gathered:
        copy.wait_recv()
    running = jnp.zeros((HD // 8, HD), F32)
    for step in range(8):
        prefix_ref[step] = running
        running = running + parts_ref[step]
    incoming_ref[z] = prefix_ref[z]
    dealt = [tell(prefix_ref.at[p[0]], incoming_ref.at[z], p) for p in line]
    for b in range(1, blocks):
        local(b)
    for copy in dealt:
        copy.wait_recv()
    earlier = incoming_ref[...].reshape(HD, HD)
    place = lax.broadcasted_iota(jnp.int32, (BLOCK, HD), 0)
    for b in range(blocks):
        carried = mm(queries[b], earlier.astype(BF16))
        position = z * length + b * BLOCK + place + 1
        divisor = jnp.sqrt((position * HD).astype(F32))
        attn_ref[b * BLOCK : (b + 1) * BLOCK, :] = ((inside[b] + carried) / divisor).astype(BF16)
        earlier = earlier + states[b]
    for copy in sent:
        copy.wait_send()
    back.wait()


def tail(y, w):
    seqs, channels, length = y.shape
    depth = seqs * channels
    vmem = pl.BlockSpec(memory_space=pltpu.VMEM)
    copies = CHUNKS * (7 + 40) + 14
    return pl.pallas_call(
        tail_kernel,
        in_specs=[ANY, ANY],
        out_specs=[ANY, vmem],
        out_shape=(
            jax.ShapeDtypeStruct((depth, length), BF16),
            jax.ShapeDtypeStruct((length, HD), BF16),
        ),
        scratch_shapes=[
            pltpu.VMEM(w.shape, BF16),
            pltpu.VMEM((depth, length), BF16),
            pltpu.VMEM((16, depth, length), BF16),
            pltpu.VMEM((3, HD, length), F32),
            pltpu.VMEM((8, HD // 8, HD), F32),
            pltpu.VMEM((8, HD // 8, HD), F32),
            pltpu.VMEM((8, HD // 8, HD), F32),
            pltpu.VMEM((8, HD // 8, HD), F32),
            pltpu.SemaphoreType.DMA((copies,)),
            pltpu.SemaphoreType.DMA((copies,)),
            pltpu.SemaphoreType.DMA((CHUNKS + 2,)),
        ],
        compiler_params=pltpu.CompilerParams(
            collective_id=2, has_side_effects=True, vmem_limit_bytes=BIG
        ),
        name="tail",
    )(y, w)


def settle_kernel(hyena_ref, attn_ref, hyena_out, attn_out):
    hyena_out[...] = hyena_ref[...]
    attn_out[...] = attn_ref[...]


def settle(hyena, attn):
    return pl.pallas_call(
        settle_kernel,
        out_shape=(
            jax.ShapeDtypeStruct(hyena.shape, hyena.dtype),
            jax.ShapeDtypeStruct(attn.shape, attn.dtype),
        ),
        name="settle",
    )(hyena, attn)


def shards(
    fine_codes,
    coarse_codes,
    frame_order,
    emb_fine,
    emb_coarse,
    norm_gain,
    w_hyena,
    short_taps,
    long_filter,
    w_attn,
):
    proj_all, factor_all, ids_all, spec = front(
        fine_codes,
        coarse_codes,
        frame_order,
        norm_gain,
        emb_fine,
        emb_coarse,
        long_filter,
        jnp.transpose(w_hyena, (1, 0, 2)),
    )
    y = convolve(
        proj_all.reshape(16, 96, 256), ids_all, factor_all.reshape(TILES, LANES), short_taps, spec
    )
    return settle(*tail(y, jnp.transpose(w_attn, (1, 0, 2))))


def solution(mesh):
    return jax.shard_map(
        shards,
        mesh=mesh,
        in_specs=(
            P(("rep", "seq")),
            P(("rep", "seq")),
            P(),
            P(None, "chan"),
            P(None, "chan"),
            P("chan"),
            P(None, None, "chan"),
            P(None, "chan", None),
            P(("chan", "seq"), None),
            P(None, None, "chan"),
        ),
        out_specs=(P("chan", ("rep", "seq")), P(("rep", "seq"), "chan")),
        check_vma=False,
    )
```

```python
import functools
import math

import jax
import jax.numpy as jnp
import numpy as np
from jax import lax
from jax.experimental import pallas as pl
from jax.experimental.pallas import tpu as pltpu
from jax.sharding import PartitionSpec as P

HD = 128
FRAME = 256
BLOCK = 512
LANES = 128
EPSILON = 1e-05
F32 = jnp.float32
BF16 = jnp.bfloat16
ANY = pl.BlockSpec(memory_space=pl.ANY)
MESH = pl.DeviceIdType.MESH
BIG = 56 << 20

ROWS_W = 72
TILES = 64
POINTS = 2 * TILES * LANES


def split_np(x):
    hi = np.asarray(x, np.float32).astype(jnp.bfloat16)
    lo = (np.asarray(x, np.float64) - hi.astype(np.float64)).astype(np.float32).astype(jnp.bfloat16)
    return hi, lo


@functools.lru_cache(None)
def tables():
    w = np.arange(ROWS_W)[:, None]
    kept = (w <= 64).astype(np.float64)
    q = np.arange(TILES)[None, :]
    angle = 2 * np.pi * ((w * q) % 128) / 128
    outer = np.concatenate([np.cos(angle) * kept, -np.sin(angle) * kept], 0)
    a = np.arange(LANES)[None, :]
    turn = 2 * np.pi * (w * a) / POINTS
    twist = np.stack([np.cos(turn) * kept, np.sin(turn) * kept]).astype(np.float32)
    m = np.arange(LANES)
    inner = 2 * np.pi * ((m[:, None] * m[None, :]) % 128) / 128
    c, s = np.cos(inner), np.sin(inner)
    forward = np.block([[c, -s], [s, c]])
    backward = np.block([[c, s], [-s, c]])
    weight = np.where((w == 0) | (w == 64), 1.0, 2.0) * kept / POINTS
    inverse = np.concatenate([(np.cos(angle) * weight).T, (-np.sin(angle) * weight).T], 1)
    outer_hi, outer_lo = split_np(outer)
    inv_hi, inv_lo = split_np(inverse)
    fwd = np.stack(split_np(forward))
    bwd = np.stack(split_np(backward))
    outer3 = np.concatenate([outer_hi, outer_lo, outer_hi], 1)
    inv3 = np.concatenate([inv_hi, inv_lo, inv_hi], 1)
    return outer3, twist, fwd, bwd, inv3


def split(x):
    hi = x.astype(BF16)
    return hi, (x - hi.astype(F32)).astype(BF16)


def mm(a, b):
    return jnp.dot(a, b, preferred_element_type=F32)


def mm3(x, table):
    hi, lo = split(x)
    return mm(hi, table[0]) + (mm(lo, table[0]) + mm(hi, table[1]))


def local_sums(codes_ref, order, emb_fine_ref, emb_coarse_ref, ids_ref, sums_ref):
    row = lax.broadcasted_iota(jnp.int32, (FRAME, FRAME), 0)
    pick = (row == order).astype(BF16)
    pick_half = (row[: FRAME // 2] == order // 2).astype(BF16)

    def looked(codes, pick):
        hi = (codes // 32).astype(F32).astype(BF16)
        lo = (codes % 32).astype(F32).astype(BF16)
        return (mm(hi, pick) * 32.0 + mm(lo, pick)).astype(jnp.int32)

    fine = looked(codes_ref[0:4, :], pick)
    coarse = looked(codes_ref[4:8, : FRAME // 2], pick_half)
    ids_ref[0:4, :] = fine
    ids_ref[4:8, :] = coarse
    vocab = lax.broadcasted_iota(jnp.int32, (emb_fine_ref.shape[0], FRAME), 0)
    dims = (((0,), (0,)), ((), ()))
    for frame in range(4):
        hot_fine = (vocab == fine[frame : frame + 1]).astype(BF16)
        hot_coarse = (vocab == coarse[frame : frame + 1]).astype(BF16)
        rows = lax.dot_general(emb_fine_ref[...], hot_fine, dims, preferred_element_type=F32)
        rows = rows + lax.dot_general(
            emb_coarse_ref[...], hot_coarse, dims, preferred_element_type=F32
        )
        rows = rows.astype(BF16).astype(F32)
        total = jnp.sum(rows * rows, axis=0, keepdims=True)
        sums_ref[2 * frame : 2 * frame + 1, :] = total[:, :LANES]
        sums_ref[2 * frame + 1 : 2 * frame + 2, :] = total[:, LANES:]


GROUP = 16


def twisted(step, twist_ref):
    cos, sin = twist_ref[0], twist_ref[1]
    rows = []
    for i in range(GROUP):
        re = step[:ROWS_W, i * LANES : (i + 1) * LANES]
        im = step[ROWS_W:, i * LANES : (i + 1) * LANES]
        rows.append(jnp.concatenate([re * cos + im * sin, im * cos - re * sin], 1))
    return jnp.concatenate(rows, 0)


def spectrum_kernel(h_ref, outer_ref, twist_ref, fwd_ref, out_ref, wide_ref):
    channels = h_ref.shape[0]
    for q in range(TILES):
        wide_ref[pl.ds(q, channels, stride=TILES), :] = h_ref[:, q * LANES : (q + 1) * LANES]

    @pl.loop(0, channels // GROUP)
    def _(step):
        pieces = []
        for i in range(GROUP):
            hi, lo = split(wide_ref[pl.ds((step * GROUP + i) * TILES, TILES), :])
            pieces.append(jnp.concatenate([hi, hi, lo], 0))
        first = mm(outer_ref[...], jnp.concatenate(pieces, 1))
        out_ref[pl.ds(step * GROUP * ROWS_W, GROUP * ROWS_W), :] = mm3(
            twisted(first, twist_ref), fwd_ref
        )


def convolve_kernel(
    proj_ref,
    ids_ref,
    factor_ref,
    taps_ref,
    spec_ref,
    outer_ref,
    twist_ref,
    fwd_ref,
    bwd_ref,
    inv_ref,
    out_ref,
    left_ref,
    wide_ref,
    gate_ref,
    mix_ref,
    y_ref,
):
    channels = 32
    for s in range(16):
        left_ref[0:96, s * 128 : (s + 1) * 128] = proj_ref[s, :, :128]
        left_ref[96:192, s * 128 : (s + 1) * 128] = proj_ref[s, :, 128:]
    vocab = lax.broadcasted_iota(jnp.int32, (1024, FRAME), 0)

    @pl.loop(0, 8)
    def _(z):
        ids = ids_ref[z]
        for i in range(4):
            hot = jnp.concatenate(
                [
                    (vocab == ids[i : i + 1]).astype(BF16),
                    (vocab == ids[4 + i : 5 + i]).astype(BF16),
                ],
                0,
            )
            both = mm(left_ref[...], hot)
            value = both[:96] + both[96:]
            for half in range(2):
                wide_ref[pl.ds(z * 8 + 2 * i + half, 96, stride=TILES), :] = value[
                    :, half * LANES : (half + 1) * LANES
                ]

    tap_row = lax.broadcasted_iota(jnp.int32, (LANES, LANES), 0)
    tap_col = lax.broadcasted_iota(jnp.int32, (LANES, LANES), 1)
    group_row = lax.broadcasted_iota(jnp.int32, taps_ref.shape[1:], 0)
    rows = 16 * TILES
    first_tile = lax.broadcasted_iota(jnp.int32, (rows, LANES), 0) % TILES == 0
    scale = jnp.concatenate([factor_ref[...]] * 16, 0)

    def filtered(k, g):
        wanted = 2 * lax.axis_index("seq") + g
        own = jnp.where(group_row == wanted, taps_ref[k].astype(F32), 0.0)
        taps = jnp.broadcast_to(jnp.sum(own, axis=0, keepdims=True), (LANES, LANES))
        turned = pltpu.roll(taps, 0, 1, stride=1, stride_axis=0)
        both = jnp.concatenate(
            [
                jnp.where(tap_col >= tap_row, turned, 0.0),
                jnp.where(tap_col < tap_row, turned, 0.0),
            ],
            1,
        ).astype(BF16)
        start = (2 * k + g) * rows
        x = (wide_ref[start : start + rows, :] * scale).astype(BF16)
        parts = mm(x, both)
        carried = jnp.where(first_tile, 0.0, pltpu.roll(parts[:, LANES:], 1, 0))
        return (parts[:, :LANES] + carried).astype(BF16)

    for g in range(2):
        gate_ref[g * rows : (g + 1) * rows, :] = filtered(0, g)
        left = filtered(1, g).astype(F32)
        mix_ref[g * rows : (g + 1) * rows, :] = (left * filtered(2, g).astype(F32)).astype(BF16)

    @pl.loop(0, channels // GROUP)
    def _(step):
        pieces = []
        for i in range(GROUP):
            x = mix_ref[pl.ds((step * GROUP + i) * TILES, TILES), :]
            pieces.append(jnp.concatenate([x, x], 0))
        first = mm(outer_ref[:, : 2 * TILES], jnp.concatenate(pieces, 1))
        spec = mm3(twisted(first, twist_ref), fwd_ref)
        other = spec_ref[pl.ds(step * GROUP * ROWS_W, GROUP * ROWS_W), :]
        re, im = spec[:, :LANES], spec[:, LANES:]
        ore, oim = other[:, :LANES], other[:, LANES:]
        back = mm3(jnp.concatenate([re * ore - im * oim, re * oim + im * ore], 1), bwd_ref)
        cos, sin = twist_ref[0], twist_ref[1]
        columns = []
        for i in range(GROUP):
            bre = back[i * ROWS_W : (i + 1) * ROWS_W, :LANES]
            bim = back[i * ROWS_W : (i + 1) * ROWS_W, LANES:]
            undone = jnp.concatenate([bre * cos - bim * sin, bim * cos + bre * sin], 0)
            hi, lo = split(undone)
            columns.append(jnp.concatenate([hi, hi, lo], 0))
        result = mm(inv_ref[...], jnp.concatenate(columns, 1))
        for i in range(GROUP):
            at = pl.ds((step * GROUP + i) * TILES, TILES)
            conv = result[:, i * LANES : (i + 1) * LANES].astype(BF16).astype(F32)
            y_ref[at, :] = gate_ref[at, :].astype(F32) * conv

    for q in range(TILES):
        out_ref[q // 8, :, (q % 8) * LANES : (q % 8 + 1) * LANES] = y_ref[
            pl.ds(q, channels, stride=TILES), :
        ].astype(BF16)


def convolve(proj, ids, factor, taps, spec, interpret=False):
    outer3, twist, fwd, bwd, inv3 = tables()
    return pl.pallas_call(
        convolve_kernel,
        out_shape=jax.ShapeDtypeStruct((8, 32, 1024), BF16),
        scratch_shapes=[
            pltpu.VMEM((192, 2048), BF16),
            pltpu.VMEM((96 * TILES, LANES), F32),
            pltpu.VMEM((32 * TILES, LANES), BF16),
            pltpu.VMEM((32 * TILES, LANES), BF16),
            pltpu.VMEM((32 * TILES, LANES), F32),
        ],
        compiler_params=pltpu.CompilerParams(vmem_limit_bytes=BIG),
        interpret=interpret,
        name="convolve",
    )(proj, ids, factor, taps, spec, outer3, twist, fwd, bwd, inv3)


def here():
    return lax.axis_index("seq"), lax.axis_index("chan"), lax.axis_index("rep")


def greet(peers):
    barrier = pltpu.get_barrier_semaphore()
    for peer in peers:
        pl.semaphore_signal(barrier, inc=1, device_id=peer, device_id_type=MESH)
    pl.semaphore_wait(barrier, len(peers))


def push(src, dst, sems, index, peer):
    copy = pltpu.make_async_remote_copy(
        src_ref=src,
        dst_ref=dst,
        send_sem=sems[0].at[index],
        recv_sem=sems[1].at[index],
        device_id=peer,
        device_id_type=MESH,
    )
    copy.start()
    return copy


def front_kernel(
    fine_ref,
    coarse_ref,
    order_ref,
    gain_ref,
    emb_fine_ref,
    emb_coarse_ref,
    filter_ref,
    outer_ref,
    twist_ref,
    fwd_ref,
    w_ref,
    proj_out,
    factor_out,
    ids_out,
    spec_ref,
    codes_ref,
    rows_ref,
    gains_ref,
    sums_ref,
    x_ref,
    wv_ref,
    proj_ref,
    wide_ref,
    send,
    recv,
    own,
):
    z, c, r = here()
    sems = (send, recv)
    plane = [(z, lax.rem(c + j, 16), r) for j in range(1, 16)]
    line = [(lax.rem(z + j, 8), c, r) for j in range(1, 8)]
    sibling = (z, c, 1 - r)
    slot = r * 8 + z
    weights = [pltpu.make_async_copy(w_ref.at[k], wv_ref.at[k], own.at[k]) for k in range(3)]
    for copy in weights:
        copy.start()
    at = pl.ds(pl.multiple_of(z * 128, 128), 128)

    @pl.when(r == 0)
    def _():
        rows_ref[c] = emb_fine_ref[at, :]

    @pl.when(r != 0)
    def _():
        rows_ref[c] = emb_coarse_ref[at, :]

    gains_ref[c] = jnp.broadcast_to(gain_ref[...].reshape(1, FRAME).astype(F32), (8, FRAME))
    greet(plane + line + [sibling])
    sent = []
    index = [0]

    def tell(src, dst, peer):
        copy = push(src, dst, sems, index[0], peer)
        index[0] += 1
        sent.append(copy)
        return copy

    gains = [tell(gains_ref.at[c], gains_ref.at[c], peer) for peer in plane]
    y, x = c // 4, lax.rem(c, 4)

    def chan(at_x, at_y):
        return lax.rem(at_y + 8, 4) * 4 + lax.rem(at_x + 8, 4)

    def hop(lead, along, across, part, direction, phase):
        axes = (0, 1) if lead == 0 else (1, 0)
        offset = [0, 0]
        offset[axes[0]], offset[axes[1]] = along, across
        step = [0, 0]
        step[axes[phase]] = direction
        target = (z, chan(x + step[0], y + step[1]), r)
        part_rows = pl.ds(lead * 64 + (0 if part is None else part * 32), 64 if part is None else 32)
        block = rows_ref.at[chan(x - offset[0], y - offset[1]), part_rows]
        number = index[0]
        tell(block, block, target)
        landed = rows_ref.at[chan(x - offset[0] - step[0], y - offset[1] - step[1]), part_rows]
        return pltpu.make_async_remote_copy(
            src_ref=landed,
            dst_ref=landed,
            send_sem=send.at[number],
            recv_sem=recv.at[number],
            device_id=target,
            device_id_type=MESH,
        )

    first = {(lead, d): hop(lead, 0, 0, None, d, 0) for lead in range(2) for d in (1, -1)}
    second = {(lead, 0, d): hop(lead, 0, 0, None, d, 1) for lead in range(2) for d in (1, -1)}
    turned = {}
    for d in (1, -1):
        for lead in range(2):
            first[lead, d].wait_recv()
            turned[lead, d] = hop(lead, d, 0, 0 if d == 1 else 1, d, 0)
            for e in (1, -1):
                second[lead, d, e] = hop(lead, d, 0, None, e, 1)
    last = []

    def onward(lead, along):
        for e in (1, -1):
            second[lead, along, e].wait_recv()
            last.append(hop(lead, along, e, 0 if e == 1 else 1, e, 1))

    for lead in range(2):
        onward(lead, 0)
    for lead in range(2):
        turned[lead, 1].wait_recv()
        turned[lead, -1].wait_recv()
        for e in (1, -1):
            second[lead, 2, e] = hop(lead, 2, 0, None, e, 1)
    for along in (1, -1):
        for lead in range(2):
            onward(lead, along)
    for lead in range(2):
        onward(lead, 2)
    for i in range(4):
        codes_ref[i : i + 1, :] = fine_ref[i * FRAME : (i + 1) * FRAME].reshape(1, FRAME)
        codes_ref[4 + i : 5 + i, : FRAME // 2] = coarse_ref[
            i * FRAME // 2 : (i + 1) * FRAME // 2
        ].reshape(1, FRAME // 2)
    local_sums(
        codes_ref,
        order_ref[...].reshape(1, FRAME),
        emb_fine_ref,
        emb_coarse_ref,
        ids_out.at[z],
        sums_ref.at[c],
    )
    sums = [tell(sums_ref.at[c], sums_ref.at[c], peer) for peer in plane]
    ids = [tell(ids_out.at[z], ids_out.at[z], peer) for peer in line]

    def prepare(origin):
        hi, lo = split(rows_ref[origin].astype(F32) * gains_ref[origin, 0:1, :])
        columns = pl.ds(pl.multiple_of(origin * 256, 256), 256)
        x_ref[0:128, columns] = hi
        x_ref[128:256, columns] = lo

    for arrival in last:
        arrival.wait_recv()
    for copy in gains:
        copy.wait_recv()
    prepare(c)
    for other in range(1, 16):
        prepare(lax.rem(c + other, 16))
    dealt = [[] for _ in range(7)]
    for k in range(3):
        weights[k].wait()
        both = mm(x_ref[...], wv_ref[k])
        hi, lo = split(jnp.transpose(both[:128] + both[128:]))
        proj_ref[k, :, :128] = hi
        proj_ref[k, :, 128:] = lo
        for j, peer in enumerate(line):
            src = proj_ref.at[k, pl.ds(pl.multiple_of(peer[0] * 32, 32), 32), :]
            dealt[j].append(tell(src, proj_out.at[slot, k], peer))
    for copy in sums:
        copy.wait_recv()
    total = sums_ref[0]
    for other in range(1, 16):
        total = total + sums_ref[other]
    factor_out[z] = lax.rsqrt(total / (16 * 256.0) + EPSILON)
    factors = [tell(factor_out.at[z], factor_out.at[z], peer) for peer in line]
    proj_out[slot] = proj_ref[:, pl.ds(pl.multiple_of(z * 32, 32), 32), :]
    across = [tell(proj_out.at[slot], proj_out.at[slot], sibling)]
    spectrum_kernel(filter_ref, outer_ref, twist_ref, fwd_ref, spec_ref, wide_ref)
    for j in range(7):
        for copy in dealt[j]:
            copy.wait_recv()
        landed = proj_out.at[r * 8 + lax.rem(z + 7 - j, 8)]
        across.append(tell(landed, landed, sibling))
    for copy in ids + factors + across:
        copy.wait_recv()
    for copy in sent:
        copy.wait_send()


def front(fine, coarse, order, gain, emb_fine, emb_coarse, long_filter, w):
    outer3, twist, fwd, _, _ = tables()
    channels = long_filter.shape[0]
    vmem = pl.BlockSpec(memory_space=pltpu.VMEM)
    copies = 30 + 40 + 7 + 21 + 7 + 8
    return pl.pallas_call(
        front_kernel,
        in_specs=[vmem] * 10 + [ANY],
        out_specs=[vmem] * 4,
        out_shape=(
            jax.ShapeDtypeStruct((16, 3, 32, 256), BF16),
            jax.ShapeDtypeStruct((8, 8, LANES), F32),
            jax.ShapeDtypeStruct((8, 8, FRAME), jnp.int32),
            jax.ShapeDtypeStruct((channels * ROWS_W, 256), F32),
        ),
        scratch_shapes=[
            pltpu.VMEM((8, FRAME), jnp.int32),
            pltpu.VMEM((16, 128, 256), BF16),
            pltpu.VMEM((16, 8, FRAME), F32),
            pltpu.VMEM((16, 8, LANES), F32),
            pltpu.VMEM((256, 4096), BF16),
            pltpu.VMEM((3, 4096, 256), BF16),
            pltpu.VMEM((3, 256, 256), BF16),
            pltpu.VMEM((channels * TILES, LANES), F32),
            pltpu.SemaphoreType.DMA((copies,)),
            pltpu.SemaphoreType.DMA((copies,)),
            pltpu.SemaphoreType.DMA((3,)),
        ],
        compiler_params=pltpu.CompilerParams(
            collective_id=0, has_side_effects=True, vmem_limit_bytes=BIG
        ),
        name="front",
    )(fine, coarse, order, gain, emb_fine, emb_coarse, long_filter, outer3, twist, fwd, w)


CHUNKS = 2


def tail_kernel(
    y_ref,
    w_ref,
    hyena_ref,
    attn_ref,
    wv_ref,
    x_ref,
    land_ref,
    acc_ref,
    state_ref,
    parts_ref,
    prefix_ref,
    incoming_ref,
    send,
    recv,
    own,
):
    z, c, r = here()
    y, x = c // 4, lax.rem(c, 4)
    sems = (send, recv)
    length = x_ref.shape[1]
    span = length // CHUNKS

    def chan(at_x, at_y):
        return lax.rem(at_y + 8, 4) * 4 + lax.rem(at_x + 8, 4)

    def device(at_x, at_y):
        return (z, chan(at_x, at_y), r)

    line = [(lax.rem(z + j, 8), c, r) for j in range(1, 8)]
    weights = pltpu.make_async_copy(w_ref, wv_ref, own.at[0])
    weights.start()
    greet(line + [device(x + 1, y), device(x - 1, y), device(x, y + 1), device(x, y - 1)])
    index = [0]
    sent = []

    def tell(src, dst, peer):
        copy = push(src, dst, sems, index[0], peer)
        index[0] += 1
        sent.append(copy)
        return copy

    mine_rows = pl.ds(pl.multiple_of(z * 32, 32), 32)
    turned = []
    kept = []
    for t in range(CHUNKS):
        at = pl.ds(t * span, span)
        kept.append(
            pltpu.make_async_copy(y_ref.at[z, :, at], x_ref.at[mine_rows, at], own.at[1 + t])
        )
        kept[-1].start()
        if t == 0:
            turned.append([tell(y_ref.at[p[0], :, at], x_ref.at[mine_rows, at], p) for p in line])
    half = x_ref.shape[0] // 2
    quarter = half // 2

    def send_block(t, lead, along, across, part, direction, phase):
        axes = (0, 1) if lead == 0 else (1, 0)
        offset = [0, 0]
        offset[axes[0]], offset[axes[1]] = along, across
        step = [0, 0]
        step[axes[phase]] = direction
        target = device(x + step[0], y + step[1])
        start = lead * half + (0 if part is None else part * quarter)
        rows = pl.ds(start, half if part is None else quarter)
        at = pl.ds(t * span, span)
        dst = land_ref.at[chan(x - offset[0], y - offset[1]), rows, at]
        src = x_ref.at[rows, at] if along == 0 and across == 0 else dst
        number = index[0]
        tell(src, dst, target)
        came = [offset[0] + step[0], offset[1] + step[1]]
        landed = land_ref.at[chan(x - came[0], y - came[1]), rows, at]
        return pltpu.make_async_remote_copy(
            src_ref=landed,
            dst_ref=landed,
            send_sem=send.at[number],
            recv_sem=recv.at[number],
            device_id=target,
            device_id_type=MESH,
        )

    first = {}
    second = {}
    forward = {}
    pending = []

    def multiply(t, lead, along, across):
        at = slice(t * span, (t + 1) * span)
        rows = slice(lead * half, (lead + 1) * half)
        offset = (along, across) if lead == 0 else (across, along)
        origin = chan(x - offset[0], y - offset[1])
        block = x_ref[rows, at] if offset == (0, 0) else land_ref[origin, rows, at]
        depth = pl.ds(pl.multiple_of(origin * 2 * half + lead * half, half), half)
        for k in range(3):
            product = lax.dot_general(
                wv_ref[k, depth, :], block, (((0,), (0,)), ((), ())), preferred_element_type=F32
            )
            if (along, across, lead) == (0, 0, 0):
                acc_ref[k, :, at] = product
            else:
                acc_ref[k, :, at] += product

    def drain(count):
        for _ in range(min(count, len(pending))):
            multiply(*pending.pop(0))

    def open_chunk(t):
        kept[t].wait()
        for copy in turned[t]:
            copy.wait_recv()
        if t + 1 < CHUNKS:
            at = pl.ds((t + 1) * span, span)
            turned.append([tell(y_ref.at[p[0], :, at], x_ref.at[mine_rows, at], p) for p in line])
        for lead in range(2):
            for d in (1, -1):
                first[t, lead, d] = send_block(t, lead, 0, 0, None, d, 0)
        for lead in range(2):
            for d in (1, -1):
                second[t, lead, 0, d] = send_block(t, lead, 0, 0, None, d, 1)
        for lead in range(2):
            pending.append((t, lead, 0, 0))

    last = []

    def onward(t, lead, along):
        for e in (1, -1):
            second[t, lead, along, e].wait_recv()
            last.append((t, lead, along, send_block(t, lead, along, e, 0 if e == 1 else 1, e, 1)))
        for e in (1, -1):
            pending.append((t, lead, along, e))

    open_chunk(0)
    weights.wait()
    for t in range(CHUNKS):
        for d in (1, -1):
            for lead in range(2):
                first[t, lead, d].wait_recv()
                forward[t, lead, d] = send_block(t, lead, d, 0, 0 if d == 1 else 1, d, 0)
                for e in (1, -1):
                    second[t, lead, d, e] = send_block(t, lead, d, 0, None, e, 1)
                pending.append((t, lead, d, 0))
        if t + 1 < CHUNKS:
            open_chunk(t + 1)
        else:
            back = pltpu.make_async_copy(x_ref, hyena_ref, own.at[CHUNKS + 1])
            back.start()
        drain(2)
        for lead in range(2):
            onward(t, lead, 0)
            drain(1)
        for lead in range(2):
            forward[t, lead, 1].wait_recv()
            forward[t, lead, -1].wait_recv()
            for e in (1, -1):
                second[t, lead, 2, e] = send_block(t, lead, 2, 0, None, e, 1)
            pending.append((t, lead, 2, 0))
            drain(1)
    for t in range(CHUNKS):
        for along in (1, -1, 2):
            for lead in range(2):
                onward(t, lead, along)
                drain(3)
    for t, lead, along, arrival in last:
        arrival.wait_recv()
    for position in range(0, len(last), 2):
        t, lead, along, _ = last[position]
        pending.append((t, lead, along, 2))
    drain(len(pending))

    blocks = length // BLOCK
    heads = [[acc_ref[k, :, b * BLOCK : (b + 1) * BLOCK].astype(BF16) for b in range(blocks)] for k in range(3)]
    states = [
        lax.dot_general(
            heads[1][b], heads[2][b], (((1,), (1,)), ((), ())), preferred_element_type=F32
        )
        for b in range(blocks)
    ]
    total = states[0]
    for b in range(1, blocks):
        total = total + states[b]
    state_ref[...] = total.reshape(8, HD // 8, HD)
    parts_ref[z] = state_ref[z]
    gathered = [tell(state_ref.at[p[0]], parts_ref.at[z], p) for p in line]
    row = lax.broadcasted_iota(jnp.int32, (BLOCK, BLOCK), 0)
    column = lax.broadcasted_iota(jnp.int32, (BLOCK, BLOCK), 1)
    queries = []
    inside = []

    def local(b):
        queries.append(jnp.transpose(heads[0][b].astype(F32)).astype(BF16))
        scores = mm(queries[b], heads[1][b])
        scores = jnp.where(row >= column, scores, 0.0).astype(BF16)
        inside.append(
            lax.dot_general(
                scores, heads[2][b], (((1,), (1,)), ((), ())), preferred_element_type=F32
            )
        )

    local(0)
    for copy in gathered:
        copy.wait_recv()
    running = jnp.zeros((HD // 8, HD), F32)
    for step in range(8):
        prefix_ref[step] = running
        running = running + parts_ref[step]
    incoming_ref[z] = prefix_ref[z]
    dealt = [tell(prefix_ref.at[p[0]], incoming_ref.at[z], p) for p in line]
    for b in range(1, blocks):
        local(b)
    for copy in dealt:
        copy.wait_recv()
    earlier = incoming_ref[...].reshape(HD, HD)
    place = lax.broadcasted_iota(jnp.int32, (BLOCK, HD), 0)
    for b in range(blocks):
        carried = mm(queries[b], earlier.astype(BF16))
        position = z * length + b * BLOCK + place + 1
        divisor = jnp.sqrt((position * HD).astype(F32))
        attn_ref[b * BLOCK : (b + 1) * BLOCK, :] = ((inside[b] + carried) / divisor).astype(BF16)
        earlier = earlier + states[b]
    for copy in sent:
        copy.wait_send()
    back.wait()


def tail(y, w):
    seqs, channels, length = y.shape
    depth = seqs * channels
    vmem = pl.BlockSpec(memory_space=pltpu.VMEM)
    copies = CHUNKS * (7 + 40) + 14
    return pl.pallas_call(
        tail_kernel,
        in_specs=[ANY, ANY],
        out_specs=[ANY, vmem],
        out_shape=(
            jax.ShapeDtypeStruct((depth, length), BF16),
            jax.ShapeDtypeStruct((length, HD), BF16),
        ),
        scratch_shapes=[
            pltpu.VMEM(w.shape, BF16),
            pltpu.VMEM((depth, length), BF16),
            pltpu.VMEM((16, depth, length), BF16),
            pltpu.VMEM((3, HD, length), F32),
            pltpu.VMEM((8, HD // 8, HD), F32),
            pltpu.VMEM((8, HD // 8, HD), F32),
            pltpu.VMEM((8, HD // 8, HD), F32),
            pltpu.VMEM((8, HD // 8, HD), F32),
            pltpu.SemaphoreType.DMA((copies,)),
            pltpu.SemaphoreType.DMA((copies,)),
            pltpu.SemaphoreType.DMA((CHUNKS + 2,)),
        ],
        compiler_params=pltpu.CompilerParams(
            collective_id=2, has_side_effects=True, vmem_limit_bytes=BIG
        ),
        name="tail",
    )(y, w)


def settle_kernel(hyena_ref, attn_ref, hyena_out, attn_out):
    hyena_out[...] = hyena_ref[...]
    attn_out[...] = attn_ref[...]


def settle(hyena, attn):
    return pl.pallas_call(
        settle_kernel,
        out_shape=(
            jax.ShapeDtypeStruct(hyena.shape, hyena.dtype),
            jax.ShapeDtypeStruct(attn.shape, attn.dtype),
        ),
        name="settle",
    )(hyena, attn)


def shards(
    fine_codes,
    coarse_codes,
    frame_order,
    emb_fine,
    emb_coarse,
    norm_gain,
    w_hyena,
    short_taps,
    long_filter,
    w_attn,
):
    proj_all, factor_all, ids_all, spec = front(
        fine_codes,
        coarse_codes,
        frame_order,
        norm_gain,
        emb_fine,
        emb_coarse,
        long_filter,
        jnp.transpose(w_hyena, (1, 0, 2)),
    )
    y = convolve(
        proj_all.reshape(16, 96, 256), ids_all, factor_all.reshape(TILES, LANES), short_taps, spec
    )
    return settle(*tail(y, jnp.transpose(w_attn, (1, 0, 2))))


def solution(mesh):
    return jax.shard_map(
        shards,
        mesh=mesh,
        in_specs=(
            P(("rep", "seq")),
            P(("rep", "seq")),
            P(),
            P(None, "chan"),
            P(None, "chan"),
            P("chan"),
            P(None, None, "chan"),
            P(None, "chan", None),
            P(("chan", "seq"), None),
            P(None, None, "chan"),
        ),
        out_specs=(P("chan", ("rep", "seq")), P(("rep", "seq"), "chan")),
        check_vma=False,
    )
```

```python
import functools
import math

import jax
import jax.numpy as jnp
import numpy as np
from jax import lax
from jax.experimental import pallas as pl
from jax.experimental.pallas import tpu as pltpu
from jax.sharding import PartitionSpec as P

HD = 128
FRAME = 256
BLOCK = 512
LANES = 128
EPSILON = 1e-05
F32 = jnp.float32
BF16 = jnp.bfloat16
ANY = pl.BlockSpec(memory_space=pl.ANY)
MESH = pl.DeviceIdType.MESH
BIG = 56 << 20

ROWS_W = 72
TILES = 64
POINTS = 2 * TILES * LANES


def split_np(x):
    hi = np.asarray(x, np.float32).astype(jnp.bfloat16)
    lo = (np.asarray(x, np.float64) - hi.astype(np.float64)).astype(np.float32).astype(jnp.bfloat16)
    return hi, lo


@functools.lru_cache(None)
def tables():
    w = np.arange(ROWS_W)[:, None]
    kept = (w <= 64).astype(np.float64)
    q = np.arange(TILES)[None, :]
    angle = 2 * np.pi * ((w * q) % 128) / 128
    outer = np.concatenate([np.cos(angle) * kept, -np.sin(angle) * kept], 0)
    a = np.arange(LANES)[None, :]
    turn = 2 * np.pi * (w * a) / POINTS
    twist = np.stack([np.cos(turn) * kept, np.sin(turn) * kept]).astype(np.float32)
    m = np.arange(LANES)
    inner = 2 * np.pi * ((m[:, None] * m[None, :]) % 128) / 128
    c, s = np.cos(inner), np.sin(inner)
    forward = np.block([[c, -s], [s, c]])
    backward = np.block([[c, s], [-s, c]])
    weight = np.where((w == 0) | (w == 64), 1.0, 2.0) * kept / POINTS
    inverse = np.concatenate([(np.cos(angle) * weight).T, (-np.sin(angle) * weight).T], 1)
    outer_hi, outer_lo = split_np(outer)
    inv_hi, inv_lo = split_np(inverse)
    fwd = np.stack(split_np(forward))
    bwd = np.stack(split_np(backward))
    outer3 = np.concatenate([outer_hi, outer_lo, outer_hi], 1)
    inv3 = np.concatenate([inv_hi, inv_lo, inv_hi], 1)
    return outer3, twist, fwd, bwd, inv3


def split(x):
    hi = x.astype(BF16)
    return hi, (x - hi.astype(F32)).astype(BF16)


def mm(a, b):
    return jnp.dot(a, b, preferred_element_type=F32)


def mm3(x, table):
    hi, lo = split(x)
    return mm(hi, table[0]) + (mm(lo, table[0]) + mm(hi, table[1]))


def local_sums(codes_ref, order, emb_fine_ref, emb_coarse_ref, ids_ref, sums_ref):
    row = lax.broadcasted_iota(jnp.int32, (FRAME, FRAME), 0)
    pick = (row == order).astype(BF16)
    pick_half = (row[: FRAME // 2] == order // 2).astype(BF16)

    def looked(codes, pick):
        hi = (codes // 32).astype(F32).astype(BF16)
        lo = (codes % 32).astype(F32).astype(BF16)
        return (mm(hi, pick) * 32.0 + mm(lo, pick)).astype(jnp.int32)

    fine = looked(codes_ref[0:4, :], pick)
    coarse = looked(codes_ref[4:8, : FRAME // 2], pick_half)
    ids_ref[0:4, :] = fine
    ids_ref[4:8, :] = coarse
    vocab = lax.broadcasted_iota(jnp.int32, (emb_fine_ref.shape[0], FRAME), 0)
    dims = (((0,), (0,)), ((), ()))
    for frame in range(4):
        hot_fine = (vocab == fine[frame : frame + 1]).astype(BF16)
        hot_coarse = (vocab == coarse[frame : frame + 1]).astype(BF16)
        rows = lax.dot_general(emb_fine_ref[...], hot_fine, dims, preferred_element_type=F32)
        rows = rows + lax.dot_general(
            emb_coarse_ref[...], hot_coarse, dims, preferred_element_type=F32
        )
        rows = rows.astype(BF16).astype(F32)
        total = jnp.sum(rows * rows, axis=0, keepdims=True)
        sums_ref[2 * frame : 2 * frame + 1, :] = total[:, :LANES]
        sums_ref[2 * frame + 1 : 2 * frame + 2, :] = total[:, LANES:]


GROUP = 16


def twisted(step, twist_ref):
    cos, sin = twist_ref[0], twist_ref[1]
    rows = []
    for i in range(GROUP):
        re = step[:ROWS_W, i * LANES : (i + 1) * LANES]
        im = step[ROWS_W:, i * LANES : (i + 1) * LANES]
        rows.append(jnp.concatenate([re * cos + im * sin, im * cos - re * sin], 1))
    return jnp.concatenate(rows, 0)


def spectrum_kernel(h_ref, outer_ref, twist_ref, fwd_ref, out_ref, wide_ref):
    channels = h_ref.shape[0]
    for q in range(TILES):
        wide_ref[pl.ds(q, channels, stride=TILES), :] = h_ref[:, q * LANES : (q + 1) * LANES]

    @pl.loop(0, channels // GROUP)
    def _(step):
        pieces = []
        for i in range(GROUP):
            hi, lo = split(wide_ref[pl.ds((step * GROUP + i) * TILES, TILES), :])
            pieces.append(jnp.concatenate([hi, hi, lo], 0))
        first = mm(outer_ref[...], jnp.concatenate(pieces, 1))
        out_ref[pl.ds(step * GROUP * ROWS_W, GROUP * ROWS_W), :] = mm3(
            twisted(first, twist_ref), fwd_ref
        )


def convolve_kernel(
    proj_ref,
    ids_ref,
    factor_ref,
    taps_ref,
    spec_ref,
    outer_ref,
    twist_ref,
    fwd_ref,
    bwd_ref,
    inv_ref,
    out_ref,
    left_ref,
    wide_ref,
    gate_ref,
    mix_ref,
    y_ref,
):
    channels = 32
    for s in range(16):
        both = proj_ref[s].reshape(96, 256)
        left_ref[0:96, s * 128 : (s + 1) * 128] = both[:, :128]
        left_ref[96:192, s * 128 : (s + 1) * 128] = both[:, 128:]
    vocab = lax.broadcasted_iota(jnp.int32, (1024, FRAME), 0)

    @pl.loop(0, 8)
    def _(z):
        ids = ids_ref[z]
        for i in range(4):
            hot = jnp.concatenate(
                [
                    (vocab == ids[i : i + 1]).astype(BF16),
                    (vocab == ids[4 + i : 5 + i]).astype(BF16),
                ],
                0,
            )
            both = mm(left_ref[...], hot)
            value = both[:96] + both[96:]
            for half in range(2):
                wide_ref[pl.ds(z * 8 + 2 * i + half, 96, stride=TILES), :] = value[
                    :, half * LANES : (half + 1) * LANES
                ]

    tap_row = lax.broadcasted_iota(jnp.int32, (LANES, LANES), 0)
    tap_col = lax.broadcasted_iota(jnp.int32, (LANES, LANES), 1)
    group_row = lax.broadcasted_iota(jnp.int32, taps_ref.shape[1:], 0)
    rows = 16 * TILES
    first_tile = lax.broadcasted_iota(jnp.int32, (rows, LANES), 0) % TILES == 0
    scale = jnp.concatenate([factor_ref[...].reshape(TILES, LANES)] * 16, 0)

    def filtered(k, g):
        wanted = 2 * lax.axis_index("seq") + g
        own = jnp.where(group_row == wanted, taps_ref[k].astype(F32), 0.0)
        taps = jnp.broadcast_to(jnp.sum(own, axis=0, keepdims=True), (LANES, LANES))
        turned = pltpu.roll(taps, 0, 1, stride=1, stride_axis=0)
        both = jnp.concatenate(
            [
                jnp.where(tap_col >= tap_row, turned, 0.0),
                jnp.where(tap_col < tap_row, turned, 0.0),
            ],
            1,
        ).astype(BF16)
        start = (2 * k + g) * rows
        x = (wide_ref[start : start + rows, :] * scale).astype(BF16)
        parts = mm(x, both)
        carried = jnp.where(first_tile, 0.0, pltpu.roll(parts[:, LANES:], 1, 0))
        return (parts[:, :LANES] + carried).astype(BF16)

    for g in range(2):
        gate_ref[g * rows : (g + 1) * rows, :] = filtered(0, g)
        left = filtered(1, g).astype(F32)
        mix_ref[g * rows : (g + 1) * rows, :] = (left * filtered(2, g).astype(F32)).astype(BF16)

    @pl.loop(0, channels // GROUP)
    def _(step):
        pieces = []
        for i in range(GROUP):
            x = mix_ref[pl.ds((step * GROUP + i) * TILES, TILES), :]
            pieces.append(jnp.concatenate([x, x], 0))
        first = mm(outer_ref[:, : 2 * TILES], jnp.concatenate(pieces, 1))
        spec = mm3(twisted(first, twist_ref), fwd_ref)
        other = spec_ref[pl.ds(step * GROUP * ROWS_W, GROUP * ROWS_W), :]
        re, im = spec[:, :LANES], spec[:, LANES:]
        ore, oim = other[:, :LANES], other[:, LANES:]
        back = mm3(jnp.concatenate([re * ore - im * oim, re * oim + im * ore], 1), bwd_ref)
        cos, sin = twist_ref[0], twist_ref[1]
        columns = []
        for i in range(GROUP):
            bre = back[i * ROWS_W : (i + 1) * ROWS_W, :LANES]
            bim = back[i * ROWS_W : (i + 1) * ROWS_W, LANES:]
            undone = jnp.concatenate([bre * cos - bim * sin, bim * cos + bre * sin], 0)
            hi, lo = split(undone)
            columns.append(jnp.concatenate([hi, hi, lo], 0))
        result = mm(inv_ref[...], jnp.concatenate(columns, 1))
        for i in range(GROUP):
            at = pl.ds((step * GROUP + i) * TILES, TILES)
            conv = result[:, i * LANES : (i + 1) * LANES].astype(BF16).astype(F32)
            y_ref[at, :] = gate_ref[at, :].astype(F32) * conv

    for q in range(TILES):
        out_ref[q // 8, :, (q % 8) * LANES : (q % 8 + 1) * LANES] = y_ref[
            pl.ds(q, channels, stride=TILES), :
        ].astype(BF16)


def here():
    return lax.axis_index("seq"), lax.axis_index("chan"), lax.axis_index("rep")


def greet(peers):
    barrier = pltpu.get_barrier_semaphore()
    for peer in peers:
        pl.semaphore_signal(barrier, inc=1, device_id=peer, device_id_type=MESH)
    pl.semaphore_wait(barrier, len(peers))


def push(src, dst, sems, index, peer):
    copy = pltpu.make_async_remote_copy(
        src_ref=src,
        dst_ref=dst,
        send_sem=sems[0].at[index],
        recv_sem=sems[1].at[index],
        device_id=peer,
        device_id_type=MESH,
    )
    copy.start()
    return copy


def front_kernel(
    fine_ref,
    coarse_ref,
    order_ref,
    gain_ref,
    emb_fine_ref,
    emb_coarse_ref,
    filter_ref,
    outer_ref,
    twist_ref,
    fwd_ref,
    bwd_ref,
    inv_ref,
    taps_ref,
    w_ref,
    out_ref,
    proj_out,
    factor_out,
    ids_out,
    spec_ref,
    left_ref,
    all_ref,
    gate_ref,
    mix_ref,
    y_ref,
    codes_ref,
    rows_ref,
    gains_ref,
    sums_ref,
    x_ref,
    wv_ref,
    proj_ref,
    wide_ref,
    send,
    recv,
    own,
):
    z, c, r = here()
    sems = (send, recv)
    plane = [(z, lax.rem(c + j, 16), r) for j in range(1, 16)]
    line = [(lax.rem(z + j, 8), c, r) for j in range(1, 8)]
    sibling = (z, c, 1 - r)
    slot = r * 8 + z
    weights = [pltpu.make_async_copy(w_ref.at[k], wv_ref.at[k], own.at[k]) for k in range(3)]
    for copy in weights:
        copy.start()
    at = pl.ds(pl.multiple_of(z * 128, 128), 128)

    @pl.when(r == 0)
    def _():
        rows_ref[c] = emb_fine_ref[at, :]

    @pl.when(r != 0)
    def _():
        rows_ref[c] = emb_coarse_ref[at, :]

    gains_ref[c] = jnp.broadcast_to(gain_ref[...].reshape(1, FRAME).astype(F32), (8, FRAME))
    greet(plane + line + [sibling])
    sent = []
    index = [0]

    def tell(src, dst, peer):
        copy = push(src, dst, sems, index[0], peer)
        index[0] += 1
        sent.append(copy)
        return copy

    gains = [tell(gains_ref.at[c], gains_ref.at[c], peer) for peer in plane]
    y, x = c // 4, lax.rem(c, 4)

    def chan(at_x, at_y):
        return lax.rem(at_y + 8, 4) * 4 + lax.rem(at_x + 8, 4)

    def hop(lead, along, across, part, direction, phase):
        axes = (0, 1) if lead == 0 else (1, 0)
        offset = [0, 0]
        offset[axes[0]], offset[axes[1]] = along, across
        step = [0, 0]
        step[axes[phase]] = direction
        target = (z, chan(x + step[0], y + step[1]), r)
        part_rows = pl.ds(lead * 64 + (0 if part is None else part * 32), 64 if part is None else 32)
        block = rows_ref.at[chan(x - offset[0], y - offset[1]), part_rows]
        number = index[0]
        tell(block, block, target)
        landed = rows_ref.at[chan(x - offset[0] - step[0], y - offset[1] - step[1]), part_rows]
        return pltpu.make_async_remote_copy(
            src_ref=landed,
            dst_ref=landed,
            send_sem=send.at[number],
            recv_sem=recv.at[number],
            device_id=target,
            device_id_type=MESH,
        )

    first = {(lead, d): hop(lead, 0, 0, None, d, 0) for lead in range(2) for d in (1, -1)}
    second = {(lead, 0, d): hop(lead, 0, 0, None, d, 1) for lead in range(2) for d in (1, -1)}
    turned = {}
    for d in (1, -1):
        for lead in range(2):
            first[lead, d].wait_recv()
            turned[lead, d] = hop(lead, d, 0, 0 if d == 1 else 1, d, 0)
            for e in (1, -1):
                second[lead, d, e] = hop(lead, d, 0, None, e, 1)
    last = []

    def onward(lead, along):
        for e in (1, -1):
            second[lead, along, e].wait_recv()
            last.append(hop(lead, along, e, 0 if e == 1 else 1, e, 1))

    for lead in range(2):
        onward(lead, 0)
    for lead in range(2):
        turned[lead, 1].wait_recv()
        turned[lead, -1].wait_recv()
        for e in (1, -1):
            second[lead, 2, e] = hop(lead, 2, 0, None, e, 1)
    for along in (1, -1):
        for lead in range(2):
            onward(lead, along)
    for lead in range(2):
        onward(lead, 2)
    for i in range(4):
        codes_ref[i : i + 1, :] = fine_ref[i * FRAME : (i + 1) * FRAME].reshape(1, FRAME)
        codes_ref[4 + i : 5 + i, : FRAME // 2] = coarse_ref[
            i * FRAME // 2 : (i + 1) * FRAME // 2
        ].reshape(1, FRAME // 2)
    local_sums(
        codes_ref,
        order_ref[...].reshape(1, FRAME),
        emb_fine_ref,
        emb_coarse_ref,
        ids_out.at[z],
        sums_ref.at[c],
    )
    sums = [tell(sums_ref.at[c], sums_ref.at[c], peer) for peer in plane]
    ids = [tell(ids_out.at[z], ids_out.at[z], peer) for peer in line]

    def prepare(origin):
        hi, lo = split(rows_ref[origin].astype(F32) * gains_ref[origin, 0:1, :])
        columns = pl.ds(pl.multiple_of(origin * 256, 256), 256)
        x_ref[0:128, columns] = hi
        x_ref[128:256, columns] = lo

    for arrival in last:
        arrival.wait_recv()
    for copy in gains:
        copy.wait_recv()
    prepare(c)
    for other in range(1, 16):
        prepare(lax.rem(c + other, 16))
    dealt = [[] for _ in range(7)]
    for k in range(3):
        weights[k].wait()
        both = mm(x_ref[...], wv_ref[k])
        hi, lo = split(jnp.transpose(both[:128] + both[128:]))
        proj_ref[k, :, :128] = hi
        proj_ref[k, :, 128:] = lo
        for j, peer in enumerate(line):
            src = proj_ref.at[k, pl.ds(pl.multiple_of(peer[0] * 32, 32), 32), :]
            dealt[j].append(tell(src, proj_out.at[slot, k], peer))
    for copy in sums:
        copy.wait_recv()
    total = sums_ref[0]
    for other in range(1, 16):
        total = total + sums_ref[other]
    factor_out[z] = lax.rsqrt(total / (16 * 256.0) + EPSILON)
    factors = [tell(factor_out.at[z], factor_out.at[z], peer) for peer in line]
    proj_out[slot] = proj_ref[:, pl.ds(pl.multiple_of(z * 32, 32), 32), :]
    across = [tell(proj_out.at[slot], proj_out.at[slot], sibling)]
    spectrum_kernel(filter_ref, outer_ref, twist_ref, fwd_ref, spec_ref, wide_ref)
    for j in range(7):
        for copy in dealt[j]:
            copy.wait_recv()
        landed = proj_out.at[r * 8 + lax.rem(z + 7 - j, 8)]
        across.append(tell(landed, landed, sibling))
    for copy in ids + factors + across:
        copy.wait_recv()
    convolve_kernel(
        proj_out,
        ids_out,
        factor_out,
        taps_ref,
        spec_ref,
        outer_ref,
        twist_ref,
        fwd_ref,
        bwd_ref,
        inv_ref,
        out_ref,
        left_ref,
        all_ref,
        gate_ref,
        mix_ref,
        y_ref,
    )
    for copy in sent:
        copy.wait_send()


def front(fine, coarse, order, gain, emb_fine, emb_coarse, long_filter, taps, w):
    outer3, twist, fwd, bwd, inv3 = tables()
    channels = long_filter.shape[0]
    vmem = pl.BlockSpec(memory_space=pltpu.VMEM)
    copies = 30 + 40 + 7 + 21 + 7 + 8
    return pl.pallas_call(
        front_kernel,
        in_specs=[vmem] * 13 + [ANY],
        out_shape=jax.ShapeDtypeStruct((8, channels, 1024), BF16),
        scratch_shapes=[
            pltpu.VMEM((16, 3, 32, 256), BF16),
            pltpu.VMEM((8, 8, LANES), F32),
            pltpu.VMEM((8, 8, FRAME), jnp.int32),
            pltpu.VMEM((channels * ROWS_W, 256), F32),
            pltpu.VMEM((192, 2048), BF16),
            pltpu.VMEM((96 * TILES, LANES), F32),
            pltpu.VMEM((channels * TILES, LANES), BF16),
            pltpu.VMEM((channels * TILES, LANES), BF16),
            pltpu.VMEM((channels * TILES, LANES), F32),
            pltpu.VMEM((8, FRAME), jnp.int32),
            pltpu.VMEM((16, 128, 256), BF16),
            pltpu.VMEM((16, 8, FRAME), F32),
            pltpu.VMEM((16, 8, LANES), F32),
            pltpu.VMEM((256, 4096), BF16),
            pltpu.VMEM((3, 4096, 256), BF16),
            pltpu.VMEM((3, 256, 256), BF16),
            pltpu.VMEM((channels * TILES, LANES), F32),
            pltpu.SemaphoreType.DMA((copies,)),
            pltpu.SemaphoreType.DMA((copies,)),
            pltpu.SemaphoreType.DMA((3,)),
        ],
        compiler_params=pltpu.CompilerParams(
            collective_id=0, has_side_effects=True, vmem_limit_bytes=BIG
        ),
        name="front",
    )(fine, coarse, order, gain, emb_fine, emb_coarse, long_filter, outer3, twist, fwd, bwd, inv3, taps, w)


CHUNKS = 2


def tail_kernel(
    y_ref,
    w_ref,
    hyena_ref,
    attn_ref,
    wv_ref,
    x_ref,
    land_ref,
    acc_ref,
    state_ref,
    parts_ref,
    prefix_ref,
    incoming_ref,
    send,
    recv,
    own,
):
    z, c, r = here()
    y, x = c // 4, lax.rem(c, 4)
    sems = (send, recv)
    length = x_ref.shape[1]
    span = length // CHUNKS

    def chan(at_x, at_y):
        return lax.rem(at_y + 8, 4) * 4 + lax.rem(at_x + 8, 4)

    def device(at_x, at_y):
        return (z, chan(at_x, at_y), r)

    line = [(lax.rem(z + j, 8), c, r) for j in range(1, 8)]
    weights = pltpu.make_async_copy(w_ref, wv_ref, own.at[0])
    weights.start()
    greet(line + [device(x + 1, y), device(x - 1, y), device(x, y + 1), device(x, y - 1)])
    index = [0]
    sent = []

    def tell(src, dst, peer):
        copy = push(src, dst, sems, index[0], peer)
        index[0] += 1
        sent.append(copy)
        return copy

    mine_rows = pl.ds(pl.multiple_of(z * 32, 32), 32)
    turned = []
    kept = []
    for t in range(CHUNKS):
        at = pl.ds(t * span, span)
        kept.append(
            pltpu.make_async_copy(y_ref.at[z, :, at], x_ref.at[mine_rows, at], own.at[1 + t])
        )
        kept[-1].start()
        if t == 0:
            turned.append([tell(y_ref.at[p[0], :, at], x_ref.at[mine_rows, at], p) for p in line])
    half = x_ref.shape[0] // 2
    quarter = half // 2

    def send_block(t, lead, along, across, part, direction, phase):
        axes = (0, 1) if lead == 0 else (1, 0)
        offset = [0, 0]
        offset[axes[0]], offset[axes[1]] = along, across
        step = [0, 0]
        step[axes[phase]] = direction
        target = device(x + step[0], y + step[1])
        start = lead * half + (0 if part is None else part * quarter)
        rows = pl.ds(start, half if part is None else quarter)
        at = pl.ds(t * span, span)
        dst = land_ref.at[chan(x - offset[0], y - offset[1]), rows, at]
        src = x_ref.at[rows, at] if along == 0 and across == 0 else dst
        number = index[0]
        tell(src, dst, target)
        came = [offset[0] + step[0], offset[1] + step[1]]
        landed = land_ref.at[chan(x - came[0], y - came[1]), rows, at]
        return pltpu.make_async_remote_copy(
            src_ref=landed,
            dst_ref=landed,
            send_sem=send.at[number],
            recv_sem=recv.at[number],
            device_id=target,
            device_id_type=MESH,
        )

    first = {}
    second = {}
    forward = {}
    pending = []

    def multiply(t, lead, along, across):
        at = slice(t * span, (t + 1) * span)
        rows = slice(lead * half, (lead + 1) * half)
        offset = (along, across) if lead == 0 else (across, along)
        origin = chan(x - offset[0], y - offset[1])
        block = x_ref[rows, at] if offset == (0, 0) else land_ref[origin, rows, at]
        depth = pl.ds(pl.multiple_of(origin * 2 * half + lead * half, half), half)
        for k in range(3):
            product = lax.dot_general(
                wv_ref[k, depth, :], block, (((0,), (0,)), ((), ())), preferred_element_type=F32
            )
            if (along, across, lead) == (0, 0, 0):
                acc_ref[k, :, at] = product
            else:
                acc_ref[k, :, at] += product

    def drain(count):
        for _ in range(min(count, len(pending))):
            multiply(*pending.pop(0))

    def open_chunk(t):
        kept[t].wait()
        for copy in turned[t]:
            copy.wait_recv()
        if t + 1 < CHUNKS:
            at = pl.ds((t + 1) * span, span)
            turned.append([tell(y_ref.at[p[0], :, at], x_ref.at[mine_rows, at], p) for p in line])
        for lead in range(2):
            for d in (1, -1):
                first[t, lead, d] = send_block(t, lead, 0, 0, None, d, 0)
        for lead in range(2):
            for d in (1, -1):
                second[t, lead, 0, d] = send_block(t, lead, 0, 0, None, d, 1)
        for lead in range(2):
            pending.append((t, lead, 0, 0))

    last = []

    def onward(t, lead, along):
        for e in (1, -1):
            second[t, lead, along, e].wait_recv()
            last.append((t, lead, along, send_block(t, lead, along, e, 0 if e == 1 else 1, e, 1)))
        for e in (1, -1):
            pending.append((t, lead, along, e))

    open_chunk(0)
    weights.wait()
    for t in range(CHUNKS):
        for d in (1, -1):
            for lead in range(2):
                first[t, lead, d].wait_recv()
                forward[t, lead, d] = send_block(t, lead, d, 0, 0 if d == 1 else 1, d, 0)
                for e in (1, -1):
                    second[t, lead, d, e] = send_block(t, lead, d, 0, None, e, 1)
                pending.append((t, lead, d, 0))
        if t + 1 < CHUNKS:
            open_chunk(t + 1)
        else:
            back = pltpu.make_async_copy(x_ref, hyena_ref, own.at[CHUNKS + 1])
            back.start()
        drain(2)
        for lead in range(2):
            onward(t, lead, 0)
            drain(1)
        for lead in range(2):
            forward[t, lead, 1].wait_recv()
            forward[t, lead, -1].wait_recv()
            for e in (1, -1):
                second[t, lead, 2, e] = send_block(t, lead, 2, 0, None, e, 1)
            pending.append((t, lead, 2, 0))
            drain(1)
    for t in range(CHUNKS):
        for along in (1, -1, 2):
            for lead in range(2):
                onward(t, lead, along)
                drain(3)
    for t, lead, along, arrival in last:
        arrival.wait_recv()
    for position in range(0, len(last), 2):
        t, lead, along, _ = last[position]
        pending.append((t, lead, along, 2))
    drain(len(pending))

    blocks = length // BLOCK
    heads = [[acc_ref[k, :, b * BLOCK : (b + 1) * BLOCK].astype(BF16) for b in range(blocks)] for k in range(3)]
    states = [
        lax.dot_general(
            heads[1][b], heads[2][b], (((1,), (1,)), ((), ())), preferred_element_type=F32
        )
        for b in range(blocks)
    ]
    total = states[0]
    for b in range(1, blocks):
        total = total + states[b]
    state_ref[...] = total.reshape(8, HD // 8, HD)
    parts_ref[z] = state_ref[z]
    gathered = [tell(state_ref.at[p[0]], parts_ref.at[z], p) for p in line]
    row = lax.broadcasted_iota(jnp.int32, (BLOCK, BLOCK), 0)
    column = lax.broadcasted_iota(jnp.int32, (BLOCK, BLOCK), 1)
    queries = []
    inside = []

    def local(b):
        queries.append(jnp.transpose(heads[0][b].astype(F32)).astype(BF16))
        scores = mm(queries[b], heads[1][b])
        scores = jnp.where(row >= column, scores, 0.0).astype(BF16)
        inside.append(
            lax.dot_general(
                scores, heads[2][b], (((1,), (1,)), ((), ())), preferred_element_type=F32
            )
        )

    local(0)
    for copy in gathered:
        copy.wait_recv()
    running = jnp.zeros((HD // 8, HD), F32)
    for step in range(8):
        prefix_ref[step] = running
        running = running + parts_ref[step]
    incoming_ref[z] = prefix_ref[z]
    dealt = [tell(prefix_ref.at[p[0]], incoming_ref.at[z], p) for p in line]
    for b in range(1, blocks):
        local(b)
    for copy in dealt:
        copy.wait_recv()
    earlier = incoming_ref[...].reshape(HD, HD)
    place = lax.broadcasted_iota(jnp.int32, (BLOCK, HD), 0)
    for b in range(blocks):
        carried = mm(queries[b], earlier.astype(BF16))
        position = z * length + b * BLOCK + place + 1
        divisor = jnp.sqrt((position * HD).astype(F32))
        attn_ref[b * BLOCK : (b + 1) * BLOCK, :] = ((inside[b] + carried) / divisor).astype(BF16)
        earlier = earlier + states[b]
    for copy in sent:
        copy.wait_send()
    back.wait()


def tail(y, w):
    seqs, channels, length = y.shape
    depth = seqs * channels
    vmem = pl.BlockSpec(memory_space=pltpu.VMEM)
    copies = CHUNKS * (7 + 40) + 14
    return pl.pallas_call(
        tail_kernel,
        in_specs=[ANY, ANY],
        out_specs=[ANY, vmem],
        out_shape=(
            jax.ShapeDtypeStruct((depth, length), BF16),
            jax.ShapeDtypeStruct((length, HD), BF16),
        ),
        scratch_shapes=[
            pltpu.VMEM(w.shape, BF16),
            pltpu.VMEM((depth, length), BF16),
            pltpu.VMEM((16, depth, length), BF16),
            pltpu.VMEM((3, HD, length), F32),
            pltpu.VMEM((8, HD // 8, HD), F32),
            pltpu.VMEM((8, HD // 8, HD), F32),
            pltpu.VMEM((8, HD // 8, HD), F32),
            pltpu.VMEM((8, HD // 8, HD), F32),
            pltpu.SemaphoreType.DMA((copies,)),
            pltpu.SemaphoreType.DMA((copies,)),
            pltpu.SemaphoreType.DMA((CHUNKS + 2,)),
        ],
        compiler_params=pltpu.CompilerParams(
            collective_id=2, has_side_effects=True, vmem_limit_bytes=BIG
        ),
        name="tail",
    )(y, w)


def settle_kernel(hyena_ref, attn_ref, hyena_out, attn_out):
    hyena_out[...] = hyena_ref[...]
    attn_out[...] = attn_ref[...]


def settle(hyena, attn):
    return pl.pallas_call(
        settle_kernel,
        out_shape=(
            jax.ShapeDtypeStruct(hyena.shape, hyena.dtype),
            jax.ShapeDtypeStruct(attn.shape, attn.dtype),
        ),
        name="settle",
    )(hyena, attn)


def shards(
    fine_codes,
    coarse_codes,
    frame_order,
    emb_fine,
    emb_coarse,
    norm_gain,
    w_hyena,
    short_taps,
    long_filter,
    w_attn,
):
    y = front(
        fine_codes,
        coarse_codes,
        frame_order,
        norm_gain,
        emb_fine,
        emb_coarse,
        long_filter,
        short_taps,
        jnp.transpose(w_hyena, (1, 0, 2)),
    )
    return settle(*tail(y, jnp.transpose(w_attn, (1, 0, 2))))


def solution(mesh):
    return jax.shard_map(
        shards,
        mesh=mesh,
        in_specs=(
            P(("rep", "seq")),
            P(("rep", "seq")),
            P(),
            P(None, "chan"),
            P(None, "chan"),
            P("chan"),
            P(None, None, "chan"),
            P(None, "chan", None),
            P(("chan", "seq"), None),
            P(None, None, "chan"),
        ),
        out_specs=(P("chan", ("rep", "seq")), P(("rep", "seq"), "chan")),
        check_vma=False,
    )
```

```python
import functools
import math

import jax
import jax.numpy as jnp
import numpy as np
from jax import lax
from jax.experimental import pallas as pl
from jax.experimental.pallas import tpu as pltpu
from jax.sharding import PartitionSpec as P

HD = 128
FRAME = 256
BLOCK = 512
LANES = 128
EPSILON = 1e-05
F32 = jnp.float32
BF16 = jnp.bfloat16
ANY = pl.BlockSpec(memory_space=pl.ANY)
MESH = pl.DeviceIdType.MESH
BIG = 56 << 20

ROWS_W = 72
TILES = 64
POINTS = 2 * TILES * LANES


def split_np(x):
    hi = np.asarray(x, np.float32).astype(jnp.bfloat16)
    lo = (np.asarray(x, np.float64) - hi.astype(np.float64)).astype(np.float32).astype(jnp.bfloat16)
    return hi, lo


@functools.lru_cache(None)
def tables():
    w = np.arange(ROWS_W)[:, None]
    kept = (w <= 64).astype(np.float64)
    q = np.arange(TILES)[None, :]
    angle = 2 * np.pi * ((w * q) % 128) / 128
    outer = np.concatenate([np.cos(angle) * kept, -np.sin(angle) * kept], 0)
    a = np.arange(LANES)[None, :]
    turn = 2 * np.pi * (w * a) / POINTS
    twist = np.stack([np.cos(turn) * kept, np.sin(turn) * kept]).astype(np.float32)
    m = np.arange(LANES)
    inner = 2 * np.pi * ((m[:, None] * m[None, :]) % 128) / 128
    c, s = np.cos(inner), np.sin(inner)
    forward = np.block([[c, -s], [s, c]])
    backward = np.block([[c, s], [-s, c]])
    weight = np.where((w == 0) | (w == 64), 1.0, 2.0) * kept / POINTS
    inverse = np.concatenate([(np.cos(angle) * weight).T, (-np.sin(angle) * weight).T], 1)
    outer_hi, outer_lo = split_np(outer)
    inv_hi, inv_lo = split_np(inverse)
    fwd = np.stack(split_np(forward))
    bwd = np.stack(split_np(backward))
    outer3 = np.concatenate([outer_hi, outer_lo, outer_hi], 1)
    inv3 = np.concatenate([inv_hi, inv_lo, inv_hi], 1)
    return outer3, twist, fwd, bwd, inv3


def split(x):
    hi = x.astype(BF16)
    return hi, (x - hi.astype(F32)).astype(BF16)


def mm(a, b):
    return jnp.dot(a, b, preferred_element_type=F32)


def mm3(x, table):
    hi, lo = split(x)
    return mm(hi, table[0]) + (mm(lo, table[0]) + mm(hi, table[1]))


def local_sums(codes_ref, order, emb_fine_ref, emb_coarse_ref, ids_ref, sums_ref):
    row = lax.broadcasted_iota(jnp.int32, (FRAME, FRAME), 0)
    pick = (row == order).astype(BF16)
    pick_half = (row[: FRAME // 2] == order // 2).astype(BF16)

    def looked(codes, pick):
        hi = (codes // 32).astype(F32).astype(BF16)
        lo = (codes % 32).astype(F32).astype(BF16)
        return (mm(hi, pick) * 32.0 + mm(lo, pick)).astype(jnp.int32)

    fine = looked(codes_ref[0:4, :], pick)
    coarse = looked(codes_ref[4:8, : FRAME // 2], pick_half)
    ids_ref[0:4, :] = fine
    ids_ref[4:8, :] = coarse
    vocab = lax.broadcasted_iota(jnp.int32, (emb_fine_ref.shape[0], FRAME), 0)
    dims = (((0,), (0,)), ((), ()))
    for frame in range(4):
        hot_fine = (vocab == fine[frame : frame + 1]).astype(BF16)
        hot_coarse = (vocab == coarse[frame : frame + 1]).astype(BF16)
        rows = lax.dot_general(emb_fine_ref[...], hot_fine, dims, preferred_element_type=F32)
        rows = rows + lax.dot_general(
            emb_coarse_ref[...], hot_coarse, dims, preferred_element_type=F32
        )
        rows = rows.astype(BF16).astype(F32)
        total = jnp.sum(rows * rows, axis=0, keepdims=True)
        sums_ref[2 * frame : 2 * frame + 1, :] = total[:, :LANES]
        sums_ref[2 * frame + 1 : 2 * frame + 2, :] = total[:, LANES:]


GROUP = 16


def twisted(step, twist_ref):
    cos, sin = twist_ref[0], twist_ref[1]
    rows = []
    for i in range(GROUP):
        re = step[:ROWS_W, i * LANES : (i + 1) * LANES]
        im = step[ROWS_W:, i * LANES : (i + 1) * LANES]
        rows.append(jnp.concatenate([re * cos + im * sin, im * cos - re * sin], 1))
    return jnp.concatenate(rows, 0)


def spectrum_kernel(h_ref, outer_ref, twist_ref, fwd_ref, out_ref, wide_ref):
    channels = h_ref.shape[0]
    for q in range(TILES):
        wide_ref[pl.ds(q, channels, stride=TILES), :] = h_ref[:, q * LANES : (q + 1) * LANES]

    @pl.loop(0, channels // GROUP)
    def _(step):
        pieces = []
        for i in range(GROUP):
            hi, lo = split(wide_ref[pl.ds((step * GROUP + i) * TILES, TILES), :])
            pieces.append(jnp.concatenate([hi, hi, lo], 0))
        first = mm(outer_ref[...], jnp.concatenate(pieces, 1))
        out_ref[pl.ds(step * GROUP * ROWS_W, GROUP * ROWS_W), :] = mm3(
            twisted(first, twist_ref), fwd_ref
        )


def convolve_kernel(
    proj_ref,
    ids_ref,
    factor_ref,
    taps_ref,
    spec_ref,
    outer_ref,
    twist_ref,
    fwd_ref,
    bwd_ref,
    inv_ref,
    out_ref,
    left_ref,
    wide_ref,
    gate_ref,
    mix_ref,
    y_ref,
):
    channels = 32
    for s in range(16):
        both = proj_ref[s].reshape(96, 256)
        left_ref[0:96, s * 128 : (s + 1) * 128] = both[:, :128]
        left_ref[96:192, s * 128 : (s + 1) * 128] = both[:, 128:]
    vocab = lax.broadcasted_iota(jnp.int32, (1024, FRAME), 0)

    @pl.loop(0, 8)
    def _(z):
        ids = ids_ref[z]
        for i in range(4):
            hot = jnp.concatenate(
                [
                    (vocab == ids[i : i + 1]).astype(BF16),
                    (vocab == ids[4 + i : 5 + i]).astype(BF16),
                ],
                0,
            )
            both = mm(left_ref[...], hot)
            value = both[:96] + both[96:]
            for half in range(2):
                wide_ref[pl.ds(z * 8 + 2 * i + half, 96, stride=TILES), :] = value[
                    :, half * LANES : (half + 1) * LANES
                ]

    tap_row = lax.broadcasted_iota(jnp.int32, (LANES, LANES), 0)
    tap_col = lax.broadcasted_iota(jnp.int32, (LANES, LANES), 1)
    group_row = lax.broadcasted_iota(jnp.int32, taps_ref.shape[1:], 0)
    rows = 16 * TILES
    first_tile = lax.broadcasted_iota(jnp.int32, (rows, LANES), 0) % TILES == 0
    scale = jnp.concatenate([factor_ref[...].reshape(TILES, LANES)] * 16, 0)

    def filtered(k, g):
        wanted = 2 * lax.axis_index("seq") + g
        own = jnp.where(group_row == wanted, taps_ref[k].astype(F32), 0.0)
        taps = jnp.broadcast_to(jnp.sum(own, axis=0, keepdims=True), (LANES, LANES))
        turned = pltpu.roll(taps, 0, 1, stride=1, stride_axis=0)
        both = jnp.concatenate(
            [
                jnp.where(tap_col >= tap_row, turned, 0.0),
                jnp.where(tap_col < tap_row, turned, 0.0),
            ],
            1,
        ).astype(BF16)
        start = (2 * k + g) * rows
        x = (wide_ref[start : start + rows, :] * scale).astype(BF16)
        parts = mm(x, both)
        carried = jnp.where(first_tile, 0.0, pltpu.roll(parts[:, LANES:], 1, 0))
        return (parts[:, :LANES] + carried).astype(BF16)

    for g in range(2):
        gate_ref[g * rows : (g + 1) * rows, :] = filtered(0, g)
        left = filtered(1, g).astype(F32)
        mix_ref[g * rows : (g + 1) * rows, :] = (left * filtered(2, g).astype(F32)).astype(BF16)

    @pl.loop(0, channels // GROUP)
    def _(step):
        pieces = []
        for i in range(GROUP):
            x = mix_ref[pl.ds((step * GROUP + i) * TILES, TILES), :]
            pieces.append(jnp.concatenate([x, x], 0))
        first = mm(outer_ref[:, : 2 * TILES], jnp.concatenate(pieces, 1))
        spec = mm3(twisted(first, twist_ref), fwd_ref)
        other = spec_ref[pl.ds(step * GROUP * ROWS_W, GROUP * ROWS_W), :]
        re, im = spec[:, :LANES], spec[:, LANES:]
        ore, oim = other[:, :LANES], other[:, LANES:]
        back = mm3(jnp.concatenate([re * ore - im * oim, re * oim + im * ore], 1), bwd_ref)
        cos, sin = twist_ref[0], twist_ref[1]
        columns = []
        for i in range(GROUP):
            bre = back[i * ROWS_W : (i + 1) * ROWS_W, :LANES]
            bim = back[i * ROWS_W : (i + 1) * ROWS_W, LANES:]
            undone = jnp.concatenate([bre * cos - bim * sin, bim * cos + bre * sin], 0)
            hi, lo = split(undone)
            columns.append(jnp.concatenate([hi, hi, lo], 0))
        result = mm(inv_ref[...], jnp.concatenate(columns, 1))
        for i in range(GROUP):
            at = pl.ds((step * GROUP + i) * TILES, TILES)
            conv = result[:, i * LANES : (i + 1) * LANES].astype(BF16).astype(F32)
            y_ref[at, :] = gate_ref[at, :].astype(F32) * conv

    for q in range(TILES):
        out_ref[q // 8, :, (q % 8) * LANES : (q % 8 + 1) * LANES] = y_ref[
            pl.ds(q, channels, stride=TILES), :
        ].astype(BF16)


def here():
    return lax.axis_index("seq"), lax.axis_index("chan"), lax.axis_index("rep")


def greet(peers):
    barrier = pltpu.get_barrier_semaphore()
    for peer in peers:
        pl.semaphore_signal(barrier, inc=1, device_id=peer, device_id_type=MESH)
    pl.semaphore_wait(barrier, len(peers))


def push(src, dst, sems, index, peer):
    copy = pltpu.make_async_remote_copy(
        src_ref=src,
        dst_ref=dst,
        send_sem=sems[0].at[index],
        recv_sem=sems[1].at[index],
        device_id=peer,
        device_id_type=MESH,
    )
    copy.start()
    return copy


def front_kernel(
    fine_ref,
    coarse_ref,
    order_ref,
    gain_ref,
    emb_fine_ref,
    emb_coarse_ref,
    filter_ref,
    outer_ref,
    twist_ref,
    fwd_ref,
    bwd_ref,
    inv_ref,
    taps_ref,
    w_ref,
    out_ref,
    proj_out,
    factor_out,
    ids_out,
    spec_ref,
    left_ref,
    all_ref,
    gate_ref,
    mix_ref,
    y_ref,
    codes_ref,
    rows_ref,
    gains_ref,
    sums_ref,
    x_ref,
    wv_ref,
    proj_ref,
    wide_ref,
    send,
    recv,
    own,
):
    z, c, r = here()
    sems = (send, recv)
    plane = [(z, lax.rem(c + j, 16), r) for j in range(1, 16)]
    line = [(lax.rem(z + j, 8), c, r) for j in range(1, 8)]
    sibling = (z, c, 1 - r)
    slot = r * 8 + z
    weights = [pltpu.make_async_copy(w_ref.at[k], wv_ref.at[k], own.at[k]) for k in range(3)]
    for copy in weights:
        copy.start()
    at = pl.ds(pl.multiple_of(z * 128, 128), 128)

    @pl.when(r == 0)
    def _():
        rows_ref[c] = emb_fine_ref[at, :]

    @pl.when(r != 0)
    def _():
        rows_ref[c] = emb_coarse_ref[at, :]

    gains_ref[c] = jnp.broadcast_to(gain_ref[...].reshape(1, FRAME).astype(F32), (8, FRAME))
    greet(plane + line + [sibling])
    sent = []
    index = [0]

    def tell(src, dst, peer):
        copy = push(src, dst, sems, index[0], peer)
        index[0] += 1
        sent.append(copy)
        return copy

    gains = [tell(gains_ref.at[c], gains_ref.at[c], peer) for peer in plane]
    y, x = c // 4, lax.rem(c, 4)

    def chan(at_x, at_y):
        return lax.rem(at_y + 8, 4) * 4 + lax.rem(at_x + 8, 4)

    def hop(lead, along, across, part, direction, phase):
        axes = (0, 1) if lead == 0 else (1, 0)
        offset = [0, 0]
        offset[axes[0]], offset[axes[1]] = along, across
        step = [0, 0]
        step[axes[phase]] = direction
        target = (z, chan(x + step[0], y + step[1]), r)
        part_rows = pl.ds(lead * 64 + (0 if part is None else part * 32), 64 if part is None else 32)
        block = rows_ref.at[chan(x - offset[0], y - offset[1]), part_rows]
        number = index[0]
        tell(block, block, target)
        landed = rows_ref.at[chan(x - offset[0] - step[0], y - offset[1] - step[1]), part_rows]
        return pltpu.make_async_remote_copy(
            src_ref=landed,
            dst_ref=landed,
            send_sem=send.at[number],
            recv_sem=recv.at[number],
            device_id=target,
            device_id_type=MESH,
        )

    first = {(lead, d): hop(lead, 0, 0, None, d, 0) for lead in range(2) for d in (1, -1)}
    second = {(lead, 0, d): hop(lead, 0, 0, None, d, 1) for lead in range(2) for d in (1, -1)}
    turned = {}
    for d in (1, -1):
        for lead in range(2):
            first[lead, d].wait_recv()
            turned[lead, d] = hop(lead, d, 0, 0 if d == 1 else 1, d, 0)
            for e in (1, -1):
                second[lead, d, e] = hop(lead, d, 0, None, e, 1)
    last = []

    def onward(lead, along):
        for e in (1, -1):
            second[lead, along, e].wait_recv()
            last.append(hop(lead, along, e, 0 if e == 1 else 1, e, 1))

    for lead in range(2):
        onward(lead, 0)
    for lead in range(2):
        turned[lead, 1].wait_recv()
        turned[lead, -1].wait_recv()
        for e in (1, -1):
            second[lead, 2, e] = hop(lead, 2, 0, None, e, 1)
    for along in (1, -1):
        for lead in range(2):
            onward(lead, along)
    for lead in range(2):
        onward(lead, 2)
    for i in range(4):
        codes_ref[i : i + 1, :] = fine_ref[i * FRAME : (i + 1) * FRAME].reshape(1, FRAME)
        codes_ref[4 + i : 5 + i, : FRAME // 2] = coarse_ref[
            i * FRAME // 2 : (i + 1) * FRAME // 2
        ].reshape(1, FRAME // 2)
    local_sums(
        codes_ref,
        order_ref[...].reshape(1, FRAME),
        emb_fine_ref,
        emb_coarse_ref,
        ids_out.at[z],
        sums_ref.at[c],
    )
    sums = [tell(sums_ref.at[c], sums_ref.at[c], peer) for peer in plane]
    ids = [tell(ids_out.at[z], ids_out.at[z], peer) for peer in line]

    def prepare(origin):
        hi, lo = split(rows_ref[origin].astype(F32) * gains_ref[origin, 0:1, :])
        columns = pl.ds(pl.multiple_of(origin * 256, 256), 256)
        x_ref[0:128, columns] = hi
        x_ref[128:256, columns] = lo

    for arrival in last:
        arrival.wait_recv()
    for copy in gains:
        copy.wait_recv()
    prepare(c)
    for other in range(1, 16):
        prepare(lax.rem(c + other, 16))
    dealt = [[] for _ in range(7)]
    for k in range(3):
        weights[k].wait()
        both = mm(x_ref[...], wv_ref[k])
        hi, lo = split(jnp.transpose(both[:128] + both[128:]))
        proj_ref[k, :, :128] = hi
        proj_ref[k, :, 128:] = lo
        for j, peer in enumerate(line):
            src = proj_ref.at[k, pl.ds(pl.multiple_of(peer[0] * 32, 32), 32), :]
            dealt[j].append(tell(src, proj_out.at[slot, k], peer))
    for copy in sums:
        copy.wait_recv()
    total = sums_ref[0]
    for other in range(1, 16):
        total = total + sums_ref[other]
    factor_out[z] = lax.rsqrt(total / (16 * 256.0) + EPSILON)
    factors = [tell(factor_out.at[z], factor_out.at[z], peer) for peer in line]
    proj_out[slot] = proj_ref[:, pl.ds(pl.multiple_of(z * 32, 32), 32), :]
    across = [tell(proj_out.at[slot], proj_out.at[slot], sibling)]
    spectrum_kernel(filter_ref, outer_ref, twist_ref, fwd_ref, spec_ref, wide_ref)
    for j in range(7):
        for copy in dealt[j]:
            copy.wait_recv()
        landed = proj_out.at[r * 8 + lax.rem(z + 7 - j, 8)]
        across.append(tell(landed, landed, sibling))
    for copy in ids + factors + across:
        copy.wait_recv()
    convolve_kernel(
        proj_out,
        ids_out,
        factor_out,
        taps_ref,
        spec_ref,
        outer_ref,
        twist_ref,
        fwd_ref,
        bwd_ref,
        inv_ref,
        out_ref,
        left_ref,
        all_ref,
        gate_ref,
        mix_ref,
        y_ref,
    )
    for copy in sent:
        copy.wait_send()


def front(fine, coarse, order, gain, emb_fine, emb_coarse, long_filter, taps, w):
    outer3, twist, fwd, bwd, inv3 = tables()
    channels = long_filter.shape[0]
    vmem = pl.BlockSpec(memory_space=pltpu.VMEM)
    copies = 30 + 40 + 7 + 21 + 7 + 8
    return pl.pallas_call(
        front_kernel,
        in_specs=[vmem] * 13 + [ANY],
        out_shape=jax.ShapeDtypeStruct((8, channels, 1024), BF16),
        scratch_shapes=[
            pltpu.VMEM((16, 3, 32, 256), BF16),
            pltpu.VMEM((8, 8, LANES), F32),
            pltpu.VMEM((8, 8, FRAME), jnp.int32),
            pltpu.VMEM((channels * ROWS_W, 256), F32),
            pltpu.VMEM((192, 2048), BF16),
            pltpu.VMEM((96 * TILES, LANES), F32),
            pltpu.VMEM((channels * TILES, LANES), BF16),
            pltpu.VMEM((channels * TILES, LANES), BF16),
            pltpu.VMEM((channels * TILES, LANES), F32),
            pltpu.VMEM((8, FRAME), jnp.int32),
            pltpu.VMEM((16, 128, 256), BF16),
            pltpu.VMEM((16, 8, FRAME), F32),
            pltpu.VMEM((16, 8, LANES), F32),
            pltpu.VMEM((256, 4096), BF16),
            pltpu.VMEM((3, 4096, 256), BF16),
            pltpu.VMEM((3, 256, 256), BF16),
            pltpu.VMEM((channels * TILES, LANES), F32),
            pltpu.SemaphoreType.DMA((copies,)),
            pltpu.SemaphoreType.DMA((copies,)),
            pltpu.SemaphoreType.DMA((3,)),
        ],
        compiler_params=pltpu.CompilerParams(
            collective_id=0, has_side_effects=True, vmem_limit_bytes=BIG
        ),
        name="front",
    )(fine, coarse, order, gain, emb_fine, emb_coarse, long_filter, outer3, twist, fwd, bwd, inv3, taps, w)


CHUNKS = 2


def tail_kernel(
    y_ref,
    w_ref,
    hyena_ref,
    attn_ref,
    wv_ref,
    x_ref,
    land_ref,
    acc_ref,
    state_ref,
    parts_ref,
    prefix_ref,
    incoming_ref,
    send,
    recv,
    own,
):
    z, c, r = here()
    y, x = c // 4, lax.rem(c, 4)
    sems = (send, recv)
    length = x_ref.shape[1]
    span = length // CHUNKS

    def chan(at_x, at_y):
        return lax.rem(at_y + 8, 4) * 4 + lax.rem(at_x + 8, 4)

    def device(at_x, at_y):
        return (z, chan(at_x, at_y), r)

    line = [(lax.rem(z + j, 8), c, r) for j in (4, 3, 5, 2, 6, 1, 7)]
    weights = [
        pltpu.make_async_copy(
            w_ref.at[k], wv_ref.at[:, pl.ds(k * HD, HD)], own.at[CHUNKS + 2 + k]
        )
        for k in range(3)
    ]
    for copy in weights:
        copy.start()
    greet(line + [device(x + 1, y), device(x - 1, y), device(x, y + 1), device(x, y - 1)])
    index = [0]
    sent = []

    def tell(src, dst, peer):
        copy = push(src, dst, sems, index[0], peer)
        index[0] += 1
        sent.append(copy)
        return copy

    mine_rows = pl.ds(pl.multiple_of(z * 32, 32), 32)
    turned = []
    kept = []
    for t in range(CHUNKS):
        at = pl.ds(t * span, span)
        kept.append(
            pltpu.make_async_copy(y_ref.at[z, :, at], x_ref.at[mine_rows, at], own.at[1 + t])
        )
        kept[-1].start()
        if t == 0:
            turned.append([tell(y_ref.at[p[0], :, at], x_ref.at[mine_rows, at], p) for p in line])
    half = x_ref.shape[0] // 2
    quarter = half // 2

    def send_block(t, lead, along, across, part, direction, phase):
        axes = (0, 1) if lead == 0 else (1, 0)
        offset = [0, 0]
        offset[axes[0]], offset[axes[1]] = along, across
        step = [0, 0]
        step[axes[phase]] = direction
        target = device(x + step[0], y + step[1])
        start = lead * half + (0 if part is None else part * quarter)
        rows = pl.ds(start, half if part is None else quarter)
        at = pl.ds(t * span, span)
        dst = land_ref.at[chan(x - offset[0], y - offset[1]), rows, at]
        src = x_ref.at[rows, at] if along == 0 and across == 0 else dst
        number = index[0]
        tell(src, dst, target)
        came = [offset[0] + step[0], offset[1] + step[1]]
        landed = land_ref.at[chan(x - came[0], y - came[1]), rows, at]
        return pltpu.make_async_remote_copy(
            src_ref=landed,
            dst_ref=landed,
            send_sem=send.at[number],
            recv_sem=recv.at[number],
            device_id=target,
            device_id_type=MESH,
        )

    first = {}
    second = {}
    forward = {}
    pending = []

    def multiply(t, lead, along, across):
        at = slice(t * span, (t + 1) * span)
        rows = slice(lead * half, (lead + 1) * half)
        offset = (along, across) if lead == 0 else (across, along)
        origin = chan(x - offset[0], y - offset[1])
        block = x_ref[rows, at] if offset == (0, 0) else land_ref[origin, rows, at]
        depth = pl.ds(pl.multiple_of(origin * 2 * half + lead * half, half), half)
        product = lax.dot_general(
            wv_ref[depth, :], block, (((0,), (0,)), ((), ())), preferred_element_type=F32
        )
        if (along, across, lead) == (0, 0, 0):
            acc_ref[:, at] = product
        else:
            acc_ref[:, at] += product

    def drain(count):
        for _ in range(min(count, len(pending))):
            multiply(*pending.pop(0))

    def open_chunk(t):
        kept[t].wait()
        for copy in turned[t]:
            copy.wait_recv()
        if t + 1 < CHUNKS:
            at = pl.ds((t + 1) * span, span)
            turned.append([tell(y_ref.at[p[0], :, at], x_ref.at[mine_rows, at], p) for p in line])
        for lead in range(2):
            for d in (1, -1):
                first[t, lead, d] = send_block(t, lead, 0, 0, None, d, 0)
        for lead in range(2):
            for d in (1, -1):
                second[t, lead, 0, d] = send_block(t, lead, 0, 0, None, d, 1)
        for lead in range(2):
            pending.append((t, lead, 0, 0))

    last = []

    def onward(t, lead, along):
        for e in (1, -1):
            second[t, lead, along, e].wait_recv()
            last.append((t, lead, along, send_block(t, lead, along, e, 0 if e == 1 else 1, e, 1)))
        for e in (1, -1):
            pending.append((t, lead, along, e))

    open_chunk(0)
    for copy in weights:
        copy.wait()
    for t in range(CHUNKS):
        for d in (1, -1):
            for lead in range(2):
                first[t, lead, d].wait_recv()
                forward[t, lead, d] = send_block(t, lead, d, 0, 0 if d == 1 else 1, d, 0)
                for e in (1, -1):
                    second[t, lead, d, e] = send_block(t, lead, d, 0, None, e, 1)
                pending.append((t, lead, d, 0))
        if t + 1 < CHUNKS:
            open_chunk(t + 1)
        else:
            back = pltpu.make_async_copy(x_ref, hyena_ref, own.at[CHUNKS + 1])
            back.start()
        drain(2)
        for lead in range(2):
            onward(t, lead, 0)
            drain(1)
        for lead in range(2):
            forward[t, lead, 1].wait_recv()
            forward[t, lead, -1].wait_recv()
            for e in (1, -1):
                second[t, lead, 2, e] = send_block(t, lead, 2, 0, None, e, 1)
            pending.append((t, lead, 2, 0))
            drain(1)
    for t in range(CHUNKS):
        for along in (1, -1, 2):
            for lead in range(2):
                onward(t, lead, along)
                drain(5)
    for t, lead, along, arrival in last:
        arrival.wait_recv()
    for position in range(0, len(last), 2):
        t, lead, along, _ = last[position]
        pending.append((t, lead, along, 2))
    drain(len(pending))

    blocks = length // BLOCK
    heads = [[acc_ref[k * HD : (k + 1) * HD, b * BLOCK : (b + 1) * BLOCK].astype(BF16) for b in range(blocks)] for k in range(3)]
    states = [
        lax.dot_general(
            heads[1][b], heads[2][b], (((1,), (1,)), ((), ())), preferred_element_type=F32
        )
        for b in range(blocks)
    ]
    total = states[0]
    for b in range(1, blocks):
        total = total + states[b]
    state_ref[...] = total.reshape(8, HD // 8, HD)
    parts_ref[z] = state_ref[z]
    gathered = [tell(state_ref.at[p[0]], parts_ref.at[z], p) for p in line]
    row = lax.broadcasted_iota(jnp.int32, (BLOCK, BLOCK), 0)
    column = lax.broadcasted_iota(jnp.int32, (BLOCK, BLOCK), 1)
    queries = []
    inside = []

    def local(b):
        queries.append(jnp.transpose(heads[0][b].astype(F32)).astype(BF16))
        scores = mm(queries[b], heads[1][b])
        scores = jnp.where(row >= column, scores, 0.0).astype(BF16)
        inside.append(
            lax.dot_general(
                scores, heads[2][b], (((1,), (1,)), ((), ())), preferred_element_type=F32
            )
        )

    local(0)
    for copy in gathered:
        copy.wait_recv()
    running = jnp.zeros((HD // 8, HD), F32)
    for step in range(8):
        prefix_ref[step] = running
        running = running + parts_ref[step]
    incoming_ref[z] = prefix_ref[z]
    dealt = [tell(prefix_ref.at[p[0]], incoming_ref.at[z], p) for p in line]
    for b in range(1, blocks):
        local(b)
    for copy in dealt:
        copy.wait_recv()
    earlier = incoming_ref[...].reshape(HD, HD)
    place = lax.broadcasted_iota(jnp.int32, (BLOCK, HD), 0)
    for b in range(blocks):
        carried = mm(queries[b], earlier.astype(BF16))
        position = z * length + b * BLOCK + place + 1
        divisor = jnp.sqrt((position * HD).astype(F32))
        attn_ref[b * BLOCK : (b + 1) * BLOCK, :] = ((inside[b] + carried) / divisor).astype(BF16)
        earlier = earlier + states[b]
    for copy in sent:
        copy.wait_send()
    back.wait()


def tail(y, w):
    seqs, channels, length = y.shape
    depth = seqs * channels
    vmem = pl.BlockSpec(memory_space=pltpu.VMEM)
    copies = CHUNKS * (7 + 40) + 14
    return pl.pallas_call(
        tail_kernel,
        in_specs=[ANY, ANY],
        out_specs=[ANY, vmem],
        out_shape=(
            jax.ShapeDtypeStruct((depth, length), BF16),
            jax.ShapeDtypeStruct((length, HD), BF16),
        ),
        scratch_shapes=[
            pltpu.VMEM((w.shape[1], 3 * HD), BF16),
            pltpu.VMEM((depth, length), BF16),
            pltpu.VMEM((16, depth, length), BF16),
            pltpu.VMEM((3 * HD, length), F32),
            pltpu.VMEM((8, HD // 8, HD), F32),
            pltpu.VMEM((8, HD // 8, HD), F32),
            pltpu.VMEM((8, HD // 8, HD), F32),
            pltpu.VMEM((8, HD // 8, HD), F32),
            pltpu.SemaphoreType.DMA((copies,)),
            pltpu.SemaphoreType.DMA((copies,)),
            pltpu.SemaphoreType.DMA((CHUNKS + 5,)),
        ],
        compiler_params=pltpu.CompilerParams(
            collective_id=2, has_side_effects=True, vmem_limit_bytes=BIG
        ),
        name="tail",
    )(y, w)


def settle_kernel(hyena_ref, attn_ref, hyena_out, attn_out):
    hyena_out[...] = hyena_ref[...]
    attn_out[...] = attn_ref[...]


def settle(hyena, attn):
    return pl.pallas_call(
        settle_kernel,
        out_shape=(
            jax.ShapeDtypeStruct(hyena.shape, hyena.dtype),
            jax.ShapeDtypeStruct(attn.shape, attn.dtype),
        ),
        name="settle",
    )(hyena, attn)


def shards(
    fine_codes,
    coarse_codes,
    frame_order,
    emb_fine,
    emb_coarse,
    norm_gain,
    w_hyena,
    short_taps,
    long_filter,
    w_attn,
):
    y = front(
        fine_codes,
        coarse_codes,
        frame_order,
        norm_gain,
        emb_fine,
        emb_coarse,
        long_filter,
        short_taps,
        jnp.transpose(w_hyena, (1, 0, 2)),
    )
    return settle(*tail(y, jnp.transpose(w_attn, (1, 0, 2))))


def solution(mesh):
    return jax.shard_map(
        shards,
        mesh=mesh,
        in_specs=(
            P(("rep", "seq")),
            P(("rep", "seq")),
            P(),
            P(None, "chan"),
            P(None, "chan"),
            P("chan"),
            P(None, None, "chan"),
            P(None, "chan", None),
            P(("chan", "seq"), None),
            P(None, None, "chan"),
        ),
        out_specs=(P("chan", ("rep", "seq")), P(("rep", "seq"), "chan")),
        check_vma=False,
    )
```
